256 devices in a mesh: batch: 64 (over z, x, core), chan: 4 (over y).
Axes of the slice: x: 4, y: 4, z: 8, core: 2. Of those that a mesh axis runs over, the one named last changes fastest.
Arguments:
- monomers: bfloat16 [65536, 1280], P('batch', 'chan'), may hold values from -8 to 8
- keep_mask: int32 [2, 65536], P(None, 'batch'), may hold values 0 or 1
- lengths: int32 [128], P('batch'), may hold values from 256 to 512
- norm_gain: float32 [1280], replicated, may hold values from 0.5 to 1.5
- weight_a: bfloat16 [5, 1280, 1280], P(None, 'batch', 'chan'), may hold values from -0.078125 to 0.078125
- weight_b: bfloat16 [5, 1280, 512], P(None, 'chan', 'batch'), may hold values from -0.078125 to 0.078125
Outputs:
- whitened: float32 [2, 65536, 512], P(None, ('batch', 'chan'))
- pair_gap: float32 [65536], P(('batch', 'chan'))
The draws below stay inside these ranges and needn't reach their ends.
All inputs are finite; a program needn't handle non-finite values. No bound on the sum of `keep_mask` on one device may be relied on, other than what follows from the above.
Results may differ from the reference program's by a relative error of at most 0.0007.
The reference program's roundings to bfloat16 on the way (of `normed` and `hidden`) count: a program that leaves them out, or rounds other values in their place, can miss the bound.
Values may be sent and summed in bfloat16 or wider, within the bound.
A program may use at most 128 MiB of HBM per device.

```python
import jax
import jax.numpy as jnp
from jax import lax

D = 1280
E = 512
LEN = 512
SEQS = 128
TOKENS = 65536


def draw_lengths(key, part):
    first, second, third = jax.random.split(jax.random.fold_in(key, 11), 3)
    values = jax.random.randint(first, (SEQS,), LEN // 2, LEN + 1)
    high_spot = jax.random.randint(second, (), 0, SEQS)
    low_spot = (high_spot + 1 + jax.random.randint(third, (), 0, SEQS - 1)) % SEQS
    values = values.at[high_spot].set(LEN)
    values = values.at[low_spot].set(LEN // 2)
    return values.astype(jnp.int32)


def draw_monomers(key, part):
    first, second, third = jax.random.split(jax.random.fold_in(key, 23), 3)
    row_draw = jax.random.uniform(first, (TOKENS, 1), jnp.float32, 0.0, 1.0)
    row_scale = jnp.exp(jnp.log(10.0) * row_draw) / 3.0
    col_draw = jax.random.uniform(second, (1, D), jnp.float32, 0.0, 1.0)
    col_scale = jnp.exp(jnp.log(4.0) * (col_draw - 0.5))
    values = jax.random.normal(third, (TOKENS, D), jnp.float32) * col_scale
    return jnp.clip(values * row_scale, -8.0, 8.0).astype(jnp.bfloat16)


def plant(values, stream_key, smallest, top_value):
    shape = values.shape
    index_at = [jax.random.randint(jax.random.fold_in(stream_key, axis), (), 0, shape[axis]) for axis in range(len(shape))]
    values = values.at[tuple(index_at)].set(smallest)
    longest = shape.index(max(shape))
    index_at[longest] = (index_at[longest] + 1) % shape[longest]
    return values.at[tuple(index_at)].set(top_value)


def block_scale(key, dims, cuts, low, top_value):
    factor_of, own = 1.0, jax.random.fold_in(key, 6)
    for axis_at, blocks in cuts:
        draws = jnp.exp(jax.random.uniform(jax.random.fold_in(own, axis_at), (blocks,), jnp.float32, low / len(cuts), top_value / len(cuts)))
        factor_of = factor_of * jnp.repeat(draws, dims[axis_at] // blocks).reshape([-1 if axis == axis_at else 1 for axis in range(len(dims))])
    return factor_of


def bell_draw(stream_key, extent, width, most, cuts=(), kind=jnp.bfloat16):
    array = jax.random.normal(stream_key, extent, jnp.float32) * width
    if len(cuts) > 0:
        array = block_scale(stream_key, extent, cuts, -0.22, 0.18) * array
    return jnp.clip(array, min=-most, max=most).astype(kind)


def setup_inputs(seed: int = 0) -> dict:
    splits = jax.random.split(jax.random.key(seed), 7)
    monomers = draw_monomers(jax.random.fold_in(splits[6], 71), 0)
    keep_mask = plant((jax.random.randint(splits[1], (2, TOKENS), 0, 20) < 17).astype(jnp.int32), jax.random.fold_in(splits[1], 1), 0, 1)
    lengths = draw_lengths(jax.random.fold_in(splits[6], 71), 0)
    norm_gain = jnp.clip(1.0 + 0.1 * jax.random.normal(splits[3], (D,), jnp.float32), 0.5, 1.5)
    weight_a = bell_draw(splits[4], (5, D, D), (5 * D) ** -0.5, 0.078125, ((1, 64), (2, 4)))
    weight_b = bell_draw(splits[5], (5, D, E), (5 * D) ** -0.5, 0.078125, ((1, 4), (2, 64)))
    return {"monomers": monomers, "keep_mask": keep_mask, "lengths": lengths, "norm_gain": norm_gain, "weight_a": weight_a, "weight_b": weight_b}


EPS_NORM = 1e-05
EPS_COV = 0.0001
FULL_PRECISION = lax.Precision.HIGHEST

def smooth_gate(values):
    return 0.5 * values * (1.0 + jnp.tanh(0.7978845608 * (values + 0.044715 * values * values * values)))

def conv_taps(inputs, kernel_weight, dilation_step):
    length = inputs.shape[1]
    padded = jnp.pad(inputs, ((0, 0), (2 * dilation_step, 2 * dilation_step), (0, 0)))
    running = None
    for kernel_tap in range(5):
        offset_input = padded[:, kernel_tap * dilation_step:kernel_tap * dilation_step + length, :].astype(jnp.float32)
        kernel_contribution = jnp.einsum('eks,sg->ekg', offset_input, kernel_weight[kernel_tap].astype(jnp.float32), precision=FULL_PRECISION)
        running = kernel_contribution if running is None else running + kernel_contribution
    return running

def reference(monomers, keep_mask, lengths, norm_gain, weight_a, weight_b):

    def one_sequence(packed):
        features, keep_rows, seq_length = packed
        alive_rows = (jnp.arange(LEN) < seq_length).astype(jnp.float32)
        viewed = features.astype(jnp.float32)[None] * keep_rows.astype(jnp.float32)[:, :, None] * alive_rows[None, :, None]
        square_mean = lax.optimization_barrier(jnp.mean(viewed * viewed, axis=-1, keepdims=True))
        normed = (viewed * lax.rsqrt(square_mean + EPS_NORM) * norm_gain).astype(jnp.bfloat16)
        hidden = smooth_gate(conv_taps(normed, weight_a, 1)).astype(jnp.bfloat16)
        return (conv_taps(hidden, weight_b, 2), alive_rows)
    keep_seq = keep_mask.reshape(2, SEQS, LEN).transpose(1, 0, 2)
    embedded, alive = lax.map(one_sequence, (monomers.reshape(SEQS, LEN, D), keep_seq, lengths))
    embedded = embedded.transpose(1, 0, 2, 3).reshape(2, SEQS * LEN, E)
    alive = alive.reshape(SEQS * LEN)
    live_count = jnp.sum(alive)
    center = lax.optimization_barrier(jnp.sum(embedded * alive[None, :, None], axis=1)) / live_count
    centered = (embedded - center[:, None, :]) * alive[None, :, None]
    covariance = jnp.einsum('vtf,vtg->vfg', centered, centered, precision=FULL_PRECISION) / live_count
    covariance = covariance + EPS_COV * jnp.eye(E, dtype=jnp.float32)[None]
    factor_low = jnp.linalg.cholesky(covariance)

    def whiten(factor, block_rows):
        return jax.scipy.linalg.solve_triangular(factor, block_rows.T, lower=True).T
    whitened = jax.vmap(whiten)(factor_low, centered)
    gap_rows = whitened[0] - whitened[1]
    pair_gap = lax.optimization_barrier(jnp.sum(gap_rows * gap_rows, axis=-1)) / E
    return (whitened, pair_gap)
```

```python
import jax
import jax.numpy as jnp
from jax import lax
from jax.experimental import pallas as pl
from jax.experimental.pallas import tpu as pltpu
from jax.sharding import Mesh
from jax.sharding import PartitionSpec as P

BATCH = ("batch_0", "batch_1", "batch_2")
BATCH_CHAN = ("batch_0", "batch_1", "batch_2", "chan")


EPS_NORM = 1e-05
EPS_COV = 0.0001
FULL_PRECISION = lax.Precision.HIGHEST


def joined_along(pieces, dim):
    pieces = jnp.moveaxis(pieces, 0, dim)
    shape = pieces.shape
    return pieces.reshape(*shape[:dim], shape[dim] * shape[dim + 1], *shape[dim + 2 :])


def copy_for_each(array, axis):
    copies = jnp.broadcast_to(array, (lax.axis_size(axis), *array.shape))
    return lax.all_to_all(copies, axis, split_axis=0, concat_axis=0, tiled=True)


def gathered_copies(array, axis, dim):
    return joined_along(copy_for_each(array, axis), dim)


def in_blocks(array, dim, size):
    shape = array.shape
    pieces = array.reshape(*shape[:dim], size, shape[dim] // size, *shape[dim + 1 :])
    return jnp.moveaxis(pieces, dim, 0)


def summed_on_arrival(array, axis, dim):
    pieces = in_blocks(array, dim, lax.axis_size(axis))
    arrived = lax.all_to_all(pieces, axis, split_axis=0, concat_axis=0, tiled=True)
    return arrived.sum(axis=0)


def sum_in_two_steps(array, axes, dim):
    far, near = axes
    own = summed_on_arrival(in_blocks(array, dim, lax.axis_size(far)), near, dim + 1)
    return jnp.sum(lax.all_to_all(own, far, 0, 0, tiled=True), axis=0)


def padded_to(lines, size):
    spare = -lines.shape[0] % size
    if not spare:
        return lines
    return jnp.concatenate([lines, jnp.zeros((spare, *lines.shape[1:]), lines.dtype)])


def gathered_by_axis(array, axes, dim):
    far, near = axes
    pieces = copy_for_each(copy_for_each(array, far), near)
    return joined_along(pieces.swapaxes(0, 1).reshape(-1, *array.shape), dim)


def total_of(array, axes):
    own = sum_in_two_steps(
        padded_to(array, lax.axis_size(axes[0]) * lax.axis_size(axes[1])), axes, 0
    )
    whole = gathered_by_axis(own, axes, 0)
    return whole[: len(array)].reshape(array.shape)


def in_one(arrays, axis):
    ends = [0]
    for a in arrays:
        ends.append(ends[-1] + a.size)
    so_far = total_of(jnp.concatenate([a.ravel() for a in arrays]), axis)
    return tuple((so_far[b:e].reshape(a.shape) for a, b, e in zip(arrays, ends, ends[1:])))


def smooth_gate(values):
    return (
        0.5
        * values
        * (1.0 + jnp.tanh(0.7978845608 * (values + 0.044715 * values * values * values)))
    )


def pad_positions(inputs, dilation_step):
    return jnp.pad(inputs, ((0, 0), (0, 0), (2 * dilation_step, 2 * dilation_step), (0, 0)))


def conv_taps(padded, kernel_weight, dilation_step, length):
    running = None
    for kernel_tap in range(5):
        offset_input = lax.slice_in_dim(
            padded, kernel_tap * dilation_step, kernel_tap * dilation_step + length, axis=2
        )
        kernel_contribution = jnp.einsum(
            "vslc,co->vslo",
            offset_input,
            kernel_weight[kernel_tap],
            preferred_element_type=jnp.float32,
        )
        running = kernel_contribution if running is None else running + kernel_contribution
    return running


def whiten(factor, block_rows):
    return jax.scipy.linalg.solve_triangular(factor, block_rows.T, lower=True).T


HI = lax.Precision.HIGHEST
MESH_IDS = pl.DeviceIdType.MESH
Z, X, CORE, Y = "batch_0", "batch_1", "batch_2", "chan"
AXES = (Z, X, CORE, Y)
BLOCK = 128
GROUP = 8


def dot_of(a, b, dims, precision=HI):
    return lax.dot_general(
        a, b, (dims, ((), ())), precision=precision, preferred_element_type=jnp.float32
    )


def in_vmem():
    return pl.BlockSpec(memory_space=pltpu.VMEM)


def block_pairs(width):
    return [(i, k) for i in range(width // BLOCK) for k in range(i + 1)]


def share_rows(width, planes):
    rows = len(block_pairs(width)) * BLOCK + GROUP
    return -(-rows // (planes * GROUP)) * GROUP


def moments_kernel(emb_ref, alive_ref, out_ref):
    views, tokens, width = emb_ref.shape
    pairs = block_pairs(width)
    at = len(pairs) * BLOCK
    alive = alive_ref[...]
    for v in range(views):
        masked = emb_ref[v] * alive
        for i in range(width // BLOCK):
            wide = (i + 1) * BLOCK
            strip = dot_of(
                masked[:, i * BLOCK : wide], masked[:, :wide], ((0,), (0,))
            )
            for k in range(i + 1):
                b = pairs.index((i, k))
                out_ref[v, b * BLOCK : (b + 1) * BLOCK, :] = strip[:, k * BLOCK : (k + 1) * BLOCK]
        out_ref[v, at:, :] = jnp.zeros((out_ref.shape[1] - at, BLOCK), jnp.float32)
        sums = jnp.sum(masked, axis=0, keepdims=True)
        for k in range(width // BLOCK):
            out_ref[v, at + k : at + k + 1, :] = sums[:, k * BLOCK : (k + 1) * BLOCK]
        count = jnp.sum(alive, axis=0, keepdims=True)
        last = at + width // BLOCK
        out_ref[v, last : last + 1, :] = jnp.broadcast_to(count, (1, BLOCK))


def moments_of(embedded, alive, planes):
    views, tokens, width = embedded.shape
    rows = share_rows(width, planes) * planes
    return pl.pallas_call(
        moments_kernel,
        out_shape=jax.ShapeDtypeStruct((views, rows, BLOCK), jnp.float32),
        in_specs=[in_vmem()] * 2,
        out_specs=in_vmem(),
        compiler_params=pltpu.CompilerParams(vmem_limit_bytes=32 << 20),
        name="moments",
    )(embedded, alive[:, None])


def total_kernel(sizes, part_ref, out_ref, pair_in, mine, plane_in, share, line_in, total, sems):
    depth, across, down = sizes
    planes = across * down
    rows = share.shape[0]
    z, x = lax.axis_index(Z), lax.axis_index(X)
    core, y = lax.axis_index(CORE), lax.axis_index(Y)
    me = x * down + y
    partner = 1 - core
    pair_send, pair_recv, plane_send, plane_recv, line_send, line_recv, back_send, back_recv = sems

    def in_plane(step):
        other = lax.rem(me + step, planes)
        return other, (z, other // down, core, lax.rem(other, down))

    def in_line(step):
        other = lax.rem(z + step, depth)
        return other, (other, x, core, y)

    barrier = pltpu.get_barrier_semaphore()
    pl.semaphore_signal(barrier, inc=1, device_id=(z, x, partner, y), device_id_type=MESH_IDS)
    for step in range(1, planes):
        pl.semaphore_signal(barrier, inc=1, device_id=in_plane(step)[1], device_id_type=MESH_IDS)
    for step in range(1, depth):
        pl.semaphore_signal(barrier, inc=1, device_id=in_line(step)[1], device_id_type=MESH_IDS)
    pl.semaphore_wait(barrier, 1 + planes - 1 + depth - 1)

    def sent(src, dst, send, recv, device):
        return pltpu.make_async_remote_copy(
            src_ref=src, dst_ref=dst, send_sem=send, recv_sem=recv,
            device_id=device, device_id_type=MESH_IDS,
        )

    swap = sent(part_ref.at[partner], pair_in, pair_send, pair_recv, (z, x, partner, y))
    swap.start()
    swap.wait()
    mine[...] = part_ref[core] + pair_in[...]

    def rows_of(index):
        return pl.ds(pl.multiple_of(index * rows, GROUP), rows)

    copies = []
    for step in range(1, planes):
        other, device = in_plane(step)
        copy = sent(
            mine.at[rows_of(other)], plane_in.at[step], plane_send.at[step], plane_recv.at[step], device
        )
        copy.start()
        copies.append(copy)
    for copy in copies:
        copy.wait()
    plane_in[0] = mine[rows_of(me)]
    acc = None
    for source in range(planes):
        piece = plane_in[lax.rem(me - source + planes, planes)]
        acc = piece if acc is None else acc + piece
    share[...] = acc

    copies = []
    for step in range(1, depth):
        _, device = in_line(step)
        copy = sent(share, line_in.at[step], line_send.at[step], line_recv.at[step], device)
        copy.start()
        copies.append(copy)
    for copy in copies:
        copy.wait()
    line_in[0] = share[...]
    acc = None
    for source in range(depth):
        piece = line_in[lax.rem(z - source + depth, depth)]
        acc = piece if acc is None else acc + piece
    total[...] = acc

    copies = []
    for step in range(1, planes):
        _, device = in_plane(step)
        copy = sent(
            total, out_ref.at[rows_of(me)], back_send.at[step], back_recv.at[step], device
        )
        copy.start()
        copies.append(copy)
    out_ref[rows_of(me)] = total[...]
    for copy in copies:
        copy.wait()


def total_moments(parts, mesh_sizes):
    depth, across, down = mesh_sizes
    planes = across * down
    _, all_rows, lanes = parts.shape
    rows = all_rows // planes
    dma = pltpu.SemaphoreType.DMA

    def kernel(part_ref, out_ref, pair_in, mine, plane_in, share, line_in, total, *sems):
        total_kernel(mesh_sizes, part_ref, out_ref, pair_in, mine, plane_in, share, line_in, total, sems)

    return pl.pallas_call(
        kernel,
        out_shape=jax.ShapeDtypeStruct((all_rows, lanes), jnp.float32),
        in_specs=[in_vmem()],
        out_specs=in_vmem(),
        scratch_shapes=[
            pltpu.VMEM((all_rows, lanes), jnp.float32),
            pltpu.VMEM((all_rows, lanes), jnp.float32),
            pltpu.VMEM((planes, rows, lanes), jnp.float32),
            pltpu.VMEM((rows, lanes), jnp.float32),
            pltpu.VMEM((depth, rows, lanes), jnp.float32),
            pltpu.VMEM((rows, lanes), jnp.float32),
            dma, dma,
            dma((planes,)), dma((planes,)),
            dma((depth,)), dma((depth,)),
            dma((planes,)), dma((planes,)),
        ],
        compiler_params=pltpu.CompilerParams(
            collective_id=1, has_side_effects=True, vmem_limit_bytes=32 << 20
        ),
        name="total_moments",
    )(parts)


def splat_row(v, a):
    return jnp.broadcast_to(v[a : a + 1, :], (GROUP, BLOCK))


def splat_lane(v, j):
    return jnp.broadcast_to(v[:, j : j + 1], (GROUP, BLOCK))


def base_inverse(load, store):
    count = BLOCK // GROUP
    groups = [load(g) for g in range(count)]
    lane = lax.broadcasted_iota(jnp.int32, (GROUP, BLOCK), 1)
    sub = lax.broadcasted_iota(jnp.int32, (GROUP, BLOCK), 0)
    steps = range(GROUP)
    for p in range(count):
        j = GROUP * p
        v = groups[p]
        cols = [splat_lane(v, j + a) for a in steps]
        e = [[splat_row(cols[a], b) if b >= a else None for a in steps] for b in steps]
        low = [[None] * GROUP for _ in steps]
        rec = []
        for a in steps:
            rec.append(1.0 / e[a][a])
            for b in range(a + 1, GROUP):
                low[b][a] = e[b][a] * rec[a]
            for b in range(a + 1, GROUP):
                for c in range(a + 1, b + 1):
                    e[b][c] = e[b][c] - low[b][a] * e[c][a]
        panel = (lane >= j) & (lane < j + GROUP)
        rows = []
        for a in steps:
            r = jnp.where(panel, jnp.where(lane == j + a, 1.0, 0.0), splat_row(v, a))
            for b in range(a):
                r = r - low[a][b] * rows[b]
            rows.append(r)
        out = None
        for a in steps:
            r = rows[a] * lax.rsqrt(e[a][a])
            out = r if out is None else jnp.where(sub == a, r, out)
        store(p, jnp.where(lane < j + GROUP, out, 0.0))
        for g in range(p + 1, count):
            x = groups[g]
            w = []
            acc = jnp.where(panel, 0.0, x)
            for a in steps:
                t = splat_lane(x, j + a)
                for b in range(a):
                    t = t - low[a][b] * w[b]
                w.append(t)
                acc = acc - (t * rec[a]) * rows[a]
            groups[g] = acc


def factor_kernel(total_ref, out_ref, work, m_ref):
    width = work.shape[1]
    blocks = width // BLOCK
    pairs = block_pairs(width)
    at = len(pairs) * BLOCK
    tail = total_ref[at : at + GROUP, :]
    count = tail[blocks : blocks + 1, 0:1]
    center = jnp.concatenate([tail[k : k + 1, :] for k in range(blocks)], axis=1) / count
    first = lax.broadcasted_iota(jnp.int32, (GROUP, width), 0) == 0
    center8 = jnp.where(first, jnp.broadcast_to(center, (GROUP, width)), 0.0)
    eye = lax.broadcasted_iota(jnp.int32, (BLOCK, BLOCK), 0) == lax.broadcasted_iota(
        jnp.int32, (BLOCK, BLOCK), 1
    )
    for b, (i, k) in enumerate(pairs):
        outer = dot_of(
            center8[:, i * BLOCK : (i + 1) * BLOCK], center8[:, k * BLOCK : (k + 1) * BLOCK], ((0,), (0,))
        )
        block = total_ref[b * BLOCK : (b + 1) * BLOCK, :] / count - outer
        if i == k:
            block = block + jnp.where(eye, EPS_COV, 0.0)
        work[i * BLOCK : (i + 1) * BLOCK, k * BLOCK : (k + 1) * BLOCK] = block
        if i != k:
            work[k * BLOCK : (k + 1) * BLOCK, i * BLOCK : (i + 1) * BLOCK] = block.T
    row_block = lax.broadcasted_iota(jnp.int32, (width, BLOCK), 0) // BLOCK
    col_block = lax.broadcasted_iota(jnp.int32, (width, width), 1) // BLOCK
    strip_block = lax.broadcasted_iota(jnp.int32, (BLOCK, width), 1) // BLOCK
    strip_eye = jnp.where(
        lax.broadcasted_iota(jnp.int32, (BLOCK, width), 1) % BLOCK
        == lax.broadcasted_iota(jnp.int32, (BLOCK, width), 0),
        1.0,
        0.0,
    )

    def step(k, _):
        here = pl.multiple_of(k * BLOCK, BLOCK)

        def load(g):
            return work[pl.ds(pl.multiple_of(here + GROUP * g, GROUP), GROUP), pl.ds(here, BLOCK)]

        def store(g, val):
            m_ref[GROUP * g : GROUP * (g + 1), :] = val

        base_inverse(load, store)
        m = m_ref[...]
        col = jnp.where(row_block > k, work[:, pl.ds(here, BLOCK)], 0.0)
        left = dot_of(col, m, ((1,), (1,)))
        row = jnp.where(strip_block == k, strip_eye, work[pl.ds(here, BLOCK), :])
        across = dot_of(m, row, ((1,), (0,)))
        work[...] = jnp.where(col_block == k, 0.0, work[...]) - dot_of(left, across, ((1,), (0,)))
        work[pl.ds(here, BLOCK), :] = jnp.where(strip_block <= k, across, 0.0)
        return 0

    lax.fori_loop(0, blocks, step, 0)
    out_ref[:width, :] = work[...]
    out_ref[width:, :] = center8


def inverse_factor(total, width):
    return pl.pallas_call(
        factor_kernel,
        out_shape=jax.ShapeDtypeStruct((width + GROUP, width), jnp.float32),
        in_specs=[in_vmem()],
        out_specs=in_vmem(),
        scratch_shapes=[
            pltpu.VMEM((width, width), jnp.float32),
            pltpu.VMEM((BLOCK, BLOCK), jnp.float32),
        ],
        compiler_params=pltpu.CompilerParams(vmem_limit_bytes=32 << 20),
        name="inverse_factor",
    )(total)


def swap_kernel(own_ref, out_ref, send, recv):
    z, x = lax.axis_index(Z), lax.axis_index(X)
    core, y = lax.axis_index(CORE), lax.axis_index(Y)
    other = (z, x, 1 - core, y)
    barrier = pltpu.get_barrier_semaphore()
    pl.semaphore_signal(barrier, inc=1, device_id=other, device_id_type=MESH_IDS)
    pl.semaphore_wait(barrier, 1)
    copy = pltpu.make_async_remote_copy(
        src_ref=own_ref, dst_ref=out_ref, send_sem=send, recv_sem=recv,
        device_id=other, device_id_type=MESH_IDS,
    )
    copy.start()
    copy.wait()


def from_partner(own):
    return pl.pallas_call(
        swap_kernel,
        out_shape=jax.ShapeDtypeStruct(own.shape, own.dtype),
        in_specs=[in_vmem()],
        out_specs=in_vmem(),
        scratch_shapes=[pltpu.SemaphoreType.DMA, pltpu.SemaphoreType.DMA],
        compiler_params=pltpu.CompilerParams(
            collective_id=2, has_side_effects=True, vmem_limit_bytes=16 << 20
        ),
        name="from_partner",
    )(own)


def whiten_kernel(emb_ref, alive_ref, own_ref, other_ref, out_ref, gap_ref):
    views, tokens, width = emb_ref.shape
    core = lax.axis_index(CORE)
    alive = alive_ref[...]
    for ref, v in ((own_ref, core), (other_ref, 1 - core)):
        centered = (emb_ref[v] - ref[width : width + 1, :]) * alive
        out_ref[v] = dot_of(centered, ref[:width, :], ((1,), (1,)))
    gap = out_ref[0] - out_ref[1]
    ones = jnp.ones((GROUP, width), jnp.float32)
    sums = dot_of(ones, gap * gap, ((1,), (1,))) / width
    for k in range(tokens // BLOCK):
        gap_ref[k : k + 1, :] = sums[0:1, k * BLOCK : (k + 1) * BLOCK]


def whitened_rows(embedded, alive, own, other):
    views, tokens, width = embedded.shape
    whitened, gap = pl.pallas_call(
        whiten_kernel,
        out_shape=(
            jax.ShapeDtypeStruct(embedded.shape, jnp.float32),
            jax.ShapeDtypeStruct((tokens // BLOCK, BLOCK), jnp.float32),
        ),
        in_specs=[in_vmem()] * 4,
        out_specs=(in_vmem(), in_vmem()),
        compiler_params=pltpu.CompilerParams(vmem_limit_bytes=32 << 20),
        name="whitened_rows",
    )(embedded, alive[:, None], own, other)
    return whitened, gap.reshape(tokens)


def whitening(embedded, alive, sizes):
    width = embedded.shape[2]
    parts = moments_of(embedded, alive, sizes[1] * sizes[2])
    total = total_moments(parts, sizes)
    own = inverse_factor(total, width)
    other = from_partner(own)
    return whitened_rows(embedded, alive, own, other)


def shards(monomers, keep_mask, lengths, norm_gain, weight_a, weight_b):
    sequences = lengths.shape[0]
    tokens_dev = monomers.shape[0]
    length = tokens_dev // sequences
    channel_count = norm_gain.shape[0]
    positions = lax.broadcasted_iota(jnp.int32, (sequences, length), 1)
    alive = (positions < lengths[:, None]).astype(jnp.float32).reshape(tokens_dev)
    kept_rows = keep_mask.astype(jnp.float32) * alive[None, :]
    gathered = gathered_copies(monomers, "chan", 1)
    viewed = gathered.astype(jnp.float32)[None] * kept_rows[:, :, None]
    square_mean = jnp.mean(viewed * viewed, axis=-1, keepdims=True)
    normed = (viewed * lax.rsqrt(square_mean + EPS_NORM) * norm_gain).astype(jnp.bfloat16)
    padded_in = pad_positions(normed.reshape(2, sequences, length, channel_count), 1)
    full_a, full_b = (
        lax.all_gather(weight_a, BATCH, axis=1, tiled=True),
        lax.all_gather(weight_b, BATCH, axis=2, tiled=True),
    )
    hidden_pre = conv_taps(padded_in, full_a, 1, length)
    hidden = smooth_gate(hidden_pre).astype(jnp.bfloat16)
    padded_hidden = pad_positions(hidden, 2)
    partial_embed = conv_taps(padded_hidden, full_b, 2, length)
    partial_embed = partial_embed.reshape(2, tokens_dev, partial_embed.shape[3])
    embedded = summed_on_arrival(partial_embed, "chan", 1)
    row_count = embedded.shape[1]
    embed_width = embedded.shape[2]
    own_alive = lax.dynamic_slice_in_dim(alive, lax.axis_index("chan") * row_count, row_count, 0)
    sizes = (lax.axis_size(Z), lax.axis_size(X), lax.axis_size(Y))
    return whitening(embedded, own_alive, sizes)


def solution(mesh):
    torus = Mesh(
        mesh.devices.reshape(8, 4, 2, mesh.shape["chan"]), ("batch_0", "batch_1", "batch_2", "chan")
    )
    in_specs = (
        P(BATCH, "chan"),
        P(None, BATCH),
        P(BATCH),
        P(),
        P(None, BATCH, "chan"),
        P(None, "chan", BATCH),
    )
    out_specs = (P(None, BATCH_CHAN, None), P(BATCH_CHAN))
    return jax.shard_map(
        shards, mesh=torus, in_specs=in_specs, out_specs=out_specs, check_vma=False
    )
```

```python
import jax
import jax.numpy as jnp
from jax import lax
from jax.experimental import pallas as pl
from jax.experimental.pallas import tpu as pltpu
from jax.sharding import Mesh
from jax.sharding import PartitionSpec as P

BATCH = ("batch_0", "batch_1", "batch_2")
BATCH_CHAN = ("batch_0", "batch_1", "batch_2", "chan")


EPS_NORM = 1e-05
EPS_COV = 0.0001
HI = lax.Precision.HIGHEST
MESH_IDS = pl.DeviceIdType.MESH
Z, X, CORE, Y = "batch_0", "batch_1", "batch_2", "chan"
AXES = (Z, X, CORE, Y)
BLOCK = 128
GROUP = 8


def dot_of(a, b, dims, precision=HI):
    return lax.dot_general(
        a, b, (dims, ((), ())), precision=precision, preferred_element_type=jnp.float32
    )


def in_vmem():
    return pl.BlockSpec(memory_space=pltpu.VMEM)


def block_pairs(width):
    return [(i, k) for i in range(width // BLOCK) for k in range(i + 1)]


def share_rows(width, planes):
    rows = len(block_pairs(width)) * BLOCK + GROUP
    return -(-rows // (planes * GROUP)) * GROUP


def moments_kernel(emb_ref, alive_ref, out_ref):
    views, tokens, width = emb_ref.shape
    pairs = block_pairs(width)
    at = len(pairs) * BLOCK
    alive = alive_ref[...]
    for v in range(views):
        masked = emb_ref[v] * alive
        for i in range(width // BLOCK):
            wide = (i + 1) * BLOCK
            strip = dot_of(
                masked[:, i * BLOCK : wide], masked[:, :wide], ((0,), (0,))
            )
            for k in range(i + 1):
                b = pairs.index((i, k))
                out_ref[v, b * BLOCK : (b + 1) * BLOCK, :] = strip[:, k * BLOCK : (k + 1) * BLOCK]
        out_ref[v, at:, :] = jnp.zeros((out_ref.shape[1] - at, BLOCK), jnp.float32)
        sums = jnp.sum(masked, axis=0, keepdims=True)
        for k in range(width // BLOCK):
            out_ref[v, at + k : at + k + 1, :] = sums[:, k * BLOCK : (k + 1) * BLOCK]
        count = jnp.sum(alive, axis=0, keepdims=True)
        last = at + width // BLOCK
        out_ref[v, last : last + 1, :] = jnp.broadcast_to(count, (1, BLOCK))


def moments_of(embedded, alive, planes):
    views, tokens, width = embedded.shape
    rows = share_rows(width, planes) * planes
    return pl.pallas_call(
        moments_kernel,
        out_shape=jax.ShapeDtypeStruct((views, rows, BLOCK), jnp.float32),
        in_specs=[in_vmem()] * 2,
        out_specs=in_vmem(),
        compiler_params=pltpu.CompilerParams(vmem_limit_bytes=32 << 20),
        name="moments",
    )(embedded, alive[:, None])


def total_kernel(sizes, part_ref, out_ref, pair_in, mine, plane_in, share, line_in, total, sems):
    depth, across, down = sizes
    planes = across * down
    rows = share.shape[0]
    z, x = lax.axis_index(Z), lax.axis_index(X)
    core, y = lax.axis_index(CORE), lax.axis_index(Y)
    me = x * down + y
    partner = 1 - core
    pair_send, pair_recv, plane_send, plane_recv, line_send, line_recv, back_send, back_recv = sems

    def in_plane(step):
        other = lax.rem(me + step, planes)
        return other, (z, other // down, core, lax.rem(other, down))

    def in_line(step):
        other = lax.rem(z + step, depth)
        return other, (other, x, core, y)

    barrier = pltpu.get_barrier_semaphore()
    pl.semaphore_signal(barrier, inc=1, device_id=(z, x, partner, y), device_id_type=MESH_IDS)
    for step in range(1, planes):
        pl.semaphore_signal(barrier, inc=1, device_id=in_plane(step)[1], device_id_type=MESH_IDS)
    for step in range(1, depth):
        pl.semaphore_signal(barrier, inc=1, device_id=in_line(step)[1], device_id_type=MESH_IDS)
    pl.semaphore_wait(barrier, 1 + planes - 1 + depth - 1)

    def sent(src, dst, send, recv, device):
        return pltpu.make_async_remote_copy(
            src_ref=src, dst_ref=dst, send_sem=send, recv_sem=recv,
            device_id=device, device_id_type=MESH_IDS,
        )

    swap = sent(part_ref.at[partner], pair_in, pair_send, pair_recv, (z, x, partner, y))
    swap.start()
    swap.wait()
    mine[...] = part_ref[core] + pair_in[...]

    def rows_of(index):
        return pl.ds(pl.multiple_of(index * rows, GROUP), rows)

    copies = []
    for step in range(1, planes):
        other, device = in_plane(step)
        copy = sent(
            mine.at[rows_of(other)], plane_in.at[step], plane_send.at[step], plane_recv.at[step], device
        )
        copy.start()
        copies.append(copy)
    for copy in copies:
        copy.wait()
    plane_in[0] = mine[rows_of(me)]
    acc = None
    for source in range(planes):
        piece = plane_in[lax.rem(me - source + planes, planes)]
        acc = piece if acc is None else acc + piece
    share[...] = acc

    copies = []
    for step in range(1, depth):
        _, device = in_line(step)
        copy = sent(share, line_in.at[step], line_send.at[step], line_recv.at[step], device)
        copy.start()
        copies.append(copy)
    for copy in copies:
        copy.wait()
    line_in[0] = share[...]
    acc = None
    for source in range(depth):
        piece = line_in[lax.rem(z - source + depth, depth)]
        acc = piece if acc is None else acc + piece
    total[...] = acc

    copies = []
    for step in range(1, planes):
        _, device = in_plane(step)
        copy = sent(
            total, out_ref.at[rows_of(me)], back_send.at[step], back_recv.at[step], device
        )
        copy.start()
        copies.append(copy)
    out_ref[rows_of(me)] = total[...]
    for copy in copies:
        copy.wait()


def total_moments(parts, mesh_sizes):
    depth, across, down = mesh_sizes
    planes = across * down
    _, all_rows, lanes = parts.shape
    rows = all_rows // planes
    dma = pltpu.SemaphoreType.DMA

    def kernel(part_ref, out_ref, pair_in, mine, plane_in, share, line_in, total, *sems):
        total_kernel(mesh_sizes, part_ref, out_ref, pair_in, mine, plane_in, share, line_in, total, sems)

    return pl.pallas_call(
        kernel,
        out_shape=jax.ShapeDtypeStruct((all_rows, lanes), jnp.float32),
        in_specs=[in_vmem()],
        out_specs=in_vmem(),
        scratch_shapes=[
            pltpu.VMEM((all_rows, lanes), jnp.float32),
            pltpu.VMEM((all_rows, lanes), jnp.float32),
            pltpu.VMEM((planes, rows, lanes), jnp.float32),
            pltpu.VMEM((rows, lanes), jnp.float32),
            pltpu.VMEM((depth, rows, lanes), jnp.float32),
            pltpu.VMEM((rows, lanes), jnp.float32),
            dma, dma,
            dma((planes,)), dma((planes,)),
            dma((depth,)), dma((depth,)),
            dma((planes,)), dma((planes,)),
        ],
        compiler_params=pltpu.CompilerParams(
            collective_id=1, has_side_effects=True, vmem_limit_bytes=32 << 20
        ),
        name="total_moments",
    )(parts)


def splat_row(v, a):
    return jnp.broadcast_to(v[a : a + 1, :], (GROUP, BLOCK))


def splat_lane(v, j):
    return jnp.broadcast_to(v[:, j : j + 1], (GROUP, BLOCK))


def base_inverse(load, store):
    count = BLOCK // GROUP
    groups = [load(g) for g in range(count)]
    lane = lax.broadcasted_iota(jnp.int32, (GROUP, BLOCK), 1)
    sub = lax.broadcasted_iota(jnp.int32, (GROUP, BLOCK), 0)
    steps = range(GROUP)
    for p in range(count):
        j = GROUP * p
        v = groups[p]
        cols = [splat_lane(v, j + a) for a in steps]
        e = [[splat_row(cols[a], b) if b >= a else None for a in steps] for b in steps]
        low = [[None] * GROUP for _ in steps]
        rec = []
        for a in steps:
            rec.append(1.0 / e[a][a])
            for b in range(a + 1, GROUP):
                low[b][a] = e[b][a] * rec[a]
            for b in range(a + 1, GROUP):
                for c in range(a + 1, b + 1):
                    e[b][c] = e[b][c] - low[b][a] * e[c][a]
        panel = (lane >= j) & (lane < j + GROUP)
        rows = []
        for a in steps:
            r = jnp.where(panel, jnp.where(lane == j + a, 1.0, 0.0), splat_row(v, a))
            for b in range(a):
                r = r - low[a][b] * rows[b]
            rows.append(r)
        out = None
        for a in steps:
            r = rows[a] * lax.rsqrt(e[a][a])
            out = r if out is None else jnp.where(sub == a, r, out)
        store(p, jnp.where(lane < j + GROUP, out, 0.0))
        for g in range(p + 1, count):
            x = groups[g]
            w = []
            acc = jnp.where(panel, 0.0, x)
            for a in steps:
                t = splat_lane(x, j + a)
                for b in range(a):
                    t = t - low[a][b] * w[b]
                w.append(t)
                acc = acc - (t * rec[a]) * rows[a]
            groups[g] = acc


def factor_kernel(total_ref, out_ref, work, m_ref):
    width = work.shape[1]
    blocks = width // BLOCK
    pairs = block_pairs(width)
    at = len(pairs) * BLOCK
    tail = total_ref[at : at + GROUP, :]
    count = tail[blocks : blocks + 1, 0:1]
    center = jnp.concatenate([tail[k : k + 1, :] for k in range(blocks)], axis=1) / count
    first = lax.broadcasted_iota(jnp.int32, (GROUP, width), 0) == 0
    center8 = jnp.where(first, jnp.broadcast_to(center, (GROUP, width)), 0.0)
    eye = lax.broadcasted_iota(jnp.int32, (BLOCK, BLOCK), 0) == lax.broadcasted_iota(
        jnp.int32, (BLOCK, BLOCK), 1
    )
    for b, (i, k) in enumerate(pairs):
        outer = dot_of(
            center8[:, i * BLOCK : (i + 1) * BLOCK], center8[:, k * BLOCK : (k + 1) * BLOCK], ((0,), (0,))
        )
        block = total_ref[b * BLOCK : (b + 1) * BLOCK, :] / count - outer
        if i == k:
            block = block + jnp.where(eye, EPS_COV, 0.0)
        work[i * BLOCK : (i + 1) * BLOCK, k * BLOCK : (k + 1) * BLOCK] = block
        if i != k:
            work[k * BLOCK : (k + 1) * BLOCK, i * BLOCK : (i + 1) * BLOCK] = block.T
    row_block = lax.broadcasted_iota(jnp.int32, (width, BLOCK), 0) // BLOCK
    col_block = lax.broadcasted_iota(jnp.int32, (width, width), 1) // BLOCK
    strip_block = lax.broadcasted_iota(jnp.int32, (BLOCK, width), 1) // BLOCK
    strip_eye = jnp.where(
        lax.broadcasted_iota(jnp.int32, (BLOCK, width), 1) % BLOCK
        == lax.broadcasted_iota(jnp.int32, (BLOCK, width), 0),
        1.0,
        0.0,
    )

    def step(k, _):
        here = pl.multiple_of(k * BLOCK, BLOCK)

        def load(g):
            return work[pl.ds(pl.multiple_of(here + GROUP * g, GROUP), GROUP), pl.ds(here, BLOCK)]

        def store(g, val):
            m_ref[GROUP * g : GROUP * (g + 1), :] = val

        base_inverse(load, store)
        m = m_ref[...]
        col = jnp.where(row_block > k, work[:, pl.ds(here, BLOCK)], 0.0)
        left = dot_of(col, m, ((1,), (1,)))
        row = jnp.where(strip_block == k, strip_eye, work[pl.ds(here, BLOCK), :])
        across = dot_of(m, row, ((1,), (0,)))
        work[...] = jnp.where(col_block == k, 0.0, work[...]) - dot_of(left, across, ((1,), (0,)))
        work[pl.ds(here, BLOCK), :] = jnp.where(strip_block <= k, across, 0.0)
        return 0

    lax.fori_loop(0, blocks, step, 0)
    out_ref[:width, :] = work[...]
    out_ref[width:, :] = center8


def inverse_factor(total, width):
    return pl.pallas_call(
        factor_kernel,
        out_shape=jax.ShapeDtypeStruct((width + GROUP, width), jnp.float32),
        in_specs=[in_vmem()],
        out_specs=in_vmem(),
        scratch_shapes=[
            pltpu.VMEM((width, width), jnp.float32),
            pltpu.VMEM((BLOCK, BLOCK), jnp.float32),
        ],
        compiler_params=pltpu.CompilerParams(vmem_limit_bytes=32 << 20),
        name="inverse_factor",
    )(total)


def swap_kernel(own_ref, out_ref, send, recv):
    z, x = lax.axis_index(Z), lax.axis_index(X)
    core, y = lax.axis_index(CORE), lax.axis_index(Y)
    other = (z, x, 1 - core, y)
    barrier = pltpu.get_barrier_semaphore()
    pl.semaphore_signal(barrier, inc=1, device_id=other, device_id_type=MESH_IDS)
    pl.semaphore_wait(barrier, 1)
    copy = pltpu.make_async_remote_copy(
        src_ref=own_ref, dst_ref=out_ref, send_sem=send, recv_sem=recv,
        device_id=other, device_id_type=MESH_IDS,
    )
    copy.start()
    copy.wait()


def from_partner(own):
    return pl.pallas_call(
        swap_kernel,
        out_shape=jax.ShapeDtypeStruct(own.shape, own.dtype),
        in_specs=[in_vmem()],
        out_specs=in_vmem(),
        scratch_shapes=[pltpu.SemaphoreType.DMA, pltpu.SemaphoreType.DMA],
        compiler_params=pltpu.CompilerParams(
            collective_id=2, has_side_effects=True, vmem_limit_bytes=16 << 20
        ),
        name="from_partner",
    )(own)


def whiten_kernel(emb_ref, alive_ref, own_ref, other_ref, out_ref, gap_ref):
    views, tokens, width = emb_ref.shape
    core = lax.axis_index(CORE)
    alive = alive_ref[...]
    for ref, v in ((own_ref, core), (other_ref, 1 - core)):
        centered = (emb_ref[v] - ref[width : width + 1, :]) * alive
        out_ref[v] = dot_of(centered, ref[:width, :], ((1,), (1,)))
    gap = out_ref[0] - out_ref[1]
    ones = jnp.ones((GROUP, width), jnp.float32)
    sums = dot_of(ones, gap * gap, ((1,), (1,))) / width
    for k in range(tokens // BLOCK):
        gap_ref[k : k + 1, :] = sums[0:1, k * BLOCK : (k + 1) * BLOCK]


def whitened_rows(embedded, alive, own, other):
    views, tokens, width = embedded.shape
    whitened, gap = pl.pallas_call(
        whiten_kernel,
        out_shape=(
            jax.ShapeDtypeStruct(embedded.shape, jnp.float32),
            jax.ShapeDtypeStruct((tokens // BLOCK, BLOCK), jnp.float32),
        ),
        in_specs=[in_vmem()] * 4,
        out_specs=(in_vmem(), in_vmem()),
        compiler_params=pltpu.CompilerParams(vmem_limit_bytes=32 << 20),
        name="whitened_rows",
    )(embedded, alive[:, None], own, other)
    return whitened, gap.reshape(tokens)


def whitening(embedded, alive, sizes):
    width = embedded.shape[2]
    parts = moments_of(embedded, alive, sizes[1] * sizes[2])
    total = total_moments(parts, sizes)
    own = inverse_factor(total, width)
    other = from_partner(own)
    return whitened_rows(embedded, alive, own, other)


def gather_kernel(sizes, xt_ref, wa_ref, wb_ref, xt_out, wa_out, wb_out, sems):
    depth, across, down = sizes
    z, x = lax.axis_index(Z), lax.axis_index(X)
    core, y = lax.axis_index(CORE), lax.axis_index(Y)
    (xs, xr, zs, zr, ps, pr, cs, cr, local) = sems

    barrier = pltpu.get_barrier_semaphore()
    peers = [(lax.rem(z + s, depth), x, core, y) for s in range(1, depth)]
    peers += [(z, lax.rem(x + s, across), core, y) for s in range(1, across)]
    peers += [(z, x, core, lax.rem(y + s, down)) for s in range(1, down)]
    peers += [(z, x, 1 - core, y)]
    for peer in peers:
        pl.semaphore_signal(barrier, inc=1, device_id=peer, device_id_type=MESH_IDS)
    pl.semaphore_wait(barrier, len(peers))

    started = []

    def send(src, dst, send_sem, recv_sem, device):
        copy = pltpu.make_async_remote_copy(
            src_ref=src, dst_ref=dst, send_sem=send_sem, recv_sem=recv_sem,
            device_id=device, device_id_type=MESH_IDS,
        )
        copy.start()
        started.append(copy)
        return copy

    weights = ((wa_ref, wa_out), (wb_ref, wb_out))
    own = []
    for i, (src, dst) in enumerate(((xt_ref, xt_out.at[y]), (wa_ref, wa_out.at[z, x, core]), (wb_ref, wb_out.at[z, x, core]))):
        copy = pltpu.make_async_copy(src, dst, local.at[i])
        copy.start()
        own.append(copy)
    from_y = []
    for s in (2, 1, 3):
        from_y.append(send(xt_ref, xt_out.at[y], xs.at[s], xr.at[s], (z, x, core, lax.rem(y + s, down))))
    along_z = {}
    order = sorted(range(1, depth), key=lambda s: (min(s, depth - s), s))
    for i, (src, dst) in enumerate(weights):
        for s in order:
            along_z[i, s] = send(
                src, dst.at[z, x, core], zs.at[i, s], zr.at[i, s], (lax.rem(z + s, depth), x, core, y)
            )
    along_x, to_core = {}, {}

    def to_partner(i, s, t):
        zz = lax.rem(z + depth - s, depth)
        xx = lax.rem(x + across - t, across)
        src, dst = weights[i]
        here = src if s == 0 and t == 0 else dst.at[zz, xx, core]
        to_core[i, s, t] = send(
            here, dst.at[zz, xx, core], cs.at[i, s, t], cr.at[i, s, t], (z, x, 1 - core, y)
        )

    for i, (src, dst) in enumerate(weights):
        for s in [0] + order:
            zz = lax.rem(z + depth - s, depth)
            if s:
                along_z[i, s].wait_recv()
            here = dst.at[zz, x, core] if s else src
            for t in range(1, across):
                along_x[i, s, t] = send(
                    here, dst.at[zz, x, core], ps.at[i, s, t], pr.at[i, s, t],
                    (z, lax.rem(x + t, across), core, y),
                )
            to_partner(i, s, 0)
    for i in range(2):
        for s in [0] + order:
            for t in range(1, across):
                along_x[i, s, t].wait_recv()
                to_partner(i, s, t)
    for copy in to_core.values():
        copy.wait_recv()
    for copy in from_y:
        copy.wait_recv()
    for copy in started:
        copy.wait_send()
    for copy in own:
        copy.wait()


def gathered_inputs(xt, wa, wb, sizes):
    depth, across, down = sizes
    dma = pltpu.SemaphoreType.DMA
    anywhere = pl.BlockSpec(memory_space=pl.ANY)

    def kernel(xt_ref, wa_ref, wb_ref, xt_out, wa_out, wb_out, *sems):
        gather_kernel(sizes, xt_ref, wa_ref, wb_ref, xt_out, wa_out, wb_out, sems)

    return pl.pallas_call(
        kernel,
        out_shape=(
            jax.ShapeDtypeStruct((down, *xt.shape), xt.dtype),
            jax.ShapeDtypeStruct((depth, across, 2, *wa.shape), wa.dtype),
            jax.ShapeDtypeStruct((depth, across, 2, *wb.shape), wb.dtype),
        ),
        in_specs=[anywhere] * 3,
        out_specs=(anywhere,) * 3,
        scratch_shapes=[
            dma((down,)), dma((down,)),
            dma((2, depth)), dma((2, depth)),
            dma((2, depth, across)), dma((2, depth, across)),
            dma((2, depth, across)), dma((2, depth, across)),
            dma((3,)),
        ],
        compiler_params=pltpu.CompilerParams(collective_id=3, has_side_effects=True),
        name="gathered_inputs",
    )(xt, wa, wb)


def gate(values):
    return 0.5 * values * (1.0 + jnp.tanh(0.7978845608 * (values + 0.044715 * values * values * values)))


PAD = 8
ROWS = 128


def conv_kernel(
    sizes, xt_ref, wa_ref, wb_ref, gain_ref, kept_ref, out_ref, n_ref, w_ref, stage, p_ref, h_ref, q_ref, cols
):
    sequences, length, out_width, taps = sizes
    channels, tokens = xt_ref.shape
    chunks, chunk_rows, lanes = wa_ref.shape
    eye = lax.broadcasted_iota(jnp.int32, (BLOCK, BLOCK), 0) == lax.broadcasted_iota(
        jnp.int32, (BLOCK, BLOCK), 1
    )
    squares = jnp.zeros((1, tokens), jnp.float32)
    for i in range(channels // BLOCK):
        part = xt_ref[i * BLOCK : (i + 1) * BLOCK, :].astype(jnp.float32)
        squares = squares + jnp.sum(part * part, axis=0, keepdims=True)
    scale = lax.rsqrt(squares / channels + EPS_NORM)
    for i in range(channels // BLOCK):
        part = xt_ref[i * BLOCK : (i + 1) * BLOCK, :].astype(jnp.float32)
        gain = jnp.sum(
            jnp.where(eye, jnp.broadcast_to(gain_ref[i : i + 1, :], (BLOCK, BLOCK)), 0.0), axis=1, keepdims=True
        )
        normed = (part * scale * gain).astype(jnp.bfloat16)
        n_ref[:, i * BLOCK : (i + 1) * BLOCK] = normed.T

    position = lax.broadcasted_iota(jnp.int32, (GROUP, tokens), 1) % length
    for k in range(taps):
        move = k - taps // 2
        rolled = kept_ref[...] if move == 0 else pltpu.roll(kept_ref[...], (-move) % tokens, 1)
        inside = (position + move >= 0) & (position + move < length)
        cols[k] = jnp.where(inside, rolled, 0.0).T

    group = 4
    def relay(q, _):
        for i in range(group):
            stage[i * chunk_rows : (i + 1) * chunk_rows, :] = wa_ref[q * group + i].astype(jnp.float32)
        at = pl.multiple_of(q * group * chunk_rows, group * chunk_rows)
        w_ref[pl.ds(at, group * chunk_rows), :] = stage[...].astype(jnp.bfloat16)
        return 0

    lax.fori_loop(0, chunks // group, relay, 0)

    width = lanes // taps
    for pad in (p_ref, q_ref):
        pad[0:PAD, :] = jnp.zeros((PAD, pad.shape[1]), jnp.float32)
        pad[PAD + length :, :] = jnp.zeros((PAD, pad.shape[1]), jnp.float32)

    def sequence(s, _):
        start = pl.multiple_of(s * length, length)
        for r in range(length // ROWS):
            p_ref[PAD + r * ROWS : PAD + (r + 1) * ROWS, :] = jnp.dot(
                n_ref[pl.ds(start + r * ROWS, ROWS), :], w_ref[...], preferred_element_type=jnp.float32
            )
        for r in range(length // ROWS):
            for v in range(2):
                acc = None
                for k in range(taps):
                    first = PAD + r * ROWS + k - taps // 2
                    piece = p_ref[first : first + ROWS, k * width : (k + 1) * width]
                    piece = piece * cols[k, pl.ds(start + r * ROWS, ROWS), v : v + 1]
                    acc = piece if acc is None else acc + piece
                h_ref[v, r * ROWS : (r + 1) * ROWS, :] = gate(acc).astype(jnp.bfloat16)
        for v in range(2):
            for k in range(taps):
                taps_b = wb_ref[:, k].astype(jnp.float32).reshape(out_width, width).astype(jnp.bfloat16)
                q_ref[PAD : PAD + length, :] = lax.dot_general(
                    h_ref[v], taps_b, (((1,), (1,)), ((), ())), preferred_element_type=jnp.float32
                )
                first = PAD + 2 * (k - taps // 2)
                piece = q_ref[first : first + length, :]
                if k == 0:
                    out_ref[v, pl.ds(start, length), :] = piece
                else:
                    out_ref[v, pl.ds(start, length), :] += piece
        return 0

    lax.fori_loop(0, sequences, sequence, 0)


def conv_block(xt, wa, wb, gain, kept, sequences):
    channels, tokens = xt.shape
    chunks, chunk_rows, lanes = wa.shape
    taps, rows, width = wb.shape[1:]
    out_width = wb.shape[0] * rows
    length = tokens // sequences
    sizes = (sequences, length, out_width, taps)
    bf, f32 = jnp.bfloat16, jnp.float32

    def kernel(*refs):
        conv_kernel(sizes, *refs)

    return pl.pallas_call(
        kernel,
        out_shape=jax.ShapeDtypeStruct((2, tokens, out_width), f32),
        in_specs=[in_vmem()] * 5,
        out_specs=in_vmem(),
        scratch_shapes=[
            pltpu.VMEM((tokens, channels), bf),
            pltpu.VMEM((channels, lanes), bf),
            pltpu.VMEM((4 * chunk_rows, lanes), f32),
            pltpu.VMEM((length + 2 * PAD, lanes), f32),
            pltpu.VMEM((2, length, width), bf),
            pltpu.VMEM((length + 2 * PAD, out_width), f32),
            pltpu.VMEM((taps, tokens, GROUP), f32),
        ],
        compiler_params=pltpu.CompilerParams(vmem_limit_bytes=60 << 20),
        name="conv_block",
    )(xt, wa, wb, gain, kept)


def spread_sum_kernel(down, part_ref, out_ref, inbox, send, recv):
    z, x = lax.axis_index(Z), lax.axis_index(X)
    core, y = lax.axis_index(CORE), lax.axis_index(Y)
    rows = out_ref.shape[1]
    barrier = pltpu.get_barrier_semaphore()
    for s in range(1, down):
        pl.semaphore_signal(
            barrier, inc=1, device_id=(z, x, core, lax.rem(y + s, down)), device_id_type=MESH_IDS
        )
    pl.semaphore_wait(barrier, down - 1)
    copies = []
    for s in (2, 1, 3):
        other = lax.rem(y + s, down)
        copy = pltpu.make_async_remote_copy(
            src_ref=part_ref.at[:, pl.ds(pl.multiple_of(other * rows, rows), rows), :],
            dst_ref=inbox.at[s],
            send_sem=send.at[s], recv_sem=recv.at[s],
            device_id=(z, x, core, other), device_id_type=MESH_IDS,
        )
        copy.start()
        copies.append(copy)
    for copy in copies:
        copy.wait()
    mine = part_ref[:, pl.ds(pl.multiple_of(y * rows, rows), rows), :]
    out_ref[...] = ((mine + inbox[1]) + inbox[2]) + inbox[3]


def spread_sum(part, down):
    views, tokens, width = part.shape
    rows = tokens // down
    dma = pltpu.SemaphoreType.DMA
    return pl.pallas_call(
        lambda *refs: spread_sum_kernel(down, *refs),
        out_shape=jax.ShapeDtypeStruct((views, rows, width), jnp.float32),
        in_specs=[in_vmem()],
        out_specs=in_vmem(),
        scratch_shapes=[
            pltpu.VMEM((down, views, rows, width), jnp.float32), dma((down,)), dma((down,)),
        ],
        compiler_params=pltpu.CompilerParams(
            collective_id=4, has_side_effects=True, vmem_limit_bytes=32 << 20
        ),
        name="spread_sum",
    )(part)


def shards(monomers, keep_mask, lengths, norm_gain, weight_a, weight_b):
    sequences = lengths.shape[0]
    tokens = monomers.shape[0]
    length = tokens // sequences
    taps, rows, width = weight_a.shape
    sizes = (lax.axis_size(Z), lax.axis_size(X), lax.axis_size(Y))
    positions = lax.broadcasted_iota(jnp.int32, (sequences, length), 1)
    alive = (positions < lengths[:, None]).astype(jnp.float32).reshape(tokens)
    kept = keep_mask.astype(jnp.float32) * alive[None, :]
    kept = jnp.pad(kept, ((0, GROUP - 2), (0, 0)))
    wa = weight_a.transpose(1, 0, 2).reshape(rows, taps * width)
    xt, wa, wb = gathered_inputs(monomers.T, wa, weight_b.transpose(0, 2, 1), sizes)
    part = conv_block(
        xt.reshape(-1, tokens),
        wa.reshape(-1, *wa.shape[3:]),
        wb.reshape(-1, *wb.shape[3:]),
        norm_gain.reshape(-1, BLOCK),
        kept,
        sequences,
    )
    embedded = spread_sum(part, sizes[2])
    own = embedded.shape[1]
    own_alive = lax.dynamic_slice_in_dim(alive, lax.axis_index(Y) * own, own, 0)
    return whitening(embedded, own_alive, sizes)


def solution(mesh):
    torus = Mesh(
        mesh.devices.reshape(8, 4, 2, mesh.shape["chan"]), ("batch_0", "batch_1", "batch_2", "chan")
    )
    in_specs = (
        P(BATCH, "chan"),
        P(None, BATCH),
        P(BATCH),
        P(),
        P(None, BATCH, "chan"),
        P(None, "chan", BATCH),
    )
    out_specs = (P(None, BATCH_CHAN, None), P(BATCH_CHAN))
    return jax.shard_map(
        shards, mesh=torus, in_specs=in_specs, out_specs=out_specs, check_vma=False
    )
```

```python
import jax
import jax.numpy as jnp
from jax import lax
from jax.experimental import pallas as pl
from jax.experimental.pallas import tpu as pltpu
from jax.sharding import Mesh
from jax.sharding import PartitionSpec as P

BATCH = ("batch_0", "batch_1", "batch_2")
BATCH_CHAN = ("batch_0", "batch_1", "batch_2", "chan")


EPS_NORM = 1e-05
EPS_COV = 0.0001
HI = lax.Precision.HIGHEST
MESH_IDS = pl.DeviceIdType.MESH
Z, X, CORE, Y = "batch_0", "batch_1", "batch_2", "chan"
AXES = (Z, X, CORE, Y)
BLOCK = 128
GROUP = 8


def dot_of(a, b, dims, precision=HI):
    return lax.dot_general(
        a, b, (dims, ((), ())), precision=precision, preferred_element_type=jnp.float32
    )


def in_vmem():
    return pl.BlockSpec(memory_space=pltpu.VMEM)


def block_pairs(width):
    return [(i, k) for i in range(width // BLOCK) for k in range(i + 1)]


def share_rows(width, planes):
    rows = len(block_pairs(width)) * BLOCK + GROUP
    return -(-rows // (planes * GROUP)) * GROUP


def alive_column(lengths_ref, tokens, length):
    start = lax.axis_index(Y) * tokens
    limit = lengths_ref[start // length] - lax.rem(start, length)
    return jnp.where(lax.broadcasted_iota(jnp.int32, (tokens, 1), 0) < limit, 1.0, 0.0)


def in_smem():
    return pl.BlockSpec(memory_space=pltpu.SMEM)


def moments_into(emb_ref, alive, out_ref):
    views, tokens, width = emb_ref.shape
    pairs = block_pairs(width)
    at = len(pairs) * BLOCK
    for v in range(views):
        masked = emb_ref[v] * alive
        for i in range(width // BLOCK):
            wide = (i + 1) * BLOCK
            strip = dot_of(
                masked[:, i * BLOCK : wide], masked[:, :wide], ((0,), (0,))
            )
            for k in range(i + 1):
                b = pairs.index((i, k))
                out_ref[v, b * BLOCK : (b + 1) * BLOCK, :] = strip[:, k * BLOCK : (k + 1) * BLOCK]
        out_ref[v, at:, :] = jnp.zeros((out_ref.shape[1] - at, BLOCK), jnp.float32)
        sums = jnp.sum(masked, axis=0, keepdims=True)
        for k in range(width // BLOCK):
            out_ref[v, at + k : at + k + 1, :] = sums[:, k * BLOCK : (k + 1) * BLOCK]
        count = jnp.sum(alive, axis=0, keepdims=True)
        last = at + width // BLOCK
        out_ref[v, last : last + 1, :] = jnp.broadcast_to(count, (1, BLOCK))


def total_kernel(sizes, parts, part_ref, out_ref, pair_in, mine, plane_in, share, line_in, total, *sems):
    depth, across, down = sizes
    planes = across * down
    rows = share.shape[0]
    z, x = lax.axis_index(Z), lax.axis_index(X)
    core, y = lax.axis_index(CORE), lax.axis_index(Y)
    me = x * down + y
    partner = 1 - core
    pair_send, pair_recv, plane_send, plane_recv, line_send, line_recv, back_send, back_recv = sems

    def in_plane(step):
        other = lax.rem(me + step, planes)
        return other, (z, other // down, core, lax.rem(other, down))

    def in_line(step):
        other = lax.rem(z + step, depth)
        return other, (other, x, core, y)

    barrier = pltpu.get_barrier_semaphore()
    pl.semaphore_signal(barrier, inc=1, device_id=(z, x, partner, y), device_id_type=MESH_IDS)
    for step in range(1, planes):
        pl.semaphore_signal(barrier, inc=1, device_id=in_plane(step)[1], device_id_type=MESH_IDS)
    for step in range(1, depth):
        pl.semaphore_signal(barrier, inc=1, device_id=in_line(step)[1], device_id_type=MESH_IDS)
    pl.semaphore_wait(barrier, 1 + planes - 1 + depth - 1)

    def sent(src, dst, send, recv, device):
        copy = pltpu.make_async_remote_copy(
            src_ref=src, dst_ref=dst, send_sem=send, recv_sem=recv,
            device_id=device, device_id_type=MESH_IDS,
        )
        copy.start()
        return copy

    sent(part_ref.at[partner], pair_in, pair_send, pair_recv, (z, x, partner, y)).wait()
    mine[...] = part_ref[core] + pair_in[...]

    starts = [sum(parts[:i]) for i in range(len(parts))]

    def rows_of(index, i):
        return pl.ds(pl.multiple_of(index * rows + starts[i], GROUP), parts[i])

    def within(i):
        return pl.ds(starts[i], parts[i])

    def summed(buffer, own, count, i):
        acc = None
        for source in range(count):
            piece = buffer[lax.rem(own - source + count, count), within(i)]
            acc = piece if acc is None else acc + piece
        return acc

    spread, lines, back = {}, {}, {}
    for i in range(len(parts)):
        for step in range(1, planes):
            other, device = in_plane(step)
            spread[i, step] = sent(
                mine.at[rows_of(other, i)], plane_in.at[step, within(i)],
                plane_send.at[i, step], plane_recv.at[i, step], device,
            )

    def to_line(i):
        for step in range(1, planes):
            spread[i, step].wait_recv()
        plane_in[0, within(i)] = mine[rows_of(me, i)]
        share[within(i)] = summed(plane_in, me, planes, i)
        for step in range(1, depth):
            lines[i, step] = sent(
                share.at[within(i)], line_in.at[step, within(i)],
                line_send.at[i, step], line_recv.at[i, step], in_line(step)[1],
            )

    def to_plane(i):
        for step in range(1, depth):
            lines[i, step].wait_recv()
        line_in[0, within(i)] = share[within(i)]
        total[within(i)] = summed(line_in, z, depth, i)
        for step in range(1, planes):
            back[i, step] = sent(
                total.at[within(i)], out_ref.at[rows_of(me, i)],
                back_send.at[i, step], back_recv.at[i, step], in_plane(step)[1],
            )
        out_ref[rows_of(me, i)] = total[within(i)]

    lag = 2
    for i in range(len(parts) + lag):
        if i < len(parts):
            to_line(i)
        if i >= lag:
            to_plane(i - lag)
    for copy in back.values():
        copy.wait_recv()
    for group in (spread, lines, back):
        for copy in group.values():
            copy.wait_send()


def total_moments(parts, mesh_sizes):
    depth, across, down = mesh_sizes
    planes = across * down
    _, all_rows, lanes = parts.shape
    rows = all_rows // planes
    tiles = rows // GROUP
    pieces = tuple(GROUP * (tiles // 4 + (1 if i < tiles % 4 else 0)) for i in range(4))
    dma = pltpu.SemaphoreType.DMA
    vm = lambda *shape: pltpu.VMEM(shape, jnp.float32)
    return pl.pallas_call(
        lambda *refs: total_kernel(mesh_sizes, pieces, *refs),
        out_shape=jax.ShapeDtypeStruct((all_rows, lanes), jnp.float32),
        in_specs=[in_vmem()],
        out_specs=in_vmem(),
        scratch_shapes=[
            vm(all_rows, lanes),
            vm(all_rows, lanes),
            vm(planes, rows, lanes),
            vm(rows, lanes),
            vm(depth, rows, lanes),
            vm(rows, lanes),
            dma, dma,
            dma((4, planes)), dma((4, planes)),
            dma((4, depth)), dma((4, depth)),
            dma((4, planes)), dma((4, planes)),
        ],
        compiler_params=pltpu.CompilerParams(
            collective_id=1, has_side_effects=True, vmem_limit_bytes=32 << 20
        ),
        name="total_moments",
    )(parts)


def splat_row(v, a):
    return jnp.broadcast_to(v[a : a + 1, :], (GROUP, BLOCK))


def splat_lane(v, j):
    return jnp.broadcast_to(v[:, j : j + 1], (GROUP, BLOCK))


def base_inverse(load, store):
    count = BLOCK // GROUP
    groups = [load(g) for g in range(count)]
    lane = lax.broadcasted_iota(jnp.int32, (GROUP, BLOCK), 1)
    sub = lax.broadcasted_iota(jnp.int32, (GROUP, BLOCK), 0)
    steps = range(GROUP)
    for p in range(count):
        j = GROUP * p
        v = groups[p]
        cols = [splat_lane(v, j + a) for a in steps]
        e = [[splat_row(cols[a], b) if b >= a else None for a in steps] for b in steps]
        low = [[None] * GROUP for _ in steps]
        rec = []
        for a in steps:
            rec.append(1.0 / e[a][a])
            for b in range(a + 1, GROUP):
                low[b][a] = e[b][a] * rec[a]
            for b in range(a + 1, GROUP):
                for c in range(a + 1, b + 1):
                    e[b][c] = e[b][c] - low[b][a] * e[c][a]
        panel = (lane >= j) & (lane < j + GROUP)
        rows = []
        for a in steps:
            r = jnp.where(panel, jnp.where(lane == j + a, 1.0, 0.0), splat_row(v, a))
            for b in range(a):
                r = r - low[a][b] * rows[b]
            rows.append(r)
        out = None
        for a in steps:
            r = rows[a] * lax.rsqrt(e[a][a])
            out = r if out is None else jnp.where(sub == a, r, out)
        store(p, jnp.where(lane < j + GROUP, out, 0.0))
        for g in range(p + 1, count):
            x = groups[g]
            w = []
            acc = jnp.where(panel, 0.0, x)
            for a in steps:
                t = splat_lane(x, j + a)
                for b in range(a):
                    t = t - low[a][b] * w[b]
                w.append(t)
                acc = acc - (t * rec[a]) * rows[a]
            groups[g] = acc


def factor_kernel(total_ref, out_ref, work, m_ref):
    width = work.shape[1]
    blocks = width // BLOCK
    pairs = block_pairs(width)
    at = len(pairs) * BLOCK
    tail = total_ref[at : at + GROUP, :]
    count = tail[blocks : blocks + 1, 0:1]
    center = jnp.concatenate([tail[k : k + 1, :] for k in range(blocks)], axis=1) / count
    first = lax.broadcasted_iota(jnp.int32, (GROUP, width), 0) == 0
    center8 = jnp.where(first, jnp.broadcast_to(center, (GROUP, width)), 0.0)
    eye = lax.broadcasted_iota(jnp.int32, (BLOCK, BLOCK), 0) == lax.broadcasted_iota(
        jnp.int32, (BLOCK, BLOCK), 1
    )
    for b, (i, k) in enumerate(pairs):
        outer = dot_of(
            center8[:, i * BLOCK : (i + 1) * BLOCK], center8[:, k * BLOCK : (k + 1) * BLOCK], ((0,), (0,))
        )
        block = total_ref[b * BLOCK : (b + 1) * BLOCK, :] / count - outer
        if i == k:
            block = block + jnp.where(eye, EPS_COV, 0.0)
        work[i * BLOCK : (i + 1) * BLOCK, k * BLOCK : (k + 1) * BLOCK] = block
        if i != k:
            work[k * BLOCK : (k + 1) * BLOCK, i * BLOCK : (i + 1) * BLOCK] = block.T
    row_block = lax.broadcasted_iota(jnp.int32, (width, BLOCK), 0) // BLOCK
    col_block = lax.broadcasted_iota(jnp.int32, (width, width), 1) // BLOCK
    strip_block = lax.broadcasted_iota(jnp.int32, (BLOCK, width), 1) // BLOCK
    strip_eye = jnp.where(
        lax.broadcasted_iota(jnp.int32, (BLOCK, width), 1) % BLOCK
        == lax.broadcasted_iota(jnp.int32, (BLOCK, width), 0),
        1.0,
        0.0,
    )

    def step(k, _):
        here = pl.multiple_of(k * BLOCK, BLOCK)

        def load(g):
            return work[pl.ds(pl.multiple_of(here + GROUP * g, GROUP), GROUP), pl.ds(here, BLOCK)]

        def store(g, val):
            m_ref[GROUP * g : GROUP * (g + 1), :] = val

        base_inverse(load, store)
        m = m_ref[...]
        col = jnp.where(row_block > k, work[:, pl.ds(here, BLOCK)], 0.0)
        left = dot_of(col, m, ((1,), (1,)))
        row = jnp.where(strip_block == k, strip_eye, work[pl.ds(here, BLOCK), :])
        across = dot_of(m, row, ((1,), (0,)))
        work[...] = jnp.where(col_block == k, 0.0, work[...]) - dot_of(left, across, ((1,), (0,)))
        work[pl.ds(here, BLOCK), :] = jnp.where(strip_block <= k, across, 0.0)
        return 0

    lax.fori_loop(0, blocks, step, 0)
    out_ref[:width, :] = work[...]
    out_ref[width:, :] = center8


def inverse_factor(total, width):
    return pl.pallas_call(
        factor_kernel,
        out_shape=jax.ShapeDtypeStruct((width + GROUP, width), jnp.float32),
        in_specs=[in_vmem()],
        out_specs=in_vmem(),
        scratch_shapes=[
            pltpu.VMEM((width, width), jnp.float32),
            pltpu.VMEM((BLOCK, BLOCK), jnp.float32),
        ],
        compiler_params=pltpu.CompilerParams(vmem_limit_bytes=32 << 20),
        name="inverse_factor",
    )(total)


def swap_kernel(own_ref, out_ref, send, recv):
    z, x = lax.axis_index(Z), lax.axis_index(X)
    core, y = lax.axis_index(CORE), lax.axis_index(Y)
    other = (z, x, 1 - core, y)
    barrier = pltpu.get_barrier_semaphore()
    pl.semaphore_signal(barrier, inc=1, device_id=other, device_id_type=MESH_IDS)
    pl.semaphore_wait(barrier, 1)
    copy = pltpu.make_async_remote_copy(
        src_ref=own_ref, dst_ref=out_ref, send_sem=send, recv_sem=recv,
        device_id=other, device_id_type=MESH_IDS,
    )
    copy.start()
    copy.wait()


def from_partner(own):
    return pl.pallas_call(
        swap_kernel,
        out_shape=jax.ShapeDtypeStruct(own.shape, own.dtype),
        in_specs=[in_vmem()],
        out_specs=in_vmem(),
        scratch_shapes=[pltpu.SemaphoreType.DMA, pltpu.SemaphoreType.DMA],
        compiler_params=pltpu.CompilerParams(
            collective_id=2, has_side_effects=True, vmem_limit_bytes=16 << 20
        ),
        name="from_partner",
    )(own)


def whiten_kernel(length, lengths_ref, emb_ref, own_ref, other_ref, out_ref, gap_ref):
    views, tokens, width = emb_ref.shape
    core = lax.axis_index(CORE)
    alive = alive_column(lengths_ref, tokens, length)
    for ref, v in ((own_ref, core), (other_ref, 1 - core)):
        centered = (emb_ref[v] - ref[width : width + 1, :]) * alive
        out_ref[v] = dot_of(centered, ref[:width, :], ((1,), (1,)))
    gap = out_ref[0] - out_ref[1]
    ones = jnp.ones((GROUP, width), jnp.float32)
    sums = dot_of(ones, gap * gap, ((1,), (1,))) / width
    for k in range(tokens // BLOCK):
        gap_ref[k : k + 1, :] = sums[0:1, k * BLOCK : (k + 1) * BLOCK]


def whitened_rows(lengths, embedded, own, other, length):
    views, tokens, width = embedded.shape
    whitened, gap = pl.pallas_call(
        lambda *refs: whiten_kernel(length, *refs),
        out_shape=(
            jax.ShapeDtypeStruct(embedded.shape, jnp.float32),
            jax.ShapeDtypeStruct((tokens // BLOCK, BLOCK), jnp.float32),
        ),
        in_specs=[in_smem()] + [in_vmem()] * 3,
        out_specs=(in_vmem(), in_vmem()),
        compiler_params=pltpu.CompilerParams(vmem_limit_bytes=32 << 20),
        name="whitened_rows",
    )(lengths, embedded, own, other)
    return whitened, gap.reshape(tokens)


class Sender:
    def __init__(self, send_sems, recv_sems):
        self.send_sems, self.recv_sems = send_sems, recv_sems
        self.started, self.used = [], 0

    def site(self):
        self.used += 1
        return self.used - 1

    def copy(self, site, src, dst, device):
        return pltpu.make_async_remote_copy(
            src_ref=src, dst_ref=dst,
            send_sem=self.send_sems.at[site], recv_sem=self.recv_sems.at[site],
            device_id=device, device_id_type=MESH_IDS,
        )

    def send(self, site, src, dst, device):
        made = self.copy(site, src, dst, device)
        made.start()
        self.started.append(made)

    def arrived(self, site, dst, device):
        self.copy(site, dst, dst, device).wait_recv()

    def finish(self):
        for made in self.started:
            made.wait_send()


class Ring:
    def __init__(self, sender, size, pos, device_at, slot_at, hops, own=None):
        self.sender, self.size, self.pos = sender, size, pos
        self.device_at, self.slot_at = device_at, slot_at
        self.hops = {1: hops[0], -1: hops[1]}
        self.own = own
        self.sites = {
            (sign, h): sender.site() for sign in (1, -1) for h in range(1, self.hops[sign] + 1)
        }

    def at(self, offset):
        return lax.rem(self.pos + offset + 2 * self.size, self.size)

    def pass_on(self, sign, h):
        source = self.at(-sign * (h - 1))
        slot = self.slot_at(source)
        src = self.own if h == 1 and self.own is not None else slot
        self.sender.send(self.sites[sign, h], src, slot, self.device_at(self.at(sign)))

    def launch(self):
        for sign in (1, -1):
            self.pass_on(sign, 1)

    def has(self, sign, h):
        return h <= self.hops[sign]

    def take(self, sign, h):
        slot = self.slot_at(self.at(-sign * h))
        self.sender.arrived(self.sites[sign, h], slot, self.device_at(self.at(-sign)))
        if h < self.hops[sign]:
            self.pass_on(sign, h + 1)
        return (sign * h) % self.size


class Place:
    def __init__(self, sizes):
        self.depth, self.across, self.down = sizes
        self.z, self.x = lax.axis_index(Z), lax.axis_index(X)
        self.core, self.y = lax.axis_index(CORE), lax.axis_index(Y)
        self.partner = (self.z, self.x, 1 - self.core, self.y)

    def z_at(self, s):
        return lax.rem(self.z - s + 2 * self.depth, self.depth)

    def x_at(self, t):
        return lax.rem(self.x - t + 2 * self.across, self.across)

    def y_at(self, s):
        return lax.rem(self.y + s + 2 * self.down, self.down)

    def along_z(self, zz):
        return (zz, self.x, self.core, self.y)

    def along_x(self, xx):
        return (self.z, xx, self.core, self.y)

    def along_y(self, yy):
        return (self.z, self.x, self.core, yy)

    def greet(self):
        peers = [self.along_z(self.z_at(s)) for s in (1, -1)]
        peers += [self.along_x(self.x_at(s)) for s in (1, -1)]
        peers += [self.along_y(self.y_at(s)) for s in range(1, self.down)]
        peers += [self.partner]
        barrier = pltpu.get_barrier_semaphore()
        for peer in peers:
            pl.semaphore_signal(barrier, inc=1, device_id=peer, device_id_type=MESH_IDS)
        pl.semaphore_wait(barrier, len(peers))


SITES = 64


def rows_of_slab(zz, xx, core, across):
    return pl.ds(pl.multiple_of(((zz * across + xx) * 2 + core) * GROUP, GROUP), GROUP)


def gather_kernel(
    sizes, xt_ref, raw_a, raw_b, xt_out, wa_out, wb_out, wa_ref, wb_ref,
    ring_send, ring_recv, pair_send, pair_recv, y_send, y_recv, local,
):
    here = Place(sizes)
    depth, across, down = sizes
    z, x, core, y = here.z, here.x, here.core, here.y
    wa_ref[...] = jnp.concatenate([raw_a[k] for k in range(raw_a.shape[0])], axis=1)
    wb_ref[...] = jnp.concatenate([raw_b[k] for k in range(raw_b.shape[0])], axis=1)
    here.greet()
    half = xt_ref.shape[0] // 2

    def slab(zz, xx, cc):
        return wb_out.at[:, rows_of_slab(zz, xx, cc, across), :]

    def own_part(yy):
        return wb_out.at[yy, rows_of_slab(z, x, core, across), :]

    own = [
        pltpu.make_async_copy(wb_ref, own_part(y), local.at[0]),
        pltpu.make_async_copy(wa_ref, wa_out.at[z, x, core], local.at[1]),
        pltpu.make_async_copy(xt_ref, xt_out.at[y], local.at[2]),
    ]
    for copy in own:
        copy.start()

    ys = Sender(y_send, y_recv)
    wb_sites = {s: ys.site() for s in range(1, down)}
    for s in range(1, down):
        ys.send(wb_sites[s], wb_ref, own_part(y), here.along_y(here.y_at(s)))

    def piece(yy, p):
        return xt_out.at[yy, p * half : (p + 1) * half, :]

    xt_sites = {(sign, p, h): ys.site() for sign in (1, -1) for p in (0, 1) for h in (1, 2)}
    for first in (0, 1):
        for sign in (1, -1):
            p = first if sign == 1 else 1 - first
            ys.send(
                xt_sites[sign, p, 1], xt_ref.at[p * half : (p + 1) * half, :], piece(y, p),
                here.along_y(here.y_at(sign)),
            )

    def first_pieces():
        for sign, p in ((1, 0), (-1, 1)):
            source = here.y_at(-sign)
            ys.arrived(xt_sites[sign, p, 1], piece(source, p), here.along_y(source))
            ys.send(xt_sites[sign, p, 2], piece(source, p), piece(source, p), here.along_y(here.y_at(sign)))

    def last_pieces():
        for sign, p in ((1, 1), (-1, 0)):
            source = here.y_at(-sign)
            ys.arrived(xt_sites[sign, p, 1], piece(source, p), here.along_y(source))
        for sign, p in ((1, 0), (-1, 1)):
            ys.arrived(xt_sites[sign, p, 2], piece(here.y_at(2), p), here.along_y(here.y_at(-sign)))

    def slabs_ready():
        for s in range(1, down):
            source = here.y_at(-s)
            ys.arrived(wb_sites[s], own_part(source), here.along_y(source))
        own[0].wait()

    pairs = Sender(pair_send, pair_recv)

    def to_partner(s, t):
        slot = wa_out.at[here.z_at(s), here.x_at(t), core]
        src = wa_ref if s == 0 and t == 0 else slot
        pairs.send(s * across + t, src, slot, here.partner)

    @pl.when(core == 0)
    def _():
        rings = Sender(ring_send, ring_recv)
        down_z = Ring(rings, depth, z, here.along_z, lambda zz: wa_out.at[zz, x, core], (4, 3), wa_ref)
        slabs_z = Ring(rings, depth, z, here.along_z, lambda zz: slab(zz, x, core), (3, 4))
        on_x = [
            Ring(
                rings, across, x, here.along_x,
                lambda xx, s=s: wa_out.at[here.z_at(s), xx, core],
                (2, 1) if s % 2 == 0 else (1, 2),
                wa_ref if s == 0 else None,
            )
            for s in range(depth)
        ]
        down_z.launch()
        on_x[0].launch()
        to_partner(0, 0)
        slabs_ready()
        slabs_z.launch()
        waiting = [0]
        for h in range(1, 5):
            arrived = []
            for sign in (1, -1):
                if down_z.has(sign, h):
                    s = down_z.take(sign, h)
                    on_x[s].launch()
                    to_partner(s, 0)
                    arrived.append(s)
            for sign in (1, -1):
                if slabs_z.has(sign, h):
                    slabs_z.take(sign, h)
            for s in waiting:
                for sign in (1, -1):
                    to_partner(s, on_x[s].take(sign, 1))
            waiting = arrived
            if h == 3:
                first_pieces()
        for s in waiting:
            for sign in (1, -1):
                to_partner(s, on_x[s].take(sign, 1))
        for s in [0, 1, 7, 2, 6, 3, 5, 4]:
            to_partner(s, on_x[s].take(1 if s % 2 == 0 else -1, 2))
        rings.finish()

    @pl.when(core == 1)
    def _():
        rings = Sender(ring_send, ring_recv)
        own_x = Ring(rings, across, x, here.along_x, lambda xx: wa_out.at[z, xx, core], (2, 1), wa_ref)
        slabs_x = Ring(rings, across, x, here.along_x, lambda xx: slab(z, xx, core), (1, 2))
        on_z = [
            Ring(
                rings, depth, z, here.along_z,
                lambda zz, t=t: wa_out.at[zz, here.x_at(t), core],
                (4, 3) if t % 2 == 0 else (3, 4),
                wa_ref if t == 0 else None,
            )
            for t in range(across)
        ]
        own_x.launch()
        on_z[0].launch()
        to_partner(0, 0)
        slabs_ready()
        slabs_x.launch()
        for sign, h in ((1, 1), (-1, 1), (1, 2)):
            t = own_x.take(sign, h)
            on_z[t].launch()
            to_partner(0, t)
        for sign, h in ((1, 1), (-1, 1), (-1, 2)):
            slabs_x.take(sign, h)
        for h in range(1, 5):
            for t in (0, 1, 3, 2):
                for sign in (1, -1):
                    if on_z[t].has(sign, h):
                        to_partner(on_z[t].take(sign, h), t)
            if h == 1:
                first_pieces()
        rings.finish()

    last_pieces()
    for s in range(depth):
        for t in range(across):
            slot = wa_out.at[here.z_at(s), here.x_at(t), 1 - core]
            made = pairs.copy(s * across + t, slot, slot, here.partner)
            made.wait_recv()
            made.wait_send()
    ys_wait = ys.started
    for made in ys_wait[: down - 1 + 4]:
        made.wait_send()
    for sign, p in ((1, 0), (-1, 1)):
        ys.copy(
            xt_sites[sign, p, 2], piece(here.y_at(-sign), p), piece(here.y_at(-sign), p),
            here.along_y(here.y_at(sign)),
        ).wait_send()
    own[1].wait()
    own[2].wait()


def gathered_inputs(xt, wa, wb, sizes):
    depth, across, down = sizes
    dma = pltpu.SemaphoreType.DMA
    anywhere = pl.BlockSpec(memory_space=pl.ANY)
    taps, rows_a, width = wa.shape
    rows_b = wb.shape[1]
    return pl.pallas_call(
        lambda *refs: gather_kernel(sizes, *refs),
        out_shape=(
            jax.ShapeDtypeStruct((down, *xt.shape), xt.dtype),
            jax.ShapeDtypeStruct((depth, across, 2, rows_a, taps * width), wa.dtype),
            jax.ShapeDtypeStruct((down, depth * across * 2 * rows_b, taps * width), wb.dtype),
        ),
        in_specs=[anywhere, in_vmem(), in_vmem()],
        out_specs=(in_vmem(), anywhere, anywhere),
        scratch_shapes=[
            pltpu.VMEM((rows_a, taps * width), wa.dtype),
            pltpu.VMEM((rows_b, taps * width), wb.dtype),
            dma((SITES,)), dma((SITES,)),
            dma((depth * across,)), dma((depth * across,)),
            dma((16,)), dma((16,)),
            dma((3,)),
        ],
        compiler_params=pltpu.CompilerParams(
            collective_id=3, has_side_effects=True, vmem_limit_bytes=16 << 20
        ),
        name="gathered_inputs",
    )(xt, wa, wb)


def gate(values):
    return 0.5 * values * (1.0 + jnp.tanh(0.7978845608 * (values + 0.044715 * values * values * values)))


PAD = 8
ROWS = 128
EDGE = 16


def conv_kernel(
    sizes, lengths_ref, xt_ref, wa_hbm, gain_ref, keep_ref, out_ref, wa_ref, n_ref, w_ref, stage, p_ref, cols, sems
):
    sequences, length, taps = sizes
    channels, tokens = xt_ref.shape
    chunks, chunk_rows, lanes = wa_ref.shape
    loads = 4
    each = chunks // loads
    arriving = [
        pltpu.make_async_copy(wa_hbm.at[pl.ds(i * each, each)], wa_ref.at[pl.ds(i * each, each)], sems.at[i])
        for i in range(loads)
    ]
    for copy in arriving:
        copy.start()
    eye = lax.broadcasted_iota(jnp.int32, (BLOCK, BLOCK), 0) == lax.broadcasted_iota(
        jnp.int32, (BLOCK, BLOCK), 1
    )
    squares = jnp.zeros((1, tokens), jnp.float32)
    for i in range(channels // BLOCK):
        part = xt_ref[i * BLOCK : (i + 1) * BLOCK, :].astype(jnp.float32)
        squares = squares + jnp.sum(part * part, axis=0, keepdims=True)
    scale = lax.rsqrt(squares / channels + EPS_NORM)
    for i in range(channels // BLOCK):
        part = xt_ref[i * BLOCK : (i + 1) * BLOCK, :].astype(jnp.float32)
        gain = jnp.sum(
            jnp.where(eye, jnp.broadcast_to(gain_ref[i : i + 1, :], (BLOCK, BLOCK)), 0.0), axis=1, keepdims=True
        )
        normed = (part * scale * gain).astype(jnp.bfloat16)
        n_ref[:, i * BLOCK : (i + 1) * BLOCK] = normed.T

    token = lax.broadcasted_iota(jnp.int32, (GROUP, tokens), 1)
    position = token % length
    limit = jnp.zeros((GROUP, tokens), jnp.int32)
    for s in range(sequences):
        limit = jnp.where(token // length == s, lengths_ref[s], limit)
    view = lax.broadcasted_iota(jnp.int32, (GROUP, tokens), 0)
    keep = jnp.where(view == 0, keep_ref[0:1, :], jnp.where(view == 1, keep_ref[1:2, :], 0))
    kept = jnp.where(position < limit, keep, 0).astype(jnp.float32)
    for k in range(taps):
        move = k - taps // 2
        rolled = kept if move == 0 else pltpu.roll(kept, (-move) % tokens, 1)
        inside = (position + move >= 0) & (position + move < length)
        cols[k] = jnp.where(inside, rolled, 0.0).T

    group = 4

    def relay(q, _):
        for i in range(group):
            stage[i * chunk_rows : (i + 1) * chunk_rows, :] = wa_ref[q * group + i].astype(jnp.float32)
        at = pl.multiple_of(q * group * chunk_rows, group * chunk_rows)
        w_ref[pl.ds(at, group * chunk_rows), :] = stage[...].astype(jnp.bfloat16)
        return 0

    for i in range(loads):
        arriving[i].wait()
        lax.fori_loop(i * each // group, (i + 1) * each // group, relay, 0)

    width = lanes // taps
    p_ref[0:PAD, :] = jnp.zeros((PAD, lanes), jnp.float32)
    p_ref[PAD + length :, :] = jnp.zeros((PAD, lanes), jnp.float32)

    def sequence(s, _):
        start = pl.multiple_of(s * length, length)
        for r in range(length // ROWS):
            p_ref[PAD + r * ROWS : PAD + (r + 1) * ROWS, :] = jnp.dot(
                n_ref[pl.ds(start + r * ROWS, ROWS), :], w_ref[...], preferred_element_type=jnp.float32
            )
        for r in range(length // ROWS):
            hidden = []
            for v in range(2):
                acc = None
                for k in range(taps):
                    first = PAD + r * ROWS + k - taps // 2
                    piece = p_ref[first : first + ROWS, k * width : (k + 1) * width]
                    piece = piece * cols[k, pl.ds(start + r * ROWS, ROWS), v : v + 1]
                    acc = piece if acc is None else acc + piece
                hidden.append(gate(acc))
            out_ref[pl.ds(start + r * ROWS, ROWS), :] = jnp.concatenate(hidden, axis=1).astype(jnp.bfloat16)
        return 0

    lax.fori_loop(0, sequences, sequence, 0)


def first_conv(lengths, xt, wa, gain, keep, taps):
    channels, tokens = xt.shape
    chunks, chunk_rows, lanes = wa.shape
    sequences = lengths.shape[0]
    length = tokens // sequences
    bf, f32 = jnp.bfloat16, jnp.float32
    return pl.pallas_call(
        lambda *refs: conv_kernel((sequences, length, taps), *refs),
        out_shape=jax.ShapeDtypeStruct((tokens, 2 * lanes // taps), bf),
        in_specs=[in_smem(), in_vmem(), pl.BlockSpec(memory_space=pl.ANY), in_vmem(), in_vmem()],
        out_specs=in_vmem(),
        scratch_shapes=[
            pltpu.VMEM(wa.shape, bf),
            pltpu.VMEM((tokens, channels), bf),
            pltpu.VMEM((channels, lanes), bf),
            pltpu.VMEM((4 * chunk_rows, lanes), f32),
            pltpu.VMEM((length + 2 * PAD, lanes), f32),
            pltpu.VMEM((taps, tokens, GROUP), f32),
            pltpu.SemaphoreType.DMA((4,)),
        ],
        compiler_params=pltpu.CompilerParams(vmem_limit_bytes=40 << 20),
        name="first_conv",
    )(lengths, xt, wa, gain, keep)


def spread_kernel(
    sizes, h_ref, wb_in, hx_out, wb_out, ring_send, ring_recv, pair_send, pair_recv, y_send, y_recv, local
):
    here = Place(sizes)
    depth, across, down = sizes
    z, x, core, y = here.z, here.x, here.core, here.y
    here.greet()
    rows = h_ref.shape[0] // down
    window = rows + EDGE

    def source_rows(yy):
        return pl.ds(pl.multiple_of(yy * rows - EDGE * lax.rem(yy, 2), EDGE), window)

    def target_rows(yy):
        return pl.ds(pl.multiple_of(EDGE - EDGE * lax.rem(yy, 2), EDGE), window)

    ys = Sender(y_send, y_recv)
    for s in (2, 1, 3):
        other = here.y_at(s)
        ys.send(s, h_ref.at[source_rows(other), :], hx_out.at[y, target_rows(other), :], here.along_y(other))
    own = pltpu.make_async_copy(h_ref.at[source_rows(y), :], hx_out.at[y, target_rows(y), :], local.at[0])
    own.start()

    def slab(zz, xx, cc):
        return wb_out.at[:, rows_of_slab(zz, xx, cc, across), :]

    pairs = Sender(pair_send, pair_recv)

    def to_partner(s, t):
        slot = slab(here.z_at(s), here.x_at(t), core)
        pairs.send(s * across + t, slot, slot, here.partner)

    @pl.when(core == 0)
    def _():
        rings = Sender(ring_send, ring_recv)
        on_x = [
            Ring(
                rings, across, x, here.along_x,
                lambda xx, s=s: slab(here.z_at(s), xx, core),
                (2, 1) if s % 2 == 0 else (1, 2),
            )
            for s in range(depth)
        ]
        for s in range(depth):
            on_x[s].launch()
        for s in range(depth):
            to_partner(s, 0)
        for s in range(depth):
            for sign in (1, -1):
                to_partner(s, on_x[s].take(sign, 1))
        for s in range(depth):
            to_partner(s, on_x[s].take(1 if s % 2 == 0 else -1, 2))
        rings.finish()

    @pl.when(core == 1)
    def _():
        rings = Sender(ring_send, ring_recv)
        on_z = [
            Ring(
                rings, depth, z, here.along_z,
                lambda zz, t=t: slab(zz, here.x_at(t), core),
                (4, 3) if t % 2 == 0 else (3, 4),
            )
            for t in range(across)
        ]
        for t in range(across):
            on_z[t].launch()
        for t in range(across):
            to_partner(0, t)
        for h in range(1, 5):
            for t in range(across):
                for sign in (1, -1):
                    if on_z[t].has(sign, h):
                        to_partner(on_z[t].take(sign, h), t)
        rings.finish()

    for s in range(depth):
        for t in range(across):
            slot = slab(here.z_at(s), here.x_at(t), 1 - core)
            made = pairs.copy(s * across + t, slot, slot, here.partner)
            made.wait_recv()
            made.wait_send()
    for s in (2, 1, 3):
        source = here.y_at(-s)
        ys.arrived(s, hx_out.at[source, target_rows(y), :], here.along_y(source))
    ys.finish()
    own.wait()


def spread_hidden(hidden, wb, sizes):
    depth, across, down = sizes
    tokens, lanes = hidden.shape
    dma = pltpu.SemaphoreType.DMA
    anywhere = pl.BlockSpec(memory_space=pl.ANY)
    return pl.pallas_call(
        lambda *refs: spread_kernel(sizes, *refs),
        out_shape=(
            jax.ShapeDtypeStruct((down, tokens // down + 2 * EDGE, lanes), hidden.dtype),
            jax.ShapeDtypeStruct(wb.shape, wb.dtype),
        ),
        in_specs=[in_vmem(), anywhere],
        out_specs=(in_vmem(), anywhere),
        input_output_aliases={1: 1},
        scratch_shapes=[
            dma((SITES,)), dma((SITES,)),
            dma((depth * across,)), dma((depth * across,)),
            dma((4,)), dma((4,)),
            dma((1,)),
        ],
        compiler_params=pltpu.CompilerParams(
            collective_id=4, has_side_effects=True, vmem_limit_bytes=16 << 20
        ),
        name="spread_hidden",
    )(hidden, wb)


def embed_kernel(taps, length, lengths_ref, hx_ref, wb_hbm, emb_ref, out_ref, wb_ref, wide, cols, sems):
    down, rows, lanes = hx_ref.shape
    arriving = [pltpu.make_async_copy(wb_hbm.at[c], wb_ref.at[c], sems.at[c]) for c in range(down)]
    for copy in arriving:
        copy.start()
    views, tokens, width = emb_ref.shape
    odd = lax.rem(lax.axis_index(Y), 2)
    row = lax.broadcasted_iota(jnp.int32, (rows, lanes), 0)
    inside = (row >= EDGE * (1 - odd)) & (row < rows - EDGE * odd)
    per = lanes // views
    for c in range(down):
        wide[...] = jnp.where(inside, hx_ref[c].astype(jnp.float32), 0.0)
        arriving[c].wait()
        for v in range(views):
            pieces = []
            for k in range(taps):
                first = EDGE + 2 * (k - taps // 2)
                pieces.append(wide[first : first + tokens, v * per : (v + 1) * per])
            cols[...] = jnp.concatenate(pieces, axis=1).astype(jnp.bfloat16)
            part = lax.dot_general(
                cols[...], wb_ref[c], (((1,), (1,)), ((), ())), preferred_element_type=jnp.float32
            )
            if c == 0:
                emb_ref[v] = part
            else:
                emb_ref[v] += part
    moments_into(emb_ref, alive_column(lengths_ref, tokens, length), out_ref)


def embedding(lengths, hx, wb, planes, taps, length):
    down, rows, lanes = hx.shape
    width = wb.shape[1]
    tokens = rows - 2 * EDGE
    parts = share_rows(width, planes) * planes
    return pl.pallas_call(
        lambda *refs: embed_kernel(taps, length, *refs),
        out_shape=(
            jax.ShapeDtypeStruct((2, tokens, width), jnp.float32),
            jax.ShapeDtypeStruct((2, parts, BLOCK), jnp.float32),
        ),
        in_specs=[in_smem(), in_vmem(), pl.BlockSpec(memory_space=pl.ANY)],
        out_specs=(in_vmem(), in_vmem()),
        scratch_shapes=[
            pltpu.VMEM(wb.shape, wb.dtype),
            pltpu.VMEM((rows, lanes), jnp.float32),
            pltpu.VMEM((tokens, wb.shape[2]), jnp.bfloat16),
            pltpu.SemaphoreType.DMA((down,)),
        ],
        compiler_params=pltpu.CompilerParams(vmem_limit_bytes=40 << 20),
        name="embedding",
    )(lengths, hx, wb)


def shards(monomers, keep_mask, lengths, norm_gain, weight_a, weight_b):
    tokens = monomers.shape[0]
    length = tokens // lengths.shape[0]
    taps = weight_a.shape[0]
    sizes = (lax.axis_size(Z), lax.axis_size(X), lax.axis_size(Y))
    xt, wa, wb = gathered_inputs(monomers.T, weight_a, weight_b.transpose(0, 2, 1), sizes)
    hidden = first_conv(
        lengths,
        xt.reshape(-1, tokens),
        wa.reshape(-1, *wa.shape[3:]),
        norm_gain.reshape(-1, BLOCK),
        keep_mask,
        taps,
    )
    hx, wb = spread_hidden(hidden, wb, sizes)
    embedded, parts = embedding(lengths, hx, wb, sizes[1] * sizes[2], taps, length)
    total = total_moments(parts, sizes)
    inverse = inverse_factor(total, embedded.shape[2])
    other = from_partner(inverse)
    return whitened_rows(lengths, embedded, inverse, other, length)


def solution(mesh):
    torus = Mesh(
        mesh.devices.reshape(8, 4, 2, mesh.shape["chan"]), ("batch_0", "batch_1", "batch_2", "chan")
    )
    in_specs = (
        P(BATCH, "chan"),
        P(None, BATCH),
        P(BATCH),
        P(),
        P(None, BATCH, "chan"),
        P(None, "chan", BATCH),
    )
    out_specs = (P(None, BATCH_CHAN, None), P(BATCH_CHAN))
    return jax.shard_map(
        shards, mesh=torus, in_specs=in_specs, out_specs=out_specs, check_vma=False
    )
```

```python
import jax
import jax.numpy as jnp
from jax import lax
from jax.experimental import pallas as pl
from jax.experimental.pallas import tpu as pltpu
from jax.sharding import Mesh
from jax.sharding import PartitionSpec as P

BATCH = ("batch_0", "batch_1", "batch_2")
BATCH_CHAN = ("batch_0", "batch_1", "batch_2", "chan")


EPS_NORM = 1e-05
EPS_COV = 0.0001
HI = lax.Precision.HIGHEST
MESH_IDS = pl.DeviceIdType.MESH
Z, X, CORE, Y = "batch_0", "batch_1", "batch_2", "chan"
AXES = (Z, X, CORE, Y)
BLOCK = 128
GROUP = 8


def dot_of(a, b, dims, precision=HI):
    return lax.dot_general(
        a, b, (dims, ((), ())), precision=precision, preferred_element_type=jnp.float32
    )


def in_vmem():
    return pl.BlockSpec(memory_space=pltpu.VMEM)


def block_pairs(width):
    return [(i, k) for i in range(width // BLOCK) for k in range(i + 1)]


def share_rows(width, planes):
    rows = len(block_pairs(width)) * BLOCK
    return -(-rows // (planes * GROUP)) * GROUP


def alive_column(lengths_ref, tokens, length):
    start = lax.axis_index(Y) * tokens
    limit = lengths_ref[start // length] - lax.rem(start, length)
    return jnp.where(lax.broadcasted_iota(jnp.int32, (tokens, 1), 0) < limit, 1.0, 0.0)


def in_smem():
    return pl.BlockSpec(memory_space=pltpu.SMEM)


def moments_into(emb_ref, alive, out_ref):
    views, tokens, width = emb_ref.shape
    pairs = block_pairs(width)
    at = len(pairs) * BLOCK
    half = BLOCK // 2
    for v in range(views):
        masked = emb_ref[v] * alive
        for i in range(width // BLOCK):
            wide = (i + 1) * BLOCK
            strip = dot_of(
                masked[:, i * BLOCK : wide], masked[:, :wide], ((0,), (0,))
            )
            for k in range(i + 1):
                b = pairs.index((i, k))
                out_ref[v, b * BLOCK : (b + 1) * BLOCK, :] = strip[:, k * BLOCK : (k + 1) * BLOCK]
        if out_ref.shape[1] > at:
            out_ref[v, at:, :] = jnp.zeros((out_ref.shape[1] - at, BLOCK), jnp.float32)
        sums = jnp.sum(masked, axis=0, keepdims=True)
        spare = [sums[:, k * half : (k + 1) * half] for k in range(width // half)]
        spare.append(jnp.broadcast_to(jnp.sum(alive, axis=0, keepdims=True), (1, half)))
        out_ref[v, 0 : len(spare), half:] = jnp.concatenate(spare, axis=0)


def total_kernel(sizes, parts, part_ref, out_ref, pair_in, mine, plane_in, share, line_in, total, *sems):
    depth, across, down = sizes
    planes = across * down
    rows = share.shape[0]
    z, x = lax.axis_index(Z), lax.axis_index(X)
    core, y = lax.axis_index(CORE), lax.axis_index(Y)
    me = x * down + y
    partner = 1 - core
    pair_send, pair_recv, plane_send, plane_recv, line_send, line_recv, back_send, back_recv = sems

    def in_plane(step):
        other = lax.rem(me + step, planes)
        return other, (z, other // down, core, lax.rem(other, down))

    def in_line(step):
        other = lax.rem(z + step, depth)
        return other, (other, x, core, y)

    barrier = pltpu.get_barrier_semaphore()
    pl.semaphore_signal(barrier, inc=1, device_id=(z, x, partner, y), device_id_type=MESH_IDS)
    for step in range(1, planes):
        pl.semaphore_signal(barrier, inc=1, device_id=in_plane(step)[1], device_id_type=MESH_IDS)
    for step in range(1, depth):
        pl.semaphore_signal(barrier, inc=1, device_id=in_line(step)[1], device_id_type=MESH_IDS)
    pl.semaphore_wait(barrier, 1 + planes - 1 + depth - 1)

    def sent(src, dst, send, recv, device):
        copy = pltpu.make_async_remote_copy(
            src_ref=src, dst_ref=dst, send_sem=send, recv_sem=recv,
            device_id=device, device_id_type=MESH_IDS,
        )
        copy.start()
        return copy

    starts = [sum(parts[:i]) for i in range(len(parts))]

    def within(i):
        return pl.ds(starts[i], parts[i])

    swaps = [
        sent(
            part_ref.at[partner, :, within(i)], pair_in.at[:, within(i)],
            pair_send.at[i], pair_recv.at[i], (z, x, partner, y),
        )
        for i in range(len(parts))
    ]

    def summed(buffer, own, count, i):
        acc = None
        for source in range(count):
            piece = buffer[lax.rem(own - source + count, count), within(i)]
            acc = piece if acc is None else acc + piece
        return acc

    spread, lines, back = {}, {}, {}
    for i in range(len(parts)):
        swaps[i].wait_recv()
        mine[:, within(i)] = part_ref[core, :, within(i)] + pair_in[:, within(i)]
        for step in range(1, planes):
            other, device = in_plane(step)
            spread[i, step] = sent(
                mine.at[other, within(i)], plane_in.at[step, within(i)],
                plane_send.at[i, step], plane_recv.at[i, step], device,
            )

    def to_line(i):
        for step in range(1, planes):
            spread[i, step].wait_recv()
        plane_in[0, within(i)] = mine[me, within(i)]
        share[within(i)] = summed(plane_in, me, planes, i)
        for step in range(1, depth):
            lines[i, step] = sent(
                share.at[within(i)], line_in.at[step, within(i)],
                line_send.at[i, step], line_recv.at[i, step], in_line(step)[1],
            )

    def to_plane(i):
        for step in range(1, depth):
            lines[i, step].wait_recv()
        line_in[0, within(i)] = share[within(i)]
        total[within(i)] = summed(line_in, z, depth, i)
        for step in range(1, planes):
            back[i, step] = sent(
                total.at[within(i)], out_ref.at[me, within(i)],
                back_send.at[i, step], back_recv.at[i, step], in_plane(step)[1],
            )
        out_ref[me, within(i)] = total[within(i)]

    lag = 2
    for i in range(len(parts) + lag):
        if i < len(parts):
            to_line(i)
        if i >= lag:
            to_plane(i - lag)
    for copy in back.values():
        copy.wait_recv()
    for copy in swaps:
        copy.wait_send()
    for group in (spread, lines, back):
        for copy in group.values():
            copy.wait_send()


def total_moments(parts, mesh_sizes):
    depth, across, down = mesh_sizes
    planes = across * down
    _, all_rows, lanes = parts.shape
    rows = all_rows // planes
    tiles = rows // GROUP
    pieces = tuple(GROUP * (tiles // 4 + (1 if i < tiles % 4 else 0)) for i in range(4))
    dma = pltpu.SemaphoreType.DMA
    vm = lambda *shape: pltpu.VMEM(shape, jnp.float32)
    return pl.pallas_call(
        lambda *refs: total_kernel(mesh_sizes, pieces, *refs),
        out_shape=jax.ShapeDtypeStruct((planes, rows, lanes), jnp.float32),
        in_specs=[in_vmem()],
        out_specs=in_vmem(),
        scratch_shapes=[
            vm(planes, rows, lanes),
            vm(planes, rows, lanes),
            vm(planes, rows, lanes),
            vm(rows, lanes),
            vm(depth, rows, lanes),
            vm(rows, lanes),
            dma((4,)), dma((4,)),
            dma((4, planes)), dma((4, planes)),
            dma((4, depth)), dma((4, depth)),
            dma((4, planes)), dma((4, planes)),
        ],
        compiler_params=pltpu.CompilerParams(
            collective_id=1, has_side_effects=True, vmem_limit_bytes=32 << 20
        ),
        name="total_moments",
    )(parts.reshape(2, planes, rows, lanes)).reshape(all_rows, lanes)


def splat_row(v, a):
    return jnp.broadcast_to(v[a : a + 1, :], (GROUP, BLOCK))


def splat_lane(v, j):
    return jnp.broadcast_to(v[:, j : j + 1], (GROUP, BLOCK))


def base_inverse(load, store):
    count = BLOCK // GROUP
    groups = [load(g) for g in range(count)]
    lane = lax.broadcasted_iota(jnp.int32, (GROUP, BLOCK), 1)
    sub = lax.broadcasted_iota(jnp.int32, (GROUP, BLOCK), 0)
    steps = range(GROUP)
    twos = range(GROUP // 2)
    for p in range(count):
        j = GROUP * p
        v = groups[p]
        cols = [splat_lane(v, j + a) for a in steps]
        e = [[splat_row(cols[a], b) if b >= a else None for a in steps] for b in steps]
        panel = (lane >= j) & (lane < j + GROUP)
        rows = [
            jnp.where(panel, jnp.where(lane == j + a, 1.0, 0.0), splat_row(v, a)) for a in steps
        ]
        f, inv = {}, []
        for t in twos:
            m, n = 2 * t, 2 * t + 1
            e00, e10, e11 = e[m][m], e[n][m], e[n][n]
            det = e00 * e11 - e10 * e10
            rd = 1.0 / det
            inv.append(rd)
            for b in range(n + 1, GROUP):
                f0 = (e11 * e[b][m] - e10 * e[b][n]) * rd
                f1 = (e00 * e[b][n] - e10 * e[b][m]) * rd
                f[b, t] = (f0, f1)
                for c in range(n + 1, b + 1):
                    e[b][c] = e[b][c] - (f0 * e[c][m] + f1 * e[c][n])
                rows[b] = rows[b] - (f0 * rows[m] + f1 * rows[n])
        out = None
        q = [None] * GROUP
        for t in reversed(twos):
            m, n = 2 * t, 2 * t + 1
            e00, e10, e11, rd = e[m][m], e[n][m], e[n][n], inv[t]
            q0 = (e11 * rows[m] - e10 * rows[n]) * rd
            q1 = (e00 * rows[n] - e10 * rows[m]) * rd
            for b in range(n + 1, GROUP):
                q0 = q0 - f[b, t][0] * q[b]
                q1 = q1 - f[b, t][1] * q[b]
            q[m], q[n] = q0, q1
        for g in range(p + 1, count):
            x = groups[g]
            terms = [splat_lane(x, j + a) * q[a] for a in steps]
            pairs = [terms[2 * t] + terms[2 * t + 1] for t in twos]
            groups[g] = jnp.where(panel, 0.0, x) - ((pairs[0] + pairs[1]) + (pairs[2] + pairs[3]))
        for t in twos:
            m, n = 2 * t, 2 * t + 1
            e00, e10, e11 = e[m][m], e[n][m], e[n][n]
            ratio = e10 / e00
            first = rows[m] * lax.rsqrt(e00)
            second = (rows[n] - ratio * rows[m]) * lax.rsqrt(e11 - ratio * e10)
            out = first if out is None else jnp.where(sub == m, first, out)
            out = jnp.where(sub == n, second, out)
        store(p, jnp.where(lane < j + GROUP, out, 0.0))


def factor_kernel(total_ref, out_ref, work, m_ref):
    width = work.shape[1]
    blocks = width // BLOCK
    pairs = block_pairs(width)
    half = BLOCK // 2
    spare = total_ref[0 : 2 * GROUP, half:]
    last = width // half
    count = spare[last : last + 1, 0:1]
    center = jnp.concatenate([spare[k : k + 1, :] for k in range(last)], axis=1) / count
    first = lax.broadcasted_iota(jnp.int32, (GROUP, width), 0) == 0
    center8 = jnp.where(first, jnp.broadcast_to(center, (GROUP, width)), 0.0)
    eye = lax.broadcasted_iota(jnp.int32, (BLOCK, BLOCK), 0) == lax.broadcasted_iota(
        jnp.int32, (BLOCK, BLOCK), 1
    )
    lower = lax.broadcasted_iota(jnp.int32, (BLOCK, BLOCK), 0) >= lax.broadcasted_iota(
        jnp.int32, (BLOCK, BLOCK), 1
    )
    for b, (i, k) in enumerate(pairs):
        outer = dot_of(
            center8[:, i * BLOCK : (i + 1) * BLOCK], center8[:, k * BLOCK : (k + 1) * BLOCK], ((0,), (0,))
        )
        raw = total_ref[b * BLOCK : (b + 1) * BLOCK, :]
        if b == 0:
            raw = jnp.where(lower, raw, raw.T)
        block = raw / count - outer
        if i == k:
            block = block + jnp.where(eye, EPS_COV, 0.0)
        work[i * BLOCK : (i + 1) * BLOCK, k * BLOCK : (k + 1) * BLOCK] = block
        if i != k:
            work[k * BLOCK : (k + 1) * BLOCK, i * BLOCK : (i + 1) * BLOCK] = block.T
    strip_block = lax.broadcasted_iota(jnp.int32, (BLOCK, width), 1) // BLOCK
    strip_eye = jnp.where(
        lax.broadcasted_iota(jnp.int32, (BLOCK, width), 1) % BLOCK
        == lax.broadcasted_iota(jnp.int32, (BLOCK, width), 0),
        1.0,
        0.0,
    )

    def step(k, _):
        here = pl.multiple_of(k * BLOCK, BLOCK)

        def load(g):
            return work[pl.ds(pl.multiple_of(here + GROUP * g, GROUP), GROUP), pl.ds(here, BLOCK)]

        def store(g, val):
            m_ref[GROUP * g : GROUP * (g + 1), :] = val

        base_inverse(load, store)
        m = m_ref[...]
        row = jnp.where(strip_block == k, strip_eye, work[pl.ds(here, BLOCK), :])
        across = dot_of(m, row, ((1,), (0,)))
        for done in range(blocks - 1):

            @pl.when(k == done)
            def _():
                first = (done + 1) * BLOCK
                col_block = lax.broadcasted_iota(jnp.int32, (width - first, width), 1) // BLOCK
                left = dot_of(work[first:, done * BLOCK : first], m, ((1,), (1,)))
                kept = jnp.where(col_block == done, 0.0, work[first:, :])
                work[first:, :] = kept - dot_of(left, across, ((1,), (0,)))

        work[pl.ds(here, BLOCK), :] = jnp.where(strip_block <= k, across, 0.0)
        return 0

    lax.fori_loop(0, blocks, step, 0)
    out_ref[:width, :] = work[...]
    out_ref[width:, :] = center8


def inverse_factor(total, width):
    return pl.pallas_call(
        factor_kernel,
        out_shape=jax.ShapeDtypeStruct((width + GROUP, width), jnp.float32),
        in_specs=[in_vmem()],
        out_specs=in_vmem(),
        scratch_shapes=[
            pltpu.VMEM((width, width), jnp.float32),
            pltpu.VMEM((BLOCK, BLOCK), jnp.float32),
        ],
        compiler_params=pltpu.CompilerParams(vmem_limit_bytes=32 << 20),
        name="inverse_factor",
    )(total)


def swap_kernel(own_ref, out_ref, send, recv):
    z, x = lax.axis_index(Z), lax.axis_index(X)
    core, y = lax.axis_index(CORE), lax.axis_index(Y)
    other = (z, x, 1 - core, y)
    barrier = pltpu.get_barrier_semaphore()
    pl.semaphore_signal(barrier, inc=1, device_id=other, device_id_type=MESH_IDS)
    pl.semaphore_wait(barrier, 1)
    copy = pltpu.make_async_remote_copy(
        src_ref=own_ref, dst_ref=out_ref, send_sem=send, recv_sem=recv,
        device_id=other, device_id_type=MESH_IDS,
    )
    copy.start()
    copy.wait()


def from_partner(own):
    return pl.pallas_call(
        swap_kernel,
        out_shape=jax.ShapeDtypeStruct(own.shape, own.dtype),
        in_specs=[in_vmem()],
        out_specs=in_vmem(),
        scratch_shapes=[pltpu.SemaphoreType.DMA, pltpu.SemaphoreType.DMA],
        compiler_params=pltpu.CompilerParams(
            collective_id=2, has_side_effects=True, vmem_limit_bytes=16 << 20
        ),
        name="from_partner",
    )(own)


def whiten_kernel(length, lengths_ref, emb_ref, own_ref, other_ref, out_ref, gap_ref):
    views, tokens, width = emb_ref.shape
    core = lax.axis_index(CORE)
    alive = alive_column(lengths_ref, tokens, length)
    for ref, v in ((own_ref, core), (other_ref, 1 - core)):
        centered = (emb_ref[v] - ref[width : width + 1, :]) * alive
        part = 2 * BLOCK
        for first in range(0, width, part):
            last = first + part
            out_ref[v, :, first:last] = dot_of(centered[:, :last], ref[first:last, :last], ((1,), (1,)))
    gap = out_ref[0] - out_ref[1]
    ones = jnp.ones((GROUP, width), jnp.float32)
    sums = dot_of(ones, gap * gap, ((1,), (1,))) / width
    for k in range(tokens // BLOCK):
        gap_ref[k : k + 1, :] = sums[0:1, k * BLOCK : (k + 1) * BLOCK]


def whitened_rows(lengths, embedded, own, other, length):
    views, tokens, width = embedded.shape
    whitened, gap = pl.pallas_call(
        lambda *refs: whiten_kernel(length, *refs),
        out_shape=(
            jax.ShapeDtypeStruct(embedded.shape, jnp.float32),
            jax.ShapeDtypeStruct((tokens // BLOCK, BLOCK), jnp.float32),
        ),
        in_specs=[in_smem()] + [in_vmem()] * 3,
        out_specs=(in_vmem(), in_vmem()),
        compiler_params=pltpu.CompilerParams(vmem_limit_bytes=32 << 20),
        name="whitened_rows",
    )(lengths, embedded, own, other)
    return whitened, gap.reshape(tokens)


class Sender:
    def __init__(self, send_sems, recv_sems):
        self.send_sems, self.recv_sems = send_sems, recv_sems
        self.started, self.used = [], 0

    def site(self):
        self.used += 1
        return self.used - 1

    def copy(self, site, src, dst, device):
        return pltpu.make_async_remote_copy(
            src_ref=src, dst_ref=dst,
            send_sem=self.send_sems.at[site], recv_sem=self.recv_sems.at[site],
            device_id=device, device_id_type=MESH_IDS,
        )

    def send(self, site, src, dst, device):
        made = self.copy(site, src, dst, device)
        made.start()
        self.started.append(made)

    def arrived(self, site, dst, device):
        self.copy(site, dst, dst, device).wait_recv()

    def finish(self):
        for made in self.started:
            made.wait_send()


class Ring:
    def __init__(self, sender, size, pos, device_at, slot_at, hops, own=None):
        self.sender, self.size, self.pos = sender, size, pos
        self.device_at, self.slot_at = device_at, slot_at
        self.hops = {1: hops[0], -1: hops[1]}
        self.own = own
        self.sites = {
            (sign, h): sender.site() for sign in (1, -1) for h in range(1, self.hops[sign] + 1)
        }

    def at(self, offset):
        return lax.rem(self.pos + offset + 2 * self.size, self.size)

    def pass_on(self, sign, h):
        source = self.at(-sign * (h - 1))
        slot = self.slot_at(source)
        src = self.own if h == 1 and self.own is not None else slot
        self.sender.send(self.sites[sign, h], src, slot, self.device_at(self.at(sign)))

    def launch(self):
        for sign in (1, -1):
            self.pass_on(sign, 1)

    def has(self, sign, h):
        return h <= self.hops[sign]

    def take(self, sign, h):
        slot = self.slot_at(self.at(-sign * h))
        self.sender.arrived(self.sites[sign, h], slot, self.device_at(self.at(-sign)))
        if h < self.hops[sign]:
            self.pass_on(sign, h + 1)
        return (sign * h) % self.size


class Place:
    def __init__(self, sizes):
        self.depth, self.across, self.down = sizes
        self.z, self.x = lax.axis_index(Z), lax.axis_index(X)
        self.core, self.y = lax.axis_index(CORE), lax.axis_index(Y)
        self.partner = (self.z, self.x, 1 - self.core, self.y)

    def z_at(self, s):
        return lax.rem(self.z - s + 2 * self.depth, self.depth)

    def x_at(self, t):
        return lax.rem(self.x - t + 2 * self.across, self.across)

    def y_at(self, s):
        return lax.rem(self.y + s + 2 * self.down, self.down)

    def along_z(self, zz):
        return (zz, self.x, self.core, self.y)

    def along_x(self, xx):
        return (self.z, xx, self.core, self.y)

    def along_y(self, yy):
        return (self.z, self.x, self.core, yy)

    def greet(self):
        self.greeted(self.greeting())

    def greeting(self):
        peers = [self.along_z(self.z_at(s)) for s in (1, -1)]
        peers += [self.along_x(self.x_at(s)) for s in (1, -1)]
        peers += [self.along_y(self.y_at(s)) for s in range(1, self.down)]
        peers += [self.partner]
        barrier = pltpu.get_barrier_semaphore()
        for peer in peers:
            pl.semaphore_signal(barrier, inc=1, device_id=peer, device_id_type=MESH_IDS)
        return len(peers)

    def greeted(self, count):
        pl.semaphore_wait(pltpu.get_barrier_semaphore(), count)


SITES = 64


def rows_of_slab(zz, xx, core, across):
    return pl.ds(pl.multiple_of(((zz * across + xx) * 2 + core) * GROUP, GROUP), GROUP)


def gather_kernel(
    sizes, xt_ref, hbm_a, hbm_b, xt_out, wa_out, wb_out, raw_a, raw_b, wa_ref, wb_ref,
    ring_send, ring_recv, pair_send, pair_recv, y_send, y_recv, local,
):
    here = Place(sizes)
    depth, across, down = sizes
    z, x, core, y = here.z, here.x, here.core, here.y
    greeted = here.greeting()
    load_a = pltpu.make_async_copy(hbm_a, raw_a, local.at[3])
    load_b = pltpu.make_async_copy(hbm_b, raw_b, local.at[4])
    load_a.start()
    load_b.start()
    load_a.wait()
    load_b.wait()
    wa_ref[...] = jnp.concatenate([raw_a[k] for k in range(raw_a.shape[0])], axis=1)
    wb_ref[...] = jnp.concatenate([raw_b[k] for k in range(raw_b.shape[0])], axis=1)
    here.greeted(greeted)
    half = xt_ref.shape[0] // 2

    def slab(zz, xx, cc):
        return wb_out.at[:, rows_of_slab(zz, xx, cc, across), :]

    def own_part(yy):
        return wb_out.at[yy, rows_of_slab(z, x, core, across), :]

    own = [
        pltpu.make_async_copy(wb_ref, own_part(y), local.at[0]),
        pltpu.make_async_copy(wa_ref, wa_out.at[z, x, core], local.at[1]),
        pltpu.make_async_copy(xt_ref, xt_out.at[y], local.at[2]),
    ]
    for copy in own:
        copy.start()

    ys = Sender(y_send, y_recv)
    wb_sites = {s: ys.site() for s in range(1, down)}
    for s in range(1, down):
        ys.send(wb_sites[s], wb_ref, own_part(y), here.along_y(here.y_at(s)))

    def piece(yy, p):
        return xt_out.at[yy, p * half : (p + 1) * half, :]

    xt_sites = {(sign, p, h): ys.site() for sign in (1, -1) for p in (0, 1) for h in (1, 2)}
    for first in (0, 1):
        for sign in (1, -1):
            p = first if sign == 1 else 1 - first
            ys.send(
                xt_sites[sign, p, 1], xt_ref.at[p * half : (p + 1) * half, :], piece(y, p),
                here.along_y(here.y_at(sign)),
            )

    def first_pieces():
        for sign, p in ((1, 0), (-1, 1)):
            source = here.y_at(-sign)
            ys.arrived(xt_sites[sign, p, 1], piece(source, p), here.along_y(source))
            ys.send(xt_sites[sign, p, 2], piece(source, p), piece(source, p), here.along_y(here.y_at(sign)))

    def last_pieces():
        for sign, p in ((1, 1), (-1, 0)):
            source = here.y_at(-sign)
            ys.arrived(xt_sites[sign, p, 1], piece(source, p), here.along_y(source))
        for sign, p in ((1, 0), (-1, 1)):
            ys.arrived(xt_sites[sign, p, 2], piece(here.y_at(2), p), here.along_y(here.y_at(-sign)))

    def slabs_ready():
        for s in range(1, down):
            source = here.y_at(-s)
            ys.arrived(wb_sites[s], own_part(source), here.along_y(source))
        own[0].wait()

    pairs = Sender(pair_send, pair_recv)

    def to_partner(s, t):
        slot = wa_out.at[here.z_at(s), here.x_at(t), core]
        src = wa_ref if s == 0 and t == 0 else slot
        pairs.send(s * across + t, src, slot, here.partner)

    @pl.when(core == 0)
    def _():
        rings = Sender(ring_send, ring_recv)
        down_z = Ring(rings, depth, z, here.along_z, lambda zz: wa_out.at[zz, x, core], (4, 3), wa_ref)
        slabs_z = Ring(rings, depth, z, here.along_z, lambda zz: slab(zz, x, core), (3, 4))
        on_x = [
            Ring(
                rings, across, x, here.along_x,
                lambda xx, s=s: wa_out.at[here.z_at(s), xx, core],
                (2, 1) if s % 2 == 0 else (1, 2),
                wa_ref if s == 0 else None,
            )
            for s in range(depth)
        ]
        down_z.launch()
        on_x[0].launch()
        to_partner(0, 0)
        slabs_ready()
        slabs_z.launch()
        waiting = [0]
        for h in range(1, 5):
            arrived = []
            for sign in (1, -1):
                if down_z.has(sign, h):
                    s = down_z.take(sign, h)
                    on_x[s].launch()
                    to_partner(s, 0)
                    arrived.append(s)
            for sign in (1, -1):
                if slabs_z.has(sign, h):
                    slabs_z.take(sign, h)
            for s in waiting:
                for sign in (1, -1):
                    to_partner(s, on_x[s].take(sign, 1))
            waiting = arrived
            if h == 3:
                first_pieces()
        for s in waiting:
            for sign in (1, -1):
                to_partner(s, on_x[s].take(sign, 1))
        for s in [0, 1, 7, 2, 6, 3, 5, 4]:
            to_partner(s, on_x[s].take(1 if s % 2 == 0 else -1, 2))
        rings.finish()

    @pl.when(core == 1)
    def _():
        rings = Sender(ring_send, ring_recv)
        own_x = Ring(rings, across, x, here.along_x, lambda xx: wa_out.at[z, xx, core], (2, 1), wa_ref)
        slabs_x = Ring(rings, across, x, here.along_x, lambda xx: slab(z, xx, core), (1, 2))
        on_z = [
            Ring(
                rings, depth, z, here.along_z,
                lambda zz, t=t: wa_out.at[zz, here.x_at(t), core],
                (4, 3) if t % 2 == 0 else (3, 4),
                wa_ref if t == 0 else None,
            )
            for t in range(across)
        ]
        own_x.launch()
        on_z[0].launch()
        to_partner(0, 0)
        slabs_ready()
        slabs_x.launch()
        for sign, h in ((1, 1), (-1, 1), (1, 2)):
            t = own_x.take(sign, h)
            on_z[t].launch()
            to_partner(0, t)
        for sign, h in ((1, 1), (-1, 1), (-1, 2)):
            slabs_x.take(sign, h)
        for h in range(1, 5):
            for t in (0, 1, 3, 2):
                for sign in (1, -1):
                    if on_z[t].has(sign, h):
                        to_partner(on_z[t].take(sign, h), t)
            if h == 1:
                first_pieces()
        rings.finish()

    last_pieces()
    for s in range(depth):
        for t in range(across):
            slot = wa_out.at[here.z_at(s), here.x_at(t), 1 - core]
            made = pairs.copy(s * across + t, slot, slot, here.partner)
            made.wait_recv()
            made.wait_send()
    ys_wait = ys.started
    for made in ys_wait[: down - 1 + 4]:
        made.wait_send()
    for sign, p in ((1, 0), (-1, 1)):
        ys.copy(
            xt_sites[sign, p, 2], piece(here.y_at(-sign), p), piece(here.y_at(-sign), p),
            here.along_y(here.y_at(sign)),
        ).wait_send()
    own[1].wait()
    own[2].wait()


def gathered_inputs(xt, wa, wb, sizes):
    depth, across, down = sizes
    dma = pltpu.SemaphoreType.DMA
    anywhere = pl.BlockSpec(memory_space=pl.ANY)
    taps, rows_a, width = wa.shape
    rows_b = wb.shape[1]
    return pl.pallas_call(
        lambda *refs: gather_kernel(sizes, *refs),
        out_shape=(
            jax.ShapeDtypeStruct((down, *xt.shape), xt.dtype),
            jax.ShapeDtypeStruct((depth, across, 2, rows_a, taps * width), wa.dtype),
            jax.ShapeDtypeStruct((down, depth * across * 2 * rows_b, taps * width), wb.dtype),
        ),
        in_specs=[anywhere] * 3,
        out_specs=(in_vmem(), anywhere, anywhere),
        scratch_shapes=[
            pltpu.VMEM(wa.shape, wa.dtype),
            pltpu.VMEM(wb.shape, wb.dtype),
            pltpu.VMEM((rows_a, taps * width), wa.dtype),
            pltpu.VMEM((rows_b, taps * width), wb.dtype),
            dma((SITES,)), dma((SITES,)),
            dma((depth * across,)), dma((depth * across,)),
            dma((16,)), dma((16,)),
            dma((5,)),
        ],
        compiler_params=pltpu.CompilerParams(
            collective_id=3, has_side_effects=True, vmem_limit_bytes=16 << 20
        ),
        name="gathered_inputs",
    )(xt, wa, wb)


def gate(values):
    return 0.5 * values * (1.0 + jnp.tanh(0.7978845608 * (values + 0.044715 * values * values * values)))


PAD = 8
ROWS = 128
EDGE = 16


def conv_kernel(
    sizes, lengths_ref, xt_ref, wa_hbm, gain_hbm, keep_hbm, out_ref,
    wa_ref, gain_ref, keep_ref, n_ref, w_ref, stage, p_ref, cols, sems,
):
    sequences, length, taps = sizes
    channels, tokens = xt_ref.shape
    chunks, chunk_rows, lanes = wa_ref.shape
    loads = 4
    each = chunks // loads
    arriving = [
        pltpu.make_async_copy(wa_hbm.at[pl.ds(i * each, each)], wa_ref.at[pl.ds(i * each, each)], sems.at[i])
        for i in range(loads)
    ]
    small = [
        pltpu.make_async_copy(gain_hbm, gain_ref, sems.at[loads]),
        pltpu.make_async_copy(keep_hbm, keep_ref, sems.at[loads + 1]),
    ]
    for copy in small + arriving:
        copy.start()
    eye = lax.broadcasted_iota(jnp.int32, (BLOCK, BLOCK), 0) == lax.broadcasted_iota(
        jnp.int32, (BLOCK, BLOCK), 1
    )
    squares = jnp.zeros((1, tokens), jnp.float32)
    for i in range(channels // BLOCK):
        part = xt_ref[i * BLOCK : (i + 1) * BLOCK, :].astype(jnp.float32)
        squares = squares + jnp.sum(part * part, axis=0, keepdims=True)
    scale = lax.rsqrt(squares / channels + EPS_NORM)
    for copy in small:
        copy.wait()
    for i in range(channels // BLOCK):
        part = xt_ref[i * BLOCK : (i + 1) * BLOCK, :].astype(jnp.float32)
        gain = jnp.sum(
            jnp.where(eye, jnp.broadcast_to(gain_ref[i : i + 1, :], (BLOCK, BLOCK)), 0.0), axis=1, keepdims=True
        )
        normed = (part * scale * gain).astype(jnp.bfloat16)
        n_ref[:, i * BLOCK : (i + 1) * BLOCK] = normed.T

    token = lax.broadcasted_iota(jnp.int32, (GROUP, tokens), 1)
    position = token % length
    limit = jnp.zeros((GROUP, tokens), jnp.int32)
    for s in range(sequences):
        limit = jnp.where(token // length == s, lengths_ref[s], limit)
    view = lax.broadcasted_iota(jnp.int32, (GROUP, tokens), 0)
    keep = jnp.where(view == 0, keep_ref[0:1, :], jnp.where(view == 1, keep_ref[1:2, :], 0))
    kept = jnp.where(position < limit, keep, 0).astype(jnp.float32)
    for k in range(taps):
        move = k - taps // 2
        rolled = kept if move == 0 else pltpu.roll(kept, (-move) % tokens, 1)
        inside = (position + move >= 0) & (position + move < length)
        cols[k] = jnp.where(inside, rolled, 0.0).T

    group = 4

    def relay(q, _):
        for i in range(group):
            stage[i * chunk_rows : (i + 1) * chunk_rows, :] = wa_ref[q * group + i].astype(jnp.float32)
        at = pl.multiple_of(q * group * chunk_rows, group * chunk_rows)
        w_ref[pl.ds(at, group * chunk_rows), :] = stage[...].astype(jnp.bfloat16)
        return 0

    for i in range(loads):
        arriving[i].wait()
        lax.fori_loop(i * each // group, (i + 1) * each // group, relay, 0)

    width = lanes // taps
    p_ref[0:PAD, :] = jnp.zeros((PAD, lanes), jnp.float32)
    p_ref[PAD + length :, :] = jnp.zeros((PAD, lanes), jnp.float32)

    def sequence(s, _):
        start = pl.multiple_of(s * length, length)
        for r in range(length // ROWS):
            p_ref[PAD + r * ROWS : PAD + (r + 1) * ROWS, :] = jnp.dot(
                n_ref[pl.ds(start + r * ROWS, ROWS), :], w_ref[...], preferred_element_type=jnp.float32
            )
        for r in range(length // ROWS):
            hidden = []
            for v in range(2):
                acc = None
                for k in range(taps):
                    first = PAD + r * ROWS + k - taps // 2
                    piece = p_ref[first : first + ROWS, k * width : (k + 1) * width]
                    piece = piece * cols[k, pl.ds(start + r * ROWS, ROWS), v : v + 1]
                    acc = piece if acc is None else acc + piece
                hidden.append(gate(acc))
            out_ref[pl.ds(start + r * ROWS, ROWS), :] = jnp.concatenate(hidden, axis=1).astype(jnp.bfloat16)
        return 0

    lax.fori_loop(0, sequences, sequence, 0)


def first_conv(lengths, xt, wa, gain, keep, taps):
    channels, tokens = xt.shape
    chunks, chunk_rows, lanes = wa.shape
    sequences = lengths.shape[0]
    length = tokens // sequences
    bf, f32 = jnp.bfloat16, jnp.float32
    return pl.pallas_call(
        lambda *refs: conv_kernel((sequences, length, taps), *refs),
        out_shape=jax.ShapeDtypeStruct((tokens, 2 * lanes // taps), bf),
        in_specs=[in_smem(), in_vmem()] + [pl.BlockSpec(memory_space=pl.ANY)] * 3,
        out_specs=in_vmem(),
        scratch_shapes=[
            pltpu.VMEM(wa.shape, bf),
            pltpu.VMEM(gain.shape, f32),
            pltpu.VMEM(keep.shape, keep.dtype),
            pltpu.VMEM((tokens, channels), bf),
            pltpu.VMEM((channels, lanes), bf),
            pltpu.VMEM((4 * chunk_rows, lanes), f32),
            pltpu.VMEM((length + 2 * PAD, lanes), f32),
            pltpu.VMEM((taps, tokens, GROUP), f32),
            pltpu.SemaphoreType.DMA((6,)),
        ],
        compiler_params=pltpu.CompilerParams(vmem_limit_bytes=40 << 20),
        name="first_conv",
    )(lengths, xt, wa, gain, keep)


def spread_kernel(
    sizes, h_ref, wb_in, hx_out, wb_out, ring_send, ring_recv, pair_send, pair_recv, y_send, y_recv, local
):
    here = Place(sizes)
    depth, across, down = sizes
    z, x, core, y = here.z, here.x, here.core, here.y
    here.greet()
    rows = h_ref.shape[0] // down
    window = rows + EDGE

    def source_rows(yy):
        return pl.ds(pl.multiple_of(yy * rows - EDGE * lax.rem(yy, 2), EDGE), window)

    def target_rows(yy):
        return pl.ds(pl.multiple_of(EDGE - EDGE * lax.rem(yy, 2), EDGE), window)

    ys = Sender(y_send, y_recv)
    for s in (2, 1, 3):
        other = here.y_at(s)
        ys.send(s, h_ref.at[source_rows(other), :], hx_out.at[y, target_rows(other), :], here.along_y(other))
    own = pltpu.make_async_copy(h_ref.at[source_rows(y), :], hx_out.at[y, target_rows(y), :], local.at[0])
    own.start()

    def slab(zz, xx, cc):
        return wb_out.at[:, rows_of_slab(zz, xx, cc, across), :]

    pairs = Sender(pair_send, pair_recv)

    def to_partner(s, t):
        slot = slab(here.z_at(s), here.x_at(t), core)
        pairs.send(s * across + t, slot, slot, here.partner)

    @pl.when(core == 0)
    def _():
        rings = Sender(ring_send, ring_recv)
        on_x = [
            Ring(
                rings, across, x, here.along_x,
                lambda xx, s=s: slab(here.z_at(s), xx, core),
                (2, 1) if s % 2 == 0 else (1, 2),
            )
            for s in range(depth)
        ]
        for s in range(depth):
            on_x[s].launch()
        for s in range(depth):
            to_partner(s, 0)
        for s in range(depth):
            for sign in (1, -1):
                to_partner(s, on_x[s].take(sign, 1))
        for s in range(depth):
            to_partner(s, on_x[s].take(1 if s % 2 == 0 else -1, 2))
        rings.finish()

    @pl.when(core == 1)
    def _():
        rings = Sender(ring_send, ring_recv)
        on_z = [
            Ring(
                rings, depth, z, here.along_z,
                lambda zz, t=t: slab(zz, here.x_at(t), core),
                (4, 3) if t % 2 == 0 else (3, 4),
            )
            for t in range(across)
        ]
        for t in range(across):
            on_z[t].launch()
        for t in range(across):
            to_partner(0, t)
        for h in range(1, 5):
            for t in range(across):
                for sign in (1, -1):
                    if on_z[t].has(sign, h):
                        to_partner(on_z[t].take(sign, h), t)
        rings.finish()

    for s in range(depth):
        for t in range(across):
            slot = slab(here.z_at(s), here.x_at(t), 1 - core)
            made = pairs.copy(s * across + t, slot, slot, here.partner)
            made.wait_recv()
            made.wait_send()
    for s in (2, 1, 3):
        source = here.y_at(-s)
        ys.arrived(s, hx_out.at[source, target_rows(y), :], here.along_y(source))
    ys.finish()
    own.wait()


def spread_hidden(hidden, wb, sizes):
    depth, across, down = sizes
    tokens, lanes = hidden.shape
    dma = pltpu.SemaphoreType.DMA
    anywhere = pl.BlockSpec(memory_space=pl.ANY)
    return pl.pallas_call(
        lambda *refs: spread_kernel(sizes, *refs),
        out_shape=(
            jax.ShapeDtypeStruct((down, tokens // down + 2 * EDGE, lanes), hidden.dtype),
            jax.ShapeDtypeStruct(wb.shape, wb.dtype),
        ),
        in_specs=[in_vmem(), anywhere],
        out_specs=(in_vmem(), anywhere),
        input_output_aliases={1: 1},
        scratch_shapes=[
            dma((SITES,)), dma((SITES,)),
            dma((depth * across,)), dma((depth * across,)),
            dma((4,)), dma((4,)),
            dma((1,)),
        ],
        compiler_params=pltpu.CompilerParams(
            collective_id=4, has_side_effects=True, vmem_limit_bytes=16 << 20
        ),
        name="spread_hidden",
    )(hidden, wb)


def embed_kernel(taps, length, lengths_ref, hx_ref, wb_hbm, emb_ref, out_ref, wb_ref, wide, cols, sems):
    down, rows, lanes = hx_ref.shape
    arriving = [pltpu.make_async_copy(wb_hbm.at[c], wb_ref.at[c], sems.at[c]) for c in range(down)]
    for copy in arriving:
        copy.start()
    views, tokens, width = emb_ref.shape
    odd = lax.rem(lax.axis_index(Y), 2)
    row = lax.broadcasted_iota(jnp.int32, (rows, lanes), 0)
    inside = (row >= EDGE * (1 - odd)) & (row < rows - EDGE * odd)
    per = lanes // views
    for c in range(down):
        wide[...] = jnp.where(inside, hx_ref[c].astype(jnp.float32), 0.0)
        arriving[c].wait()
        for v in range(views):
            pieces = []
            for k in range(taps):
                first = EDGE + 2 * (k - taps // 2)
                pieces.append(wide[first : first + tokens, v * per : (v + 1) * per])
            cols[...] = jnp.concatenate(pieces, axis=1).astype(jnp.bfloat16)
            part = lax.dot_general(
                cols[...], wb_ref[c], (((1,), (1,)), ((), ())), preferred_element_type=jnp.float32
            )
            if c == 0:
                emb_ref[v] = part
            else:
                emb_ref[v] += part
    moments_into(emb_ref, alive_column(lengths_ref, tokens, length), out_ref)


def embedding(lengths, hx, wb, planes, taps, length):
    down, rows, lanes = hx.shape
    width = wb.shape[1]
    tokens = rows - 2 * EDGE
    parts = share_rows(width, planes) * planes
    return pl.pallas_call(
        lambda *refs: embed_kernel(taps, length, *refs),
        out_shape=(
            jax.ShapeDtypeStruct((2, tokens, width), jnp.float32),
            jax.ShapeDtypeStruct((2, parts, BLOCK), jnp.float32),
        ),
        in_specs=[in_smem(), in_vmem(), pl.BlockSpec(memory_space=pl.ANY)],
        out_specs=(in_vmem(), in_vmem()),
        scratch_shapes=[
            pltpu.VMEM(wb.shape, wb.dtype),
            pltpu.VMEM((rows, lanes), jnp.float32),
            pltpu.VMEM((tokens, wb.shape[2]), jnp.bfloat16),
            pltpu.SemaphoreType.DMA((down,)),
        ],
        compiler_params=pltpu.CompilerParams(vmem_limit_bytes=40 << 20),
        name="embedding",
    )(lengths, hx, wb)


def shards(monomers, keep_mask, lengths, norm_gain, weight_a, weight_b):
    tokens = monomers.shape[0]
    length = tokens // lengths.shape[0]
    taps = weight_a.shape[0]
    sizes = (lax.axis_size(Z), lax.axis_size(X), lax.axis_size(Y))
    xt, wa, wb = gathered_inputs(monomers.T, weight_a, weight_b.transpose(0, 2, 1), sizes)
    hidden = first_conv(
        lengths,
        xt.reshape(-1, tokens),
        wa.reshape(-1, *wa.shape[3:]),
        norm_gain.reshape(-1, BLOCK),
        keep_mask,
        taps,
    )
    hx, wb = spread_hidden(hidden, wb, sizes)
    embedded, parts = embedding(lengths, hx, wb, sizes[1] * sizes[2], taps, length)
    total = total_moments(parts, sizes)
    inverse = inverse_factor(total, embedded.shape[2])
    other = from_partner(inverse)
    return whitened_rows(lengths, embedded, inverse, other, length)


def solution(mesh):
    torus = Mesh(
        mesh.devices.reshape(8, 4, 2, mesh.shape["chan"]), ("batch_0", "batch_1", "batch_2", "chan")
    )
    in_specs = (
        P(BATCH, "chan"),
        P(None, BATCH),
        P(BATCH),
        P(),
        P(None, BATCH, "chan"),
        P(None, "chan", BATCH),
    )
    out_specs = (P(None, BATCH_CHAN, None), P(BATCH_CHAN))
    return jax.shard_map(
        shards, mesh=torus, in_specs=in_specs, out_specs=out_specs, check_vma=False
    )
```

```python
import jax
import jax.numpy as jnp
from jax import lax
from jax.experimental import pallas as pl
from jax.experimental.pallas import tpu as pltpu
from jax.sharding import Mesh
from jax.sharding import PartitionSpec as P

BATCH = ("batch_0", "batch_1", "batch_2")
BATCH_CHAN = ("batch_0", "batch_1", "batch_2", "chan")


EPS_NORM = 1e-05
EPS_COV = 0.0001
HI = lax.Precision.HIGHEST
MESH_IDS = pl.DeviceIdType.MESH
Z, X, CORE, Y = "batch_0", "batch_1", "batch_2", "chan"
AXES = (Z, X, CORE, Y)
BLOCK = 128
GROUP = 8


def dot_of(a, b, dims, precision=HI):
    return lax.dot_general(
        a, b, (dims, ((), ())), precision=precision, preferred_element_type=jnp.float32
    )


def in_vmem():
    return pl.BlockSpec(memory_space=pltpu.VMEM)


def block_pairs(width):
    return [(i, k) for i in range(width // BLOCK) for k in range(i + 1)]


def share_rows(width, planes):
    rows = len(block_pairs(width)) * BLOCK
    return -(-rows // (planes * GROUP)) * GROUP


def alive_column(lengths_ref, tokens, length):
    start = lax.axis_index(Y) * tokens
    limit = lengths_ref[start // length] - lax.rem(start, length)
    return jnp.where(lax.broadcasted_iota(jnp.int32, (tokens, 1), 0) < limit, 1.0, 0.0)


def in_smem():
    return pl.BlockSpec(memory_space=pltpu.SMEM)


def moments_into(emb_ref, alive, out_ref):
    views, tokens, width = emb_ref.shape
    pairs = block_pairs(width)
    at = len(pairs) * BLOCK
    half = BLOCK // 2
    for v in range(views):
        masked = emb_ref[v] * alive
        for i in range(width // BLOCK):
            wide = (i + 1) * BLOCK
            strip = dot_of(
                masked[:, i * BLOCK : wide], masked[:, :wide], ((0,), (0,))
            )
            for k in range(i + 1):
                b = pairs.index((i, k))
                out_ref[v, b * BLOCK : (b + 1) * BLOCK, :] = strip[:, k * BLOCK : (k + 1) * BLOCK]
        if out_ref.shape[1] > at:
            out_ref[v, at:, :] = jnp.zeros((out_ref.shape[1] - at, BLOCK), jnp.float32)
        sums = jnp.sum(masked, axis=0, keepdims=True)
        spare = [sums[:, k * half : (k + 1) * half] for k in range(width // half)]
        spare.append(jnp.broadcast_to(jnp.sum(alive, axis=0, keepdims=True), (1, half)))
        out_ref[v, 0 : len(spare), half:] = jnp.concatenate(spare, axis=0)


def total_kernel(sizes, parts, part_ref, out_ref, pair_in, mine, plane_in, share, line_in, total, *sems):
    depth, across, down = sizes
    planes = across * down
    rows = share.shape[0]
    z, x = lax.axis_index(Z), lax.axis_index(X)
    core, y = lax.axis_index(CORE), lax.axis_index(Y)
    me = x * down + y
    partner = 1 - core
    pair_send, pair_recv, plane_send, plane_recv, line_send, line_recv, back_send, back_recv = sems

    def in_plane(step):
        other = lax.rem(me + step, planes)
        return other, (z, other // down, core, lax.rem(other, down))

    def in_line(step):
        other = lax.rem(z + step, depth)
        return other, (other, x, core, y)

    barrier = pltpu.get_barrier_semaphore()
    pl.semaphore_signal(barrier, inc=1, device_id=(z, x, partner, y), device_id_type=MESH_IDS)
    for step in range(1, planes):
        pl.semaphore_signal(barrier, inc=1, device_id=in_plane(step)[1], device_id_type=MESH_IDS)
    for step in range(1, depth):
        pl.semaphore_signal(barrier, inc=1, device_id=in_line(step)[1], device_id_type=MESH_IDS)
    pl.semaphore_wait(barrier, 1 + planes - 1 + depth - 1)

    def sent(src, dst, send, recv, device):
        copy = pltpu.make_async_remote_copy(
            src_ref=src, dst_ref=dst, send_sem=send, recv_sem=recv,
            device_id=device, device_id_type=MESH_IDS,
        )
        copy.start()
        return copy

    starts = [sum(parts[:i]) for i in range(len(parts))]

    def within(i):
        return pl.ds(starts[i], parts[i])

    swaps = [
        sent(
            part_ref.at[partner, :, within(i)], pair_in.at[:, within(i)],
            pair_send.at[i], pair_recv.at[i], (z, x, partner, y),
        )
        for i in range(len(parts))
    ]

    def summed(buffer, own, count, i):
        acc = None
        for source in range(count):
            piece = buffer[lax.rem(own - source + count, count), within(i)]
            acc = piece if acc is None else acc + piece
        return acc

    spread, lines, back = {}, {}, {}
    for i in range(len(parts)):
        swaps[i].wait_recv()
        mine[:, within(i)] = part_ref[core, :, within(i)] + pair_in[:, within(i)]
        for step in range(1, planes):
            other, device = in_plane(step)
            spread[i, step] = sent(
                mine.at[other, within(i)], plane_in.at[step, within(i)],
                plane_send.at[i, step], plane_recv.at[i, step], device,
            )

    def to_line(i):
        for step in range(1, planes):
            spread[i, step].wait_recv()
        plane_in[0, within(i)] = mine[me, within(i)]
        share[within(i)] = summed(plane_in, me, planes, i)
        for step in range(1, depth):
            lines[i, step] = sent(
                share.at[within(i)], line_in.at[step, within(i)],
                line_send.at[i, step], line_recv.at[i, step], in_line(step)[1],
            )

    def to_plane(i):
        for step in range(1, depth):
            lines[i, step].wait_recv()
        line_in[0, within(i)] = share[within(i)]
        total[within(i)] = summed(line_in, z, depth, i)
        for step in range(1, planes):
            back[i, step] = sent(
                total.at[within(i)], out_ref.at[me, within(i)],
                back_send.at[i, step], back_recv.at[i, step], in_plane(step)[1],
            )
        out_ref[me, within(i)] = total[within(i)]

    lag = 2
    for i in range(len(parts) + lag):
        if i < len(parts):
            to_line(i)
        if i >= lag:
            to_plane(i - lag)
    for copy in back.values():
        copy.wait_recv()
    for copy in swaps:
        copy.wait_send()
    for group in (spread, lines, back):
        for copy in group.values():
            copy.wait_send()


def total_moments(parts, mesh_sizes):
    depth, across, down = mesh_sizes
    planes = across * down
    _, all_rows, lanes = parts.shape
    rows = all_rows // planes
    tiles = rows // GROUP
    pieces = tuple(GROUP * (tiles // 4 + (1 if i < tiles % 4 else 0)) for i in range(4))
    dma = pltpu.SemaphoreType.DMA
    vm = lambda *shape: pltpu.VMEM(shape, jnp.float32)
    return pl.pallas_call(
        lambda *refs: total_kernel(mesh_sizes, pieces, *refs),
        out_shape=jax.ShapeDtypeStruct((planes, rows, lanes), jnp.float32),
        in_specs=[in_vmem()],
        out_specs=in_vmem(),
        scratch_shapes=[
            vm(planes, rows, lanes),
            vm(planes, rows, lanes),
            vm(planes, rows, lanes),
            vm(rows, lanes),
            vm(depth, rows, lanes),
            vm(rows, lanes),
            dma((4,)), dma((4,)),
            dma((4, planes)), dma((4, planes)),
            dma((4, depth)), dma((4, depth)),
            dma((4, planes)), dma((4, planes)),
        ],
        compiler_params=pltpu.CompilerParams(
            collective_id=1, has_side_effects=True, vmem_limit_bytes=32 << 20
        ),
        name="total_moments",
    )(parts.reshape(2, planes, rows, lanes)).reshape(all_rows, lanes)


def splat_row(v, a):
    return jnp.broadcast_to(v[a : a + 1, :], (GROUP, BLOCK))


def splat_lane(v, j):
    return jnp.broadcast_to(v[:, j : j + 1], (GROUP, BLOCK))


def base_inverse(load, store):
    count = BLOCK // GROUP
    groups = [load(g) for g in range(count)]
    lane = lax.broadcasted_iota(jnp.int32, (GROUP, BLOCK), 1)
    sub = lax.broadcasted_iota(jnp.int32, (GROUP, BLOCK), 0)
    steps = range(GROUP)
    twos = range(GROUP // 2)
    for p in range(count):
        j = GROUP * p
        v = groups[p]
        cols = [splat_lane(v, j + a) for a in steps]
        e = [[splat_row(cols[a], b) if b >= a else None for a in steps] for b in steps]
        panel = (lane >= j) & (lane < j + GROUP)
        rows = [
            jnp.where(panel, jnp.where(lane == j + a, 1.0, 0.0), splat_row(v, a)) for a in steps
        ]
        f, inv = {}, []
        for t in twos:
            m, n = 2 * t, 2 * t + 1
            e00, e10, e11 = e[m][m], e[n][m], e[n][n]
            det = e00 * e11 - e10 * e10
            rd = 1.0 / det
            inv.append(rd)
            for b in range(n + 1, GROUP):
                f0 = (e11 * e[b][m] - e10 * e[b][n]) * rd
                f1 = (e00 * e[b][n] - e10 * e[b][m]) * rd
                f[b, t] = (f0, f1)
                for c in range(n + 1, b + 1):
                    e[b][c] = e[b][c] - (f0 * e[c][m] + f1 * e[c][n])
                rows[b] = rows[b] - (f0 * rows[m] + f1 * rows[n])
        out = None
        q = [None] * GROUP
        for t in reversed(twos):
            m, n = 2 * t, 2 * t + 1
            e00, e10, e11, rd = e[m][m], e[n][m], e[n][n], inv[t]
            q0 = (e11 * rows[m] - e10 * rows[n]) * rd
            q1 = (e00 * rows[n] - e10 * rows[m]) * rd
            for b in reversed(range(n + 1, GROUP)):
                q0 = q0 - f[b, t][0] * q[b]
                q1 = q1 - f[b, t][1] * q[b]
            q[m], q[n] = q0, q1
        for g in range(p + 1, count):
            x = groups[g]
            terms = [splat_lane(x, j + a) * q[a] for a in steps]
            pairs = [terms[2 * t] + terms[2 * t + 1] for t in twos]
            late = jnp.where(panel, 0.0, x) - ((pairs[3] + pairs[2]) + pairs[1])
            groups[g] = late - pairs[0]
        for t in twos:
            m, n = 2 * t, 2 * t + 1
            e00, e10, e11 = e[m][m], e[n][m], e[n][n]
            ratio = e10 / e00
            first = rows[m] * lax.rsqrt(e00)
            second = (rows[n] - ratio * rows[m]) * lax.rsqrt(e11 - ratio * e10)
            out = first if out is None else jnp.where(sub == m, first, out)
            out = jnp.where(sub == n, second, out)
        store(p, jnp.where(lane < j + GROUP, out, 0.0))


def factor_kernel(total_ref, out_ref, work, m_ref):
    width = work.shape[1]
    blocks = width // BLOCK
    pairs = block_pairs(width)
    half = BLOCK // 2
    spare = total_ref[0 : 2 * GROUP, half:]
    last = width // half
    count = spare[last : last + 1, 0:1]
    center = jnp.concatenate([spare[k : k + 1, :] for k in range(last)], axis=1) / count
    sub = lax.broadcasted_iota(jnp.int32, (GROUP, width), 0)
    center8 = jnp.where(sub == 0, jnp.broadcast_to(center, (GROUP, width)), 0.0)
    high = center.astype(jnp.bfloat16).astype(jnp.float32)
    middle = (center - high).astype(jnp.bfloat16).astype(jnp.float32)
    low = center - high - middle

    def stacked(parts):
        rows = jnp.zeros((GROUP, width), jnp.float32)
        for i, part in enumerate(parts):
            rows = jnp.where(sub == i, jnp.broadcast_to(part, (GROUP, width)), rows)
        return rows.astype(jnp.bfloat16)

    one_side = stacked((high, high, middle, high, low, middle, middle, low))
    other_side = stacked((high, middle, high, low, high, middle, low, middle))
    eye = lax.broadcasted_iota(jnp.int32, (BLOCK, BLOCK), 0) == lax.broadcasted_iota(
        jnp.int32, (BLOCK, BLOCK), 1
    )
    lower = lax.broadcasted_iota(jnp.int32, (BLOCK, BLOCK), 0) >= lax.broadcasted_iota(
        jnp.int32, (BLOCK, BLOCK), 1
    )
    for b, (i, k) in enumerate(pairs):
        outer = dot_of(
            one_side[:, i * BLOCK : (i + 1) * BLOCK],
            other_side[:, k * BLOCK : (k + 1) * BLOCK],
            ((0,), (0,)),
            lax.Precision.DEFAULT,
        )
        raw = total_ref[b * BLOCK : (b + 1) * BLOCK, :]
        if b == 0:
            raw = jnp.where(lower, raw, raw.T)
        block = raw / count - outer
        if i == k:
            block = block + jnp.where(eye, EPS_COV, 0.0)
        work[i * BLOCK : (i + 1) * BLOCK, k * BLOCK : (k + 1) * BLOCK] = block
        if i != k:
            work[k * BLOCK : (k + 1) * BLOCK, i * BLOCK : (i + 1) * BLOCK] = block.T
    strip_block = lax.broadcasted_iota(jnp.int32, (BLOCK, width), 1) // BLOCK
    strip_eye = jnp.where(
        lax.broadcasted_iota(jnp.int32, (BLOCK, width), 1) % BLOCK
        == lax.broadcasted_iota(jnp.int32, (BLOCK, width), 0),
        1.0,
        0.0,
    )

    def step(k, _):
        here = pl.multiple_of(k * BLOCK, BLOCK)

        def load(g):
            return work[pl.ds(pl.multiple_of(here + GROUP * g, GROUP), GROUP), pl.ds(here, BLOCK)]

        def store(g, val):
            m_ref[GROUP * g : GROUP * (g + 1), :] = val

        base_inverse(load, store)
        m = m_ref[...]
        row = jnp.where(strip_block == k, strip_eye, work[pl.ds(here, BLOCK), :])
        across = dot_of(m, row, ((1,), (0,)))
        for done in range(blocks - 1):

            @pl.when(k == done)
            def _():
                first = (done + 1) * BLOCK
                col_block = lax.broadcasted_iota(jnp.int32, (width - first, width), 1) // BLOCK
                left = dot_of(work[first:, done * BLOCK : first], m, ((1,), (1,)))
                kept = jnp.where(col_block == done, 0.0, work[first:, :])
                work[first:, :] = kept - dot_of(left, across, ((1,), (0,)))

        work[pl.ds(here, BLOCK), :] = jnp.where(strip_block <= k, across, 0.0)
        return 0

    lax.fori_loop(0, blocks, step, 0)
    out_ref[:width, :] = work[...]
    out_ref[width:, :] = center8


def inverse_factor(total, width):
    return pl.pallas_call(
        factor_kernel,
        out_shape=jax.ShapeDtypeStruct((width + GROUP, width), jnp.float32),
        in_specs=[in_vmem()],
        out_specs=in_vmem(),
        scratch_shapes=[
            pltpu.VMEM((width, width), jnp.float32),
            pltpu.VMEM((BLOCK, BLOCK), jnp.float32),
        ],
        compiler_params=pltpu.CompilerParams(vmem_limit_bytes=32 << 20),
        name="inverse_factor",
    )(total)


def swap_kernel(own_ref, out_ref, send, recv):
    z, x = lax.axis_index(Z), lax.axis_index(X)
    core, y = lax.axis_index(CORE), lax.axis_index(Y)
    other = (z, x, 1 - core, y)
    barrier = pltpu.get_barrier_semaphore()
    pl.semaphore_signal(barrier, inc=1, device_id=other, device_id_type=MESH_IDS)
    pl.semaphore_wait(barrier, 1)
    copy = pltpu.make_async_remote_copy(
        src_ref=own_ref, dst_ref=out_ref, send_sem=send, recv_sem=recv,
        device_id=other, device_id_type=MESH_IDS,
    )
    copy.start()
    copy.wait()


def from_partner(own):
    return pl.pallas_call(
        swap_kernel,
        out_shape=jax.ShapeDtypeStruct(own.shape, own.dtype),
        in_specs=[in_vmem()],
        out_specs=in_vmem(),
        scratch_shapes=[pltpu.SemaphoreType.DMA, pltpu.SemaphoreType.DMA],
        compiler_params=pltpu.CompilerParams(
            collective_id=2, has_side_effects=True, vmem_limit_bytes=16 << 20
        ),
        name="from_partner",
    )(own)


def whiten_kernel(length, lengths_ref, emb_ref, own_ref, other_ref, out_ref, gap_ref):
    views, tokens, width = emb_ref.shape
    core = lax.axis_index(CORE)
    alive = alive_column(lengths_ref, tokens, length)
    for ref, v in ((own_ref, core), (other_ref, 1 - core)):
        centered = (emb_ref[v] - ref[width : width + 1, :]) * alive
        part = 2 * BLOCK
        for first in range(0, width, part):
            last = first + part
            out_ref[v, :, first:last] = dot_of(centered[:, :last], ref[first:last, :last], ((1,), (1,)))
    gap = out_ref[0] - out_ref[1]
    ones = jnp.ones((GROUP, width), jnp.float32)
    sums = dot_of(ones, gap * gap, ((1,), (1,))) / width
    for k in range(tokens // BLOCK):
        gap_ref[k : k + 1, :] = sums[0:1, k * BLOCK : (k + 1) * BLOCK]


def whitened_rows(lengths, embedded, own, other, length):
    views, tokens, width = embedded.shape
    whitened, gap = pl.pallas_call(
        lambda *refs: whiten_kernel(length, *refs),
        out_shape=(
            jax.ShapeDtypeStruct(embedded.shape, jnp.float32),
            jax.ShapeDtypeStruct((tokens // BLOCK, BLOCK), jnp.float32),
        ),
        in_specs=[in_smem()] + [in_vmem()] * 3,
        out_specs=(in_vmem(), in_vmem()),
        compiler_params=pltpu.CompilerParams(vmem_limit_bytes=32 << 20),
        name="whitened_rows",
    )(lengths, embedded, own, other)
    return whitened, gap.reshape(tokens)


class Sender:
    def __init__(self, send_sems, recv_sems):
        self.send_sems, self.recv_sems = send_sems, recv_sems
        self.started, self.used = [], 0

    def site(self):
        self.used += 1
        return self.used - 1

    def copy(self, site, src, dst, device):
        return pltpu.make_async_remote_copy(
            src_ref=src, dst_ref=dst,
            send_sem=self.send_sems.at[site], recv_sem=self.recv_sems.at[site],
            device_id=device, device_id_type=MESH_IDS,
        )

    def send(self, site, src, dst, device):
        made = self.copy(site, src, dst, device)
        made.start()
        self.started.append(made)

    def arrived(self, site, dst, device):
        self.copy(site, dst, dst, device).wait_recv()

    def finish(self):
        for made in self.started:
            made.wait_send()


class Ring:
    def __init__(self, sender, size, pos, device_at, slot_at, hops, own=None):
        self.sender, self.size, self.pos = sender, size, pos
        self.device_at, self.slot_at = device_at, slot_at
        self.hops = {1: hops[0], -1: hops[1]}
        self.own = own
        self.sites = {
            (sign, h): sender.site() for sign in (1, -1) for h in range(1, self.hops[sign] + 1)
        }

    def at(self, offset):
        return lax.rem(self.pos + offset + 2 * self.size, self.size)

    def pass_on(self, sign, h):
        source = self.at(-sign * (h - 1))
        slot = self.slot_at(source)
        src = self.own if h == 1 and self.own is not None else slot
        self.sender.send(self.sites[sign, h], src, slot, self.device_at(self.at(sign)))

    def launch(self):
        for sign in (1, -1):
            self.pass_on(sign, 1)

    def has(self, sign, h):
        return h <= self.hops[sign]

    def take(self, sign, h):
        slot = self.slot_at(self.at(-sign * h))
        self.sender.arrived(self.sites[sign, h], slot, self.device_at(self.at(-sign)))
        if h < self.hops[sign]:
            self.pass_on(sign, h + 1)
        return (sign * h) % self.size


class Place:
    def __init__(self, sizes):
        self.depth, self.across, self.down = sizes
        self.z, self.x = lax.axis_index(Z), lax.axis_index(X)
        self.core, self.y = lax.axis_index(CORE), lax.axis_index(Y)
        self.partner = (self.z, self.x, 1 - self.core, self.y)

    def z_at(self, s):
        return lax.rem(self.z - s + 2 * self.depth, self.depth)

    def x_at(self, t):
        return lax.rem(self.x - t + 2 * self.across, self.across)

    def y_at(self, s):
        return lax.rem(self.y + s + 2 * self.down, self.down)

    def along_z(self, zz):
        return (zz, self.x, self.core, self.y)

    def along_x(self, xx):
        return (self.z, xx, self.core, self.y)

    def along_y(self, yy):
        return (self.z, self.x, self.core, yy)

    def greet(self):
        self.greeted(self.greeting())

    def greeting(self):
        peers = [self.along_z(self.z_at(s)) for s in (1, -1)]
        peers += [self.along_x(self.x_at(s)) for s in (1, -1)]
        peers += [self.along_y(self.y_at(s)) for s in range(1, self.down)]
        peers += [self.partner]
        barrier = pltpu.get_barrier_semaphore()
        for peer in peers:
            pl.semaphore_signal(barrier, inc=1, device_id=peer, device_id_type=MESH_IDS)
        return len(peers)

    def greeted(self, count):
        pl.semaphore_wait(pltpu.get_barrier_semaphore(), count)


SITES = 64
FEW = 4


def rows_of_slab(zz, xx, core, across):
    return pl.ds(pl.multiple_of(((zz * across + xx) * 2 + core) * GROUP, GROUP), GROUP)


def gather_kernel(
    sizes, xt_ref, hbm_a, hbm_b, xt_out, wa_out, wb_out, raw_a, raw_b, wa_ref, wb_ref,
    ring_send, ring_recv, pair_send, pair_recv, y_send, y_recv, local,
):
    here = Place(sizes)
    depth, across, down = sizes
    z, x, core, y = here.z, here.x, here.core, here.y
    greeted = here.greeting()
    load_a = pltpu.make_async_copy(hbm_a, raw_a, local.at[3])
    load_b = pltpu.make_async_copy(hbm_b, raw_b, local.at[4])
    load_a.start()
    load_b.start()
    load_a.wait()
    load_b.wait()
    rows_a = jnp.concatenate([raw_a[k] for k in range(raw_a.shape[0])], axis=1)
    for i in range(wa_ref.shape[0]):
        wa_ref[i] = rows_a[i * FEW : (i + 1) * FEW, :]
    wb_ref[...] = jnp.concatenate([raw_b[k] for k in range(raw_b.shape[0])], axis=1)
    here.greeted(greeted)
    half = xt_ref.shape[0] // 2

    def slab(zz, xx, cc):
        return wb_out.at[:, rows_of_slab(zz, xx, cc, across), :]

    def own_part(yy):
        return wb_out.at[yy, rows_of_slab(z, x, core, across), :]

    own = [
        pltpu.make_async_copy(wb_ref, own_part(y), local.at[0]),
        pltpu.make_async_copy(wa_ref, wa_out.at[z, x, core], local.at[1]),
        pltpu.make_async_copy(xt_ref, xt_out.at[y], local.at[2]),
    ]
    for copy in own:
        copy.start()

    ys = Sender(y_send, y_recv)
    wb_sites = {s: ys.site() for s in range(1, down)}
    for s in range(1, down):
        ys.send(wb_sites[s], wb_ref, own_part(y), here.along_y(here.y_at(s)))

    def piece(yy, p):
        return xt_out.at[yy, p * half : (p + 1) * half, :]

    xt_sites = {(sign, p, h): ys.site() for sign in (1, -1) for p in (0, 1) for h in (1, 2)}
    for first in (0, 1):
        for sign in (1, -1):
            p = first if sign == 1 else 1 - first
            ys.send(
                xt_sites[sign, p, 1], xt_ref.at[p * half : (p + 1) * half, :], piece(y, p),
                here.along_y(here.y_at(sign)),
            )

    def first_pieces():
        for sign, p in ((1, 0), (-1, 1)):
            source = here.y_at(-sign)
            ys.arrived(xt_sites[sign, p, 1], piece(source, p), here.along_y(source))
            ys.send(xt_sites[sign, p, 2], piece(source, p), piece(source, p), here.along_y(here.y_at(sign)))

    def last_pieces():
        for sign, p in ((1, 1), (-1, 0)):
            source = here.y_at(-sign)
            ys.arrived(xt_sites[sign, p, 1], piece(source, p), here.along_y(source))
        for sign, p in ((1, 0), (-1, 1)):
            ys.arrived(xt_sites[sign, p, 2], piece(here.y_at(2), p), here.along_y(here.y_at(-sign)))

    def slabs_ready():
        for s in range(1, down):
            source = here.y_at(-s)
            ys.arrived(wb_sites[s], own_part(source), here.along_y(source))
        own[0].wait()

    pairs = Sender(pair_send, pair_recv)

    def to_partner(s, t):
        slot = wa_out.at[here.z_at(s), here.x_at(t), core]
        src = wa_ref if s == 0 and t == 0 else slot
        pairs.send(s * across + t, src, slot, here.partner)

    @pl.when(core == 0)
    def _():
        rings = Sender(ring_send, ring_recv)
        down_z = Ring(rings, depth, z, here.along_z, lambda zz: wa_out.at[zz, x, core], (4, 3), wa_ref)
        slabs_z = Ring(rings, depth, z, here.along_z, lambda zz: slab(zz, x, core), (3, 4))
        on_x = [
            Ring(
                rings, across, x, here.along_x,
                lambda xx, s=s: wa_out.at[here.z_at(s), xx, core],
                (2, 1) if s % 2 == 0 else (1, 2),
                wa_ref if s == 0 else None,
            )
            for s in range(depth)
        ]
        down_z.launch()
        on_x[0].launch()
        to_partner(0, 0)
        slabs_ready()
        slabs_z.launch()
        waiting = [0]
        for h in range(1, 5):
            arrived = []
            for sign in (1, -1):
                if down_z.has(sign, h):
                    s = down_z.take(sign, h)
                    on_x[s].launch()
                    to_partner(s, 0)
                    arrived.append(s)
            for sign in (1, -1):
                if slabs_z.has(sign, h):
                    slabs_z.take(sign, h)
            for s in waiting:
                for sign in (1, -1):
                    to_partner(s, on_x[s].take(sign, 1))
            waiting = arrived
            if h == 3:
                first_pieces()
        for s in waiting:
            for sign in (1, -1):
                to_partner(s, on_x[s].take(sign, 1))
        for s in [0, 1, 7, 2, 6, 3, 5, 4]:
            to_partner(s, on_x[s].take(1 if s % 2 == 0 else -1, 2))
        rings.finish()

    @pl.when(core == 1)
    def _():
        rings = Sender(ring_send, ring_recv)
        own_x = Ring(rings, across, x, here.along_x, lambda xx: wa_out.at[z, xx, core], (2, 1), wa_ref)
        slabs_x = Ring(rings, across, x, here.along_x, lambda xx: slab(z, xx, core), (1, 2))
        on_z = [
            Ring(
                rings, depth, z, here.along_z,
                lambda zz, t=t: wa_out.at[zz, here.x_at(t), core],
                (4, 3) if t % 2 == 0 else (3, 4),
                wa_ref if t == 0 else None,
            )
            for t in range(across)
        ]
        own_x.launch()
        on_z[0].launch()
        to_partner(0, 0)
        slabs_ready()
        slabs_x.launch()
        for sign, h in ((1, 1), (-1, 1), (1, 2)):
            t = own_x.take(sign, h)
            on_z[t].launch()
            to_partner(0, t)
        for sign, h in ((1, 1), (-1, 1), (-1, 2)):
            slabs_x.take(sign, h)
        for h in range(1, 5):
            for t in (0, 1, 3, 2):
                for sign in (1, -1):
                    if on_z[t].has(sign, h):
                        to_partner(on_z[t].take(sign, h), t)
            if h == 1:
                first_pieces()
        rings.finish()

    last_pieces()
    for s in range(depth):
        for t in range(across):
            slot = wa_out.at[here.z_at(s), here.x_at(t), 1 - core]
            made = pairs.copy(s * across + t, slot, slot, here.partner)
            made.wait_recv()
            made.wait_send()
    ys_wait = ys.started
    for made in ys_wait[: down - 1 + 4]:
        made.wait_send()
    for sign, p in ((1, 0), (-1, 1)):
        ys.copy(
            xt_sites[sign, p, 2], piece(here.y_at(-sign), p), piece(here.y_at(-sign), p),
            here.along_y(here.y_at(sign)),
        ).wait_send()
    own[1].wait()
    own[2].wait()


def gathered_inputs(xt, wa, wb, sizes):
    depth, across, down = sizes
    dma = pltpu.SemaphoreType.DMA
    anywhere = pl.BlockSpec(memory_space=pl.ANY)
    taps, rows_a, width = wa.shape
    rows_b = wb.shape[1]
    return pl.pallas_call(
        lambda *refs: gather_kernel(sizes, *refs),
        out_shape=(
            jax.ShapeDtypeStruct((down, *xt.shape), xt.dtype),
            jax.ShapeDtypeStruct((depth, across, 2, rows_a // FEW, FEW, taps * width), wa.dtype),
            jax.ShapeDtypeStruct((down, depth * across * 2 * rows_b, taps * width), wb.dtype),
        ),
        in_specs=[anywhere] * 3,
        out_specs=(in_vmem(), anywhere, anywhere),
        scratch_shapes=[
            pltpu.VMEM(wa.shape, wa.dtype),
            pltpu.VMEM(wb.shape, wb.dtype),
            pltpu.VMEM((rows_a // FEW, FEW, taps * width), wa.dtype),
            pltpu.VMEM((rows_b, taps * width), wb.dtype),
            dma((SITES,)), dma((SITES,)),
            dma((depth * across,)), dma((depth * across,)),
            dma((16,)), dma((16,)),
            dma((5,)),
        ],
        compiler_params=pltpu.CompilerParams(
            collective_id=3, has_side_effects=True, vmem_limit_bytes=16 << 20
        ),
        cost_estimate=pl.CostEstimate(flops=20_000_000_000, bytes_accessed=80_000_000, transcendentals=0),
        name="gathered_inputs",
    )(xt, wa, wb)


def gate(values):
    return 0.5 * values * (1.0 + jnp.tanh(0.7978845608 * (values + 0.044715 * values * values * values)))


PAD = 8
ROWS = 128
EDGE = 16


def conv_kernel(
    sizes, lengths_ref, xt_ref, wa_hbm, gain_hbm, keep_hbm, out_ref,
    wa_ref, gain_ref, keep_ref, n_ref, w_ref, stage, p_ref, cols, sems,
):
    sequences, length, taps = sizes
    channels, tokens = xt_ref.shape
    chunks, few_count, _, lanes = wa_ref.shape
    chunk_rows = few_count * FEW
    loads = 4
    each = chunks // loads
    arriving = [
        pltpu.make_async_copy(wa_hbm.at[pl.ds(i * each, each)], wa_ref.at[pl.ds(i * each, each)], sems.at[i])
        for i in range(loads)
    ]
    small = [
        pltpu.make_async_copy(gain_hbm, gain_ref, sems.at[loads]),
        pltpu.make_async_copy(keep_hbm, keep_ref, sems.at[loads + 1]),
    ]
    for copy in small + arriving:
        copy.start()
    eye = lax.broadcasted_iota(jnp.int32, (BLOCK, BLOCK), 0) == lax.broadcasted_iota(
        jnp.int32, (BLOCK, BLOCK), 1
    )
    squares = jnp.zeros((1, tokens), jnp.float32)
    for i in range(channels // BLOCK):
        part = xt_ref[i * BLOCK : (i + 1) * BLOCK, :].astype(jnp.float32)
        squares = squares + jnp.sum(part * part, axis=0, keepdims=True)
    scale = lax.rsqrt(squares / channels + EPS_NORM)
    for copy in small:
        copy.wait()
    for i in range(channels // BLOCK):
        part = xt_ref[i * BLOCK : (i + 1) * BLOCK, :].astype(jnp.float32)
        gain = jnp.sum(
            jnp.where(eye, jnp.broadcast_to(gain_ref[i : i + 1, :], (BLOCK, BLOCK)), 0.0), axis=1, keepdims=True
        )
        normed = (part * scale * gain).astype(jnp.bfloat16)
        n_ref[:, i * BLOCK : (i + 1) * BLOCK] = normed.T

    token = lax.broadcasted_iota(jnp.int32, (GROUP, tokens), 1)
    position = token % length
    limit = jnp.zeros((GROUP, tokens), jnp.int32)
    for s in range(sequences):
        limit = jnp.where(token // length == s, lengths_ref[s], limit)
    view = lax.broadcasted_iota(jnp.int32, (GROUP, tokens), 0)
    keep = jnp.where(view == 0, keep_ref[0:1, :], jnp.where(view == 1, keep_ref[1:2, :], 0))
    kept = jnp.where(position < limit, keep, 0).astype(jnp.float32)
    for k in range(taps):
        move = k - taps // 2
        rolled = kept if move == 0 else pltpu.roll(kept, (-move) % tokens, 1)
        inside = (position + move >= 0) & (position + move < length)
        cols[k] = jnp.where(inside, rolled, 0.0).T

    group = 4

    def relay(q, _):
        for i in range(group):
            for r in range(few_count):
                first = i * chunk_rows + r * FEW
                stage[first : first + FEW, :] = wa_ref[q * group + i, r].astype(jnp.float32)
        at = pl.multiple_of(q * group * chunk_rows, group * chunk_rows)
        w_ref[pl.ds(at, group * chunk_rows), :] = stage[...].astype(jnp.bfloat16)
        return 0

    for i in range(loads):
        arriving[i].wait()
        lax.fori_loop(i * each // group, (i + 1) * each // group, relay, 0)

    width = lanes // taps
    p_ref[0:PAD, :] = jnp.zeros((PAD, lanes), jnp.float32)
    p_ref[PAD + length :, :] = jnp.zeros((PAD, lanes), jnp.float32)

    def sequence(s, _):
        start = pl.multiple_of(s * length, length)
        for r in range(length // ROWS):
            p_ref[PAD + r * ROWS : PAD + (r + 1) * ROWS, :] = jnp.dot(
                n_ref[pl.ds(start + r * ROWS, ROWS), :], w_ref[...], preferred_element_type=jnp.float32
            )
        for r in range(length // ROWS):
            hidden = []
            for v in range(2):
                acc = None
                for k in range(taps):
                    first = PAD + r * ROWS + k - taps // 2
                    piece = p_ref[first : first + ROWS, k * width : (k + 1) * width]
                    piece = piece * cols[k, pl.ds(start + r * ROWS, ROWS), v : v + 1]
                    acc = piece if acc is None else acc + piece
                hidden.append(gate(acc))
            out_ref[pl.ds(start + r * ROWS, ROWS), :] = jnp.concatenate(hidden, axis=1).astype(jnp.bfloat16)
        return 0

    lax.fori_loop(0, sequences, sequence, 0)


def first_conv(lengths, xt, wa, gain, keep, taps):
    channels, tokens = xt.shape
    chunks, few_count, _, lanes = wa.shape
    chunk_rows = few_count * FEW
    sequences = lengths.shape[0]
    length = tokens // sequences
    bf, f32 = jnp.bfloat16, jnp.float32
    return pl.pallas_call(
        lambda *refs: conv_kernel((sequences, length, taps), *refs),
        out_shape=jax.ShapeDtypeStruct((tokens, 2 * lanes // taps), bf),
        in_specs=[in_smem(), in_vmem()] + [pl.BlockSpec(memory_space=pl.ANY)] * 3,
        out_specs=in_vmem(),
        scratch_shapes=[
            pltpu.VMEM(wa.shape, bf),
            pltpu.VMEM(gain.shape, f32),
            pltpu.VMEM(keep.shape, keep.dtype),
            pltpu.VMEM((tokens, channels), bf),
            pltpu.VMEM((channels, lanes), bf),
            pltpu.VMEM((4 * chunk_rows, lanes), f32),
            pltpu.VMEM((length + 2 * PAD, lanes), f32),
            pltpu.VMEM((taps, tokens, GROUP), f32),
            pltpu.SemaphoreType.DMA((6,)),
        ],
        compiler_params=pltpu.CompilerParams(vmem_limit_bytes=40 << 20),
        name="first_conv",
    )(lengths, xt, wa, gain, keep)


def spread_kernel(
    sizes, h_ref, wb_in, hx_out, wb_out, ring_send, ring_recv, pair_send, pair_recv, y_send, y_recv, local
):
    here = Place(sizes)
    depth, across, down = sizes
    z, x, core, y = here.z, here.x, here.core, here.y
    here.greet()
    rows = h_ref.shape[0] // down
    window = rows + EDGE

    def source_rows(yy):
        return pl.ds(pl.multiple_of(yy * rows - EDGE * lax.rem(yy, 2), EDGE), window)

    def target_rows(yy):
        return pl.ds(pl.multiple_of(EDGE - EDGE * lax.rem(yy, 2), EDGE), window)

    ys = Sender(y_send, y_recv)
    for s in (2, 1, 3):
        other = here.y_at(s)
        ys.send(s, h_ref.at[source_rows(other), :], hx_out.at[y, target_rows(other), :], here.along_y(other))
    own = pltpu.make_async_copy(h_ref.at[source_rows(y), :], hx_out.at[y, target_rows(y), :], local.at[0])
    own.start()

    def slab(zz, xx, cc):
        return wb_out.at[:, rows_of_slab(zz, xx, cc, across), :]

    pairs = Sender(pair_send, pair_recv)

    def to_partner(s, t):
        slot = slab(here.z_at(s), here.x_at(t), core)
        pairs.send(s * across + t, slot, slot, here.partner)

    @pl.when(core == 0)
    def _():
        rings = Sender(ring_send, ring_recv)
        on_x = [
            Ring(
                rings, across, x, here.along_x,
                lambda xx, s=s: slab(here.z_at(s), xx, core),
                (2, 1) if s % 2 == 0 else (1, 2),
            )
            for s in range(depth)
        ]
        for s in range(depth):
            on_x[s].launch()
        for s in range(depth):
            to_partner(s, 0)
        for s in range(depth):
            for sign in (1, -1):
                to_partner(s, on_x[s].take(sign, 1))
        for s in range(depth):
            to_partner(s, on_x[s].take(1 if s % 2 == 0 else -1, 2))
        rings.finish()

    @pl.when(core == 1)
    def _():
        rings = Sender(ring_send, ring_recv)
        on_z = [
            Ring(
                rings, depth, z, here.along_z,
                lambda zz, t=t: slab(zz, here.x_at(t), core),
                (4, 3) if t % 2 == 0 else (3, 4),
            )
            for t in range(across)
        ]
        for t in range(across):
            on_z[t].launch()
        for t in range(across):
            to_partner(0, t)
        for h in range(1, 5):
            for t in range(across):
                for sign in (1, -1):
                    if on_z[t].has(sign, h):
                        to_partner(on_z[t].take(sign, h), t)
        rings.finish()

    for s in range(depth):
        for t in range(across):
            slot = slab(here.z_at(s), here.x_at(t), 1 - core)
            made = pairs.copy(s * across + t, slot, slot, here.partner)
            made.wait_recv()
            made.wait_send()
    for s in (2, 1, 3):
        source = here.y_at(-s)
        ys.arrived(s, hx_out.at[source, target_rows(y), :], here.along_y(source))
    ys.finish()
    own.wait()


def spread_hidden(hidden, wb, sizes):
    depth, across, down = sizes
    tokens, lanes = hidden.shape
    dma = pltpu.SemaphoreType.DMA
    anywhere = pl.BlockSpec(memory_space=pl.ANY)
    return pl.pallas_call(
        lambda *refs: spread_kernel(sizes, *refs),
        out_shape=(
            jax.ShapeDtypeStruct((down, tokens // down + 2 * EDGE, lanes), hidden.dtype),
            jax.ShapeDtypeStruct(wb.shape, wb.dtype),
        ),
        in_specs=[in_vmem(), anywhere],
        out_specs=(in_vmem(), anywhere),
        input_output_aliases={1: 1},
        scratch_shapes=[
            dma((SITES,)), dma((SITES,)),
            dma((depth * across,)), dma((depth * across,)),
            dma((4,)), dma((4,)),
            dma((1,)),
        ],
        compiler_params=pltpu.CompilerParams(
            collective_id=4, has_side_effects=True, vmem_limit_bytes=16 << 20
        ),
        cost_estimate=pl.CostEstimate(flops=10_000_000_000, bytes_accessed=40_000_000, transcendentals=0),
        name="spread_hidden",
    )(hidden, wb)


def embed_kernel(taps, length, lengths_ref, hx_ref, wb_hbm, emb_ref, out_ref, wb_ref, wide, cols, sems):
    down, rows, lanes = hx_ref.shape
    arriving = [pltpu.make_async_copy(wb_hbm.at[c], wb_ref.at[c], sems.at[c]) for c in range(down)]
    for copy in arriving:
        copy.start()
    views, tokens, width = emb_ref.shape
    odd = lax.rem(lax.axis_index(Y), 2)
    row = lax.broadcasted_iota(jnp.int32, (rows, lanes), 0)
    inside = (row >= EDGE * (1 - odd)) & (row < rows - EDGE * odd)
    per = lanes // views
    for c in range(down):
        wide[...] = jnp.where(inside, hx_ref[c].astype(jnp.float32), 0.0)
        arriving[c].wait()
        for v in range(views):
            pieces = []
            for k in range(taps):
                first = EDGE + 2 * (k - taps // 2)
                pieces.append(wide[first : first + tokens, v * per : (v + 1) * per])
            cols[...] = jnp.concatenate(pieces, axis=1).astype(jnp.bfloat16)
            part = lax.dot_general(
                cols[...], wb_ref[c], (((1,), (1,)), ((), ())), preferred_element_type=jnp.float32
            )
            if c == 0:
                emb_ref[v] = part
            else:
                emb_ref[v] += part
    moments_into(emb_ref, alive_column(lengths_ref, tokens, length), out_ref)


def embedding(lengths, hx, wb, planes, taps, length):
    down, rows, lanes = hx.shape
    width = wb.shape[1]
    tokens = rows - 2 * EDGE
    parts = share_rows(width, planes) * planes
    return pl.pallas_call(
        lambda *refs: embed_kernel(taps, length, *refs),
        out_shape=(
            jax.ShapeDtypeStruct((2, tokens, width), jnp.float32),
            jax.ShapeDtypeStruct((2, parts, BLOCK), jnp.float32),
        ),
        in_specs=[in_smem(), in_vmem(), pl.BlockSpec(memory_space=pl.ANY)],
        out_specs=(in_vmem(), in_vmem()),
        scratch_shapes=[
            pltpu.VMEM(wb.shape, wb.dtype),
            pltpu.VMEM((rows, lanes), jnp.float32),
            pltpu.VMEM((tokens, wb.shape[2]), jnp.bfloat16),
            pltpu.SemaphoreType.DMA((down,)),
        ],
        compiler_params=pltpu.CompilerParams(vmem_limit_bytes=40 << 20),
        name="embedding",
    )(lengths, hx, wb)


def shards(monomers, keep_mask, lengths, norm_gain, weight_a, weight_b):
    tokens = monomers.shape[0]
    length = tokens // lengths.shape[0]
    taps = weight_a.shape[0]
    sizes = (lax.axis_size(Z), lax.axis_size(X), lax.axis_size(Y))
    xt, wa, wb = gathered_inputs(monomers.T, weight_a, weight_b.transpose(0, 2, 1), sizes)
    hidden = first_conv(
        lengths,
        xt.reshape(-1, tokens),
        wa.reshape(-1, *wa.shape[3:]),
        norm_gain.reshape(-1, BLOCK),
        keep_mask,
        taps,
    )
    hx, wb = spread_hidden(hidden, wb, sizes)
    embedded, parts = embedding(lengths, hx, wb, sizes[1] * sizes[2], taps, length)
    total = total_moments(parts, sizes)
    inverse = inverse_factor(total, embedded.shape[2])
    other = from_partner(inverse)
    return whitened_rows(lengths, embedded, inverse, other, length)


def solution(mesh):
    torus = Mesh(
        mesh.devices.reshape(8, 4, 2, mesh.shape["chan"]), ("batch_0", "batch_1", "batch_2", "chan")
    )
    in_specs = (
        P(BATCH, "chan"),
        P(None, BATCH),
        P(BATCH),
        P(),
        P(None, BATCH, "chan"),
        P(None, "chan", BATCH),
    )
    out_specs = (P(None, BATCH_CHAN, None), P(BATCH_CHAN))
    return jax.shard_map(
        shards, mesh=torus, in_specs=in_specs, out_specs=out_specs, check_vma=False
    )
```

```python
import jax
import jax.numpy as jnp
from jax import lax
from jax.experimental import pallas as pl
from jax.experimental.pallas import tpu as pltpu
from jax.sharding import Mesh
from jax.sharding import PartitionSpec as P

BATCH = ("batch_0", "batch_1", "batch_2")
BATCH_CHAN = ("batch_0", "batch_1", "batch_2", "chan")


EPS_NORM = 1e-05
EPS_COV = 0.0001
HI = lax.Precision.HIGHEST
MESH_IDS = pl.DeviceIdType.MESH
Z, X, CORE, Y = "batch_0", "batch_1", "batch_2", "chan"
AXES = (Z, X, CORE, Y)
BLOCK = 128
GROUP = 8
LOWEST = -3.0e38


def dot_of(a, b, dims, precision=HI):
    return lax.dot_general(
        a, b, (dims, ((), ())), precision=precision, preferred_element_type=jnp.float32
    )


def in_vmem():
    return pl.BlockSpec(memory_space=pltpu.VMEM)


def block_pairs(width):
    return [(i, k) for i in range(width // BLOCK) for k in range(i + 1)]


def share_rows(width, planes):
    rows = len(block_pairs(width)) * BLOCK
    return -(-rows // (planes * GROUP)) * GROUP


def alive_column(lengths_ref, tokens, length):
    start = lax.axis_index(Y) * tokens
    limit = lengths_ref[start // length] - lax.rem(start, length)
    return jnp.where(lax.broadcasted_iota(jnp.int32, (tokens, 1), 0) < limit, 1.0, 0.0)


def in_smem():
    return pl.BlockSpec(memory_space=pltpu.SMEM)


def moments_into(emb_ref, alive, out_ref):
    views, tokens, width = emb_ref.shape
    pairs = block_pairs(width)
    at = len(pairs) * BLOCK
    half = BLOCK // 2
    for v in range(views):
        masked = emb_ref[v] * alive
        for i in range(width // BLOCK):
            wide = (i + 1) * BLOCK
            strip = dot_of(
                masked[:, i * BLOCK : wide], masked[:, :wide], ((0,), (0,))
            )
            for k in range(i + 1):
                b = pairs.index((i, k))
                out_ref[v, b * BLOCK : (b + 1) * BLOCK, :] = strip[:, k * BLOCK : (k + 1) * BLOCK]
        if out_ref.shape[1] > at:
            out_ref[v, at:, :] = jnp.zeros((out_ref.shape[1] - at, BLOCK), jnp.float32)
        sums = jnp.sum(masked, axis=0, keepdims=True)
        spare = [sums[:, k * half : (k + 1) * half] for k in range(width // half)]
        spare.append(jnp.broadcast_to(jnp.sum(alive, axis=0, keepdims=True), (1, half)))
        out_ref[v, 0 : len(spare), half:] = jnp.concatenate(spare, axis=0)


def total_kernel(sizes, parts, part_ref, out_ref, pair_in, mine, plane_in, share, line_in, total, *sems):
    depth, across, down = sizes
    planes = across * down
    rows = share.shape[0]
    z, x = lax.axis_index(Z), lax.axis_index(X)
    core, y = lax.axis_index(CORE), lax.axis_index(Y)
    me = x * down + y
    partner = 1 - core
    pair_send, pair_recv, plane_send, plane_recv, line_send, line_recv, back_send, back_recv = sems

    def in_plane(step):
        other = lax.rem(me + step, planes)
        return other, (z, other // down, core, lax.rem(other, down))

    def in_line(step):
        other = lax.rem(z + step, depth)
        return other, (other, x, core, y)

    barrier = pltpu.get_barrier_semaphore()
    pl.semaphore_signal(barrier, inc=1, device_id=(z, x, partner, y), device_id_type=MESH_IDS)
    for step in range(1, planes):
        pl.semaphore_signal(barrier, inc=1, device_id=in_plane(step)[1], device_id_type=MESH_IDS)
    for step in range(1, depth):
        pl.semaphore_signal(barrier, inc=1, device_id=in_line(step)[1], device_id_type=MESH_IDS)
    pl.semaphore_wait(barrier, 1 + planes - 1 + depth - 1)

    def sent(src, dst, send, recv, device):
        copy = pltpu.make_async_remote_copy(
            src_ref=src, dst_ref=dst, send_sem=send, recv_sem=recv,
            device_id=device, device_id_type=MESH_IDS,
        )
        copy.start()
        return copy

    starts = [sum(parts[:i]) for i in range(len(parts))]

    def within(i):
        return pl.ds(starts[i], parts[i])

    swaps = [
        sent(
            part_ref.at[partner, :, within(i)], pair_in.at[:, within(i)],
            pair_send.at[i], pair_recv.at[i], (z, x, partner, y),
        )
        for i in range(len(parts))
    ]

    def summed(buffer, own, count, i):
        acc = None
        for source in range(count):
            piece = buffer[lax.rem(own - source + count, count), within(i)]
            acc = piece if acc is None else acc + piece
        return acc

    spread, lines, back = {}, {}, {}
    for i in range(len(parts)):
        swaps[i].wait_recv()
        mine[:, within(i)] = part_ref[core, :, within(i)] + pair_in[:, within(i)]
        for step in range(1, planes):
            other, device = in_plane(step)
            spread[i, step] = sent(
                mine.at[other, within(i)], plane_in.at[step, within(i)],
                plane_send.at[i, step], plane_recv.at[i, step], device,
            )

    def to_line(i):
        for step in range(1, planes):
            spread[i, step].wait_recv()
        plane_in[0, within(i)] = mine[me, within(i)]
        share[within(i)] = summed(plane_in, me, planes, i)
        for step in range(1, depth):
            lines[i, step] = sent(
                share.at[within(i)], line_in.at[step, within(i)],
                line_send.at[i, step], line_recv.at[i, step], in_line(step)[1],
            )

    def to_plane(i):
        for step in range(1, depth):
            lines[i, step].wait_recv()
        line_in[0, within(i)] = share[within(i)]
        total[within(i)] = summed(line_in, z, depth, i)
        for step in range(1, planes):
            back[i, step] = sent(
                total.at[within(i)], out_ref.at[me, within(i)],
                back_send.at[i, step], back_recv.at[i, step], in_plane(step)[1],
            )
        out_ref[me, within(i)] = total[within(i)]

    lag = 2
    for i in range(len(parts) + lag):
        if i < len(parts):
            to_line(i)
        if i >= lag:
            to_plane(i - lag)
    for copy in back.values():
        copy.wait_recv()
    for copy in swaps:
        copy.wait_send()
    for group in (spread, lines, back):
        for copy in group.values():
            copy.wait_send()


def total_moments(parts, mesh_sizes):
    depth, across, down = mesh_sizes
    planes = across * down
    _, all_rows, lanes = parts.shape
    rows = all_rows // planes
    tiles = rows // GROUP
    pieces = tuple(GROUP * (tiles // 4 + (1 if i < tiles % 4 else 0)) for i in range(4))
    dma = pltpu.SemaphoreType.DMA
    vm = lambda *shape: pltpu.VMEM(shape, jnp.float32)
    return pl.pallas_call(
        lambda *refs: total_kernel(mesh_sizes, pieces, *refs),
        out_shape=jax.ShapeDtypeStruct((planes, rows, lanes), jnp.float32),
        in_specs=[in_vmem()],
        out_specs=in_vmem(),
        scratch_shapes=[
            vm(planes, rows, lanes),
            vm(planes, rows, lanes),
            vm(planes, rows, lanes),
            vm(rows, lanes),
            vm(depth, rows, lanes),
            vm(rows, lanes),
            dma((4,)), dma((4,)),
            dma((4, planes)), dma((4, planes)),
            dma((4, depth)), dma((4, depth)),
            dma((4, planes)), dma((4, planes)),
        ],
        compiler_params=pltpu.CompilerParams(
            collective_id=1, has_side_effects=True, vmem_limit_bytes=32 << 20
        ),
        name="total_moments",
    )(parts.reshape(2, planes, rows, lanes)).reshape(all_rows, lanes)


def splat_row(v, a):
    return jnp.broadcast_to(v[a : a + 1, :], (GROUP, BLOCK))


def splat_lane(v, j):
    return jnp.broadcast_to(v[:, j : j + 1], (GROUP, BLOCK))


def base_inverse(load, store):
    count = BLOCK // GROUP
    groups = [load(g) for g in range(count)]
    lane = lax.broadcasted_iota(jnp.int32, (GROUP, BLOCK), 1)
    sub = lax.broadcasted_iota(jnp.int32, (GROUP, BLOCK), 0)
    steps = range(GROUP)
    twos = range(GROUP // 2)
    for p in range(count):
        j = GROUP * p
        v = groups[p]
        cols = [jnp.maximum(splat_lane(v, j + a), LOWEST) for a in steps]
        e = [[splat_row(cols[a], b) if b >= a else None for a in steps] for b in steps]
        panel = (lane >= j) & (lane < j + GROUP)
        rows = [
            jnp.where(panel, jnp.where(lane == j + a, 1.0, 0.0), splat_row(v, a)) for a in steps
        ]
        f, inv = {}, []
        for t in twos:
            m, n = 2 * t, 2 * t + 1
            e00, e10, e11 = e[m][m], e[n][m], e[n][n]
            det = e00 * e11 - e10 * e10
            rd = 1.0 / det
            inv.append(rd)
            for b in range(n + 1, GROUP):
                f0 = (e11 * e[b][m] - e10 * e[b][n]) * rd
                f1 = (e00 * e[b][n] - e10 * e[b][m]) * rd
                f[b, t] = (f0, f1)
                for c in range(n + 1, b + 1):
                    e[b][c] = e[b][c] - (f0 * e[c][m] + f1 * e[c][n])
                rows[b] = rows[b] - (f0 * rows[m] + f1 * rows[n])
        out = None
        q = [None] * GROUP
        for t in reversed(twos):
            m, n = 2 * t, 2 * t + 1
            e00, e10, e11, rd = e[m][m], e[n][m], e[n][n], inv[t]
            q0 = (e11 * rows[m] - e10 * rows[n]) * rd
            q1 = (e00 * rows[n] - e10 * rows[m]) * rd
            for b in reversed(range(n + 1, GROUP)):
                q0 = q0 - f[b, t][0] * q[b]
                q1 = q1 - f[b, t][1] * q[b]
            q[m], q[n] = q0, q1
        for g in range(p + 1, count):
            x = groups[g]
            terms = [splat_lane(x, j + a) * q[a] for a in steps]
            pairs = [terms[2 * t] + terms[2 * t + 1] for t in twos]
            late = jnp.where(panel, 0.0, x) - ((pairs[3] + pairs[2]) + pairs[1])
            groups[g] = late - pairs[0]
        for t in twos:
            m, n = 2 * t, 2 * t + 1
            e00, e10, e11 = e[m][m], e[n][m], e[n][n]
            ratio = e10 / e00
            first = rows[m] * lax.rsqrt(e00)
            second = (rows[n] - ratio * rows[m]) * lax.rsqrt(e11 - ratio * e10)
            out = first if out is None else jnp.where(sub == m, first, out)
            out = jnp.where(sub == n, second, out)
        store(p, jnp.where(lane < j + GROUP, out, 0.0))


def factor_kernel(total_ref, out_ref, work, m_ref):
    width = work.shape[1]
    blocks = width // BLOCK
    pairs = block_pairs(width)
    half = BLOCK // 2
    spare = total_ref[0 : 2 * GROUP, half:]
    last = width // half
    count = spare[last : last + 1, 0:1]
    center = jnp.concatenate([spare[k : k + 1, :] for k in range(last)], axis=1) / count
    sub = lax.broadcasted_iota(jnp.int32, (GROUP, width), 0)
    center8 = jnp.where(sub == 0, jnp.broadcast_to(center, (GROUP, width)), 0.0)
    high = center.astype(jnp.bfloat16).astype(jnp.float32)
    middle = (center - high).astype(jnp.bfloat16).astype(jnp.float32)
    low = center - high - middle

    def stacked(parts):
        rows = jnp.zeros((GROUP, width), jnp.float32)
        for i, part in enumerate(parts):
            rows = jnp.where(sub == i, jnp.broadcast_to(part, (GROUP, width)), rows)
        return rows.astype(jnp.bfloat16)

    one_side = stacked((high, high, middle, high, low, middle, middle, low))
    other_side = stacked((high, middle, high, low, high, middle, low, middle))
    eye = lax.broadcasted_iota(jnp.int32, (BLOCK, BLOCK), 0) == lax.broadcasted_iota(
        jnp.int32, (BLOCK, BLOCK), 1
    )
    lower = lax.broadcasted_iota(jnp.int32, (BLOCK, BLOCK), 0) >= lax.broadcasted_iota(
        jnp.int32, (BLOCK, BLOCK), 1
    )
    for b, (i, k) in enumerate(pairs):
        outer = dot_of(
            one_side[:, i * BLOCK : (i + 1) * BLOCK],
            other_side[:, k * BLOCK : (k + 1) * BLOCK],
            ((0,), (0,)),
            lax.Precision.DEFAULT,
        )
        raw = total_ref[b * BLOCK : (b + 1) * BLOCK, :]
        if b == 0:
            raw = jnp.where(lower, raw, raw.T)
        block = raw / count - outer
        if i == k:
            block = block + jnp.where(eye, EPS_COV, 0.0)
        work[i * BLOCK : (i + 1) * BLOCK, k * BLOCK : (k + 1) * BLOCK] = block
        if i != k:
            work[k * BLOCK : (k + 1) * BLOCK, i * BLOCK : (i + 1) * BLOCK] = block.T
    strip_block = lax.broadcasted_iota(jnp.int32, (BLOCK, width), 1) // BLOCK
    strip_eye = jnp.where(
        lax.broadcasted_iota(jnp.int32, (BLOCK, width), 1) % BLOCK
        == lax.broadcasted_iota(jnp.int32, (BLOCK, width), 0),
        1.0,
        0.0,
    )

    def step(k, _):
        here = pl.multiple_of(k * BLOCK, BLOCK)

        def load(g):
            return work[pl.ds(pl.multiple_of(here + GROUP * g, GROUP), GROUP), pl.ds(here, BLOCK)]

        def store(g, val):
            m_ref[GROUP * g : GROUP * (g + 1), :] = val

        base_inverse(load, store)
        m = m_ref[...]
        row = jnp.where(strip_block == k, strip_eye, work[pl.ds(here, BLOCK), :])
        across = dot_of(m, row, ((1,), (0,)))
        for done in range(blocks - 1):

            @pl.when(k == done)
            def _():
                first = (done + 1) * BLOCK
                col_block = lax.broadcasted_iota(jnp.int32, (width - first, width), 1) // BLOCK
                left = dot_of(work[first:, done * BLOCK : first], m, ((1,), (1,)))
                kept = jnp.where(col_block == done, 0.0, work[first:, :])
                work[first:, :] = kept - dot_of(left, across, ((1,), (0,)))

        work[pl.ds(here, BLOCK), :] = jnp.where(strip_block <= k, across, 0.0)
        return 0

    lax.fori_loop(0, blocks, step, 0)
    out_ref[:width, :] = work[...]
    out_ref[width:, :] = center8


def inverse_factor(total, width):
    return pl.pallas_call(
        factor_kernel,
        out_shape=jax.ShapeDtypeStruct((width + GROUP, width), jnp.float32),
        in_specs=[in_vmem()],
        out_specs=in_vmem(),
        scratch_shapes=[
            pltpu.VMEM((width, width), jnp.float32),
            pltpu.VMEM((BLOCK, BLOCK), jnp.float32),
        ],
        compiler_params=pltpu.CompilerParams(vmem_limit_bytes=32 << 20),
        name="inverse_factor",
    )(total)


def swap_kernel(own_ref, out_ref, send, recv):
    z, x = lax.axis_index(Z), lax.axis_index(X)
    core, y = lax.axis_index(CORE), lax.axis_index(Y)
    other = (z, x, 1 - core, y)
    barrier = pltpu.get_barrier_semaphore()
    pl.semaphore_signal(barrier, inc=1, device_id=other, device_id_type=MESH_IDS)
    pl.semaphore_wait(barrier, 1)
    copy = pltpu.make_async_remote_copy(
        src_ref=own_ref, dst_ref=out_ref, send_sem=send, recv_sem=recv,
        device_id=other, device_id_type=MESH_IDS,
    )
    copy.start()
    copy.wait()


def from_partner(own):
    return pl.pallas_call(
        swap_kernel,
        out_shape=jax.ShapeDtypeStruct(own.shape, own.dtype),
        in_specs=[in_vmem()],
        out_specs=in_vmem(),
        scratch_shapes=[pltpu.SemaphoreType.DMA, pltpu.SemaphoreType.DMA],
        compiler_params=pltpu.CompilerParams(
            collective_id=2, has_side_effects=True, vmem_limit_bytes=16 << 20
        ),
        name="from_partner",
    )(own)


def whiten_kernel(length, lengths_ref, emb_ref, own_ref, other_ref, out_ref, gap_ref):
    views, tokens, width = emb_ref.shape
    core = lax.axis_index(CORE)
    alive = alive_column(lengths_ref, tokens, length)
    for ref, v in ((own_ref, core), (other_ref, 1 - core)):
        centered = (emb_ref[v] - ref[width : width + 1, :]) * alive
        part = 2 * BLOCK
        for first in range(0, width, part):
            last = first + part
            out_ref[v, :, first:last] = dot_of(centered[:, :last], ref[first:last, :last], ((1,), (1,)))
    gap = out_ref[0] - out_ref[1]
    ones = jnp.ones((GROUP, width), jnp.float32)
    sums = dot_of(ones, gap * gap, ((1,), (1,))) / width
    for k in range(tokens // BLOCK):
        gap_ref[k : k + 1, :] = sums[0:1, k * BLOCK : (k + 1) * BLOCK]


def whitened_rows(lengths, embedded, own, other, length):
    views, tokens, width = embedded.shape
    whitened, gap = pl.pallas_call(
        lambda *refs: whiten_kernel(length, *refs),
        out_shape=(
            jax.ShapeDtypeStruct(embedded.shape, jnp.float32),
            jax.ShapeDtypeStruct((tokens // BLOCK, BLOCK), jnp.float32),
        ),
        in_specs=[in_smem()] + [in_vmem()] * 3,
        out_specs=(in_vmem(), in_vmem()),
        compiler_params=pltpu.CompilerParams(vmem_limit_bytes=32 << 20),
        name="whitened_rows",
    )(lengths, embedded, own, other)
    return whitened, gap.reshape(tokens)


class Sender:
    def __init__(self, send_sems, recv_sems):
        self.send_sems, self.recv_sems = send_sems, recv_sems
        self.started, self.used = [], 0

    def site(self):
        self.used += 1
        return self.used - 1

    def copy(self, site, src, dst, device):
        return pltpu.make_async_remote_copy(
            src_ref=src, dst_ref=dst,
            send_sem=self.send_sems.at[site], recv_sem=self.recv_sems.at[site],
            device_id=device, device_id_type=MESH_IDS,
        )

    def send(self, site, src, dst, device):
        made = self.copy(site, src, dst, device)
        made.start()
        self.started.append(made)

    def arrived(self, site, dst, device):
        self.copy(site, dst, dst, device).wait_recv()

    def finish(self):
        for made in self.started:
            made.wait_send()


class Ring:
    def __init__(self, sender, size, pos, device_at, slot_at, hops, own=None):
        self.sender, self.size, self.pos = sender, size, pos
        self.device_at, self.slot_at = device_at, slot_at
        self.hops = {1: hops[0], -1: hops[1]}
        self.own = own
        self.sites = {
            (sign, h): sender.site() for sign in (1, -1) for h in range(1, self.hops[sign] + 1)
        }

    def at(self, offset):
        return lax.rem(self.pos + offset + 2 * self.size, self.size)

    def pass_on(self, sign, h):
        source = self.at(-sign * (h - 1))
        slot = self.slot_at(source)
        src = self.own if h == 1 and self.own is not None else slot
        self.sender.send(self.sites[sign, h], src, slot, self.device_at(self.at(sign)))

    def launch(self):
        for sign in (1, -1):
            self.pass_on(sign, 1)

    def has(self, sign, h):
        return h <= self.hops[sign]

    def take(self, sign, h):
        slot = self.slot_at(self.at(-sign * h))
        self.sender.arrived(self.sites[sign, h], slot, self.device_at(self.at(-sign)))
        if h < self.hops[sign]:
            self.pass_on(sign, h + 1)
        return (sign * h) % self.size


class Place:
    def __init__(self, sizes):
        self.depth, self.across, self.down = sizes
        self.z, self.x = lax.axis_index(Z), lax.axis_index(X)
        self.core, self.y = lax.axis_index(CORE), lax.axis_index(Y)
        self.partner = (self.z, self.x, 1 - self.core, self.y)

    def z_at(self, s):
        return lax.rem(self.z - s + 2 * self.depth, self.depth)

    def x_at(self, t):
        return lax.rem(self.x - t + 2 * self.across, self.across)

    def y_at(self, s):
        return lax.rem(self.y + s + 2 * self.down, self.down)

    def along_z(self, zz):
        return (zz, self.x, self.core, self.y)

    def along_x(self, xx):
        return (self.z, xx, self.core, self.y)

    def along_y(self, yy):
        return (self.z, self.x, self.core, yy)

    def greet(self):
        self.greeted(self.greeting())

    def greeting(self):
        peers = [self.along_z(self.z_at(s)) for s in (1, -1)]
        peers += [self.along_x(self.x_at(s)) for s in (1, -1)]
        peers += [self.along_y(self.y_at(s)) for s in range(1, self.down)]
        peers += [self.partner]
        barrier = pltpu.get_barrier_semaphore()
        for peer in peers:
            pl.semaphore_signal(barrier, inc=1, device_id=peer, device_id_type=MESH_IDS)
        return len(peers)

    def greeted(self, count):
        pl.semaphore_wait(pltpu.get_barrier_semaphore(), count)


SITES = 64
FEW = 4


def rows_of_slab(zz, xx, core, across):
    return pl.ds(pl.multiple_of(((zz * across + xx) * 2 + core) * GROUP, GROUP), GROUP)


def gather_kernel(
    sizes, xt_ref, hbm_a, hbm_b, xt_out, wa_out, wb_out, raw_a, raw_b, wa_ref, wb_ref,
    ring_send, ring_recv, pair_send, pair_recv, y_send, y_recv, local,
):
    here = Place(sizes)
    depth, across, down = sizes
    z, x, core, y = here.z, here.x, here.core, here.y
    greeted = here.greeting()
    load_a = pltpu.make_async_copy(hbm_a, raw_a, local.at[3])
    load_b = pltpu.make_async_copy(hbm_b, raw_b, local.at[4])
    load_a.start()
    load_b.start()
    load_a.wait()
    load_b.wait()
    rows_a = jnp.concatenate([raw_a[k] for k in range(raw_a.shape[0])], axis=1)
    for i in range(wa_ref.shape[0]):
        wa_ref[i] = rows_a[i * FEW : (i + 1) * FEW, :]
    wb_ref[...] = jnp.concatenate([raw_b[k] for k in range(raw_b.shape[0])], axis=1)
    here.greeted(greeted)
    half = xt_ref.shape[0] // 2

    def slab(zz, xx, cc):
        return wb_out.at[:, rows_of_slab(zz, xx, cc, across), :]

    def own_part(yy):
        return wb_out.at[yy, rows_of_slab(z, x, core, across), :]

    own = [
        pltpu.make_async_copy(wb_ref, own_part(y), local.at[0]),
        pltpu.make_async_copy(wa_ref, wa_out.at[z, x, core], local.at[1]),
        pltpu.make_async_copy(xt_ref, xt_out.at[y], local.at[2]),
    ]
    for copy in own:
        copy.start()

    ys = Sender(y_send, y_recv)
    wb_sites = {s: ys.site() for s in range(1, down)}
    for s in range(1, down):
        ys.send(wb_sites[s], wb_ref, own_part(y), here.along_y(here.y_at(s)))

    def piece(yy, p):
        return xt_out.at[yy, p * half : (p + 1) * half, :]

    xt_sites = {(sign, p, h): ys.site() for sign in (1, -1) for p in (0, 1) for h in (1, 2)}
    for first in (0, 1):
        for sign in (1, -1):
            p = first if sign == 1 else 1 - first
            ys.send(
                xt_sites[sign, p, 1], xt_ref.at[p * half : (p + 1) * half, :], piece(y, p),
                here.along_y(here.y_at(sign)),
            )

    def first_pieces():
        for sign, p in ((1, 0), (-1, 1)):
            source = here.y_at(-sign)
            ys.arrived(xt_sites[sign, p, 1], piece(source, p), here.along_y(source))
            ys.send(xt_sites[sign, p, 2], piece(source, p), piece(source, p), here.along_y(here.y_at(sign)))

    def last_pieces():
        for sign, p in ((1, 1), (-1, 0)):
            source = here.y_at(-sign)
            ys.arrived(xt_sites[sign, p, 1], piece(source, p), here.along_y(source))
        for sign, p in ((1, 0), (-1, 1)):
            ys.arrived(xt_sites[sign, p, 2], piece(here.y_at(2), p), here.along_y(here.y_at(-sign)))

    def slabs_ready():
        for s in range(1, down):
            source = here.y_at(-s)
            ys.arrived(wb_sites[s], own_part(source), here.along_y(source))
        own[0].wait()

    pairs = Sender(pair_send, pair_recv)

    def to_partner(s, t):
        slot = wa_out.at[here.z_at(s), here.x_at(t), core]
        src = wa_ref if s == 0 and t == 0 else slot
        pairs.send(s * across + t, src, slot, here.partner)

    @pl.when(core == 0)
    def _():
        rings = Sender(ring_send, ring_recv)
        down_z = Ring(rings, depth, z, here.along_z, lambda zz: wa_out.at[zz, x, core], (4, 3), wa_ref)
        slabs_z = Ring(rings, depth, z, here.along_z, lambda zz: slab(zz, x, core), (3, 4))
        on_x = [
            Ring(
                rings, across, x, here.along_x,
                lambda xx, s=s: wa_out.at[here.z_at(s), xx, core],
                (2, 1) if s % 2 == 0 else (1, 2),
                wa_ref if s == 0 else None,
            )
            for s in range(depth)
        ]
        down_z.launch()
        on_x[0].launch()
        to_partner(0, 0)
        slabs_ready()
        slabs_z.launch()
        waiting = [0]
        for h in range(1, 5):
            arrived = []
            for sign in (1, -1):
                if down_z.has(sign, h):
                    s = down_z.take(sign, h)
                    on_x[s].launch()
                    to_partner(s, 0)
                    arrived.append(s)
            for sign in (1, -1):
                if slabs_z.has(sign, h):
                    slabs_z.take(sign, h)
            for s in waiting:
                for sign in (1, -1):
                    to_partner(s, on_x[s].take(sign, 1))
            waiting = arrived
            if h == 3:
                first_pieces()
        for s in waiting:
            for sign in (1, -1):
                to_partner(s, on_x[s].take(sign, 1))
        for s in [0, 1, 7, 2, 6, 3, 5, 4]:
            to_partner(s, on_x[s].take(1 if s % 2 == 0 else -1, 2))
        rings.finish()

    @pl.when(core == 1)
    def _():
        rings = Sender(ring_send, ring_recv)
        own_x = Ring(rings, across, x, here.along_x, lambda xx: wa_out.at[z, xx, core], (2, 1), wa_ref)
        slabs_x = Ring(rings, across, x, here.along_x, lambda xx: slab(z, xx, core), (1, 2))
        on_z = [
            Ring(
                rings, depth, z, here.along_z,
                lambda zz, t=t: wa_out.at[zz, here.x_at(t), core],
                (4, 3) if t % 2 == 0 else (3, 4),
                wa_ref if t == 0 else None,
            )
            for t in range(across)
        ]
        own_x.launch()
        on_z[0].launch()
        to_partner(0, 0)
        slabs_ready()
        slabs_x.launch()
        for sign, h in ((1, 1), (-1, 1), (1, 2)):
            t = own_x.take(sign, h)
            on_z[t].launch()
            to_partner(0, t)
        for sign, h in ((1, 1), (-1, 1), (-1, 2)):
            slabs_x.take(sign, h)
        for h in range(1, 5):
            for t in (0, 1, 3, 2):
                for sign in (1, -1):
                    if on_z[t].has(sign, h):
                        to_partner(on_z[t].take(sign, h), t)
            if h == 1:
                first_pieces()
        rings.finish()

    last_pieces()
    for s in range(depth):
        for t in range(across):
            slot = wa_out.at[here.z_at(s), here.x_at(t), 1 - core]
            made = pairs.copy(s * across + t, slot, slot, here.partner)
            made.wait_recv()
            made.wait_send()
    ys_wait = ys.started
    for made in ys_wait[: down - 1 + 4]:
        made.wait_send()
    for sign, p in ((1, 0), (-1, 1)):
        ys.copy(
            xt_sites[sign, p, 2], piece(here.y_at(-sign), p), piece(here.y_at(-sign), p),
            here.along_y(here.y_at(sign)),
        ).wait_send()
    own[1].wait()
    own[2].wait()


def gathered_inputs(xt, wa, wb, sizes):
    depth, across, down = sizes
    dma = pltpu.SemaphoreType.DMA
    anywhere = pl.BlockSpec(memory_space=pl.ANY)
    taps, rows_a, width = wa.shape
    rows_b = wb.shape[1]
    return pl.pallas_call(
        lambda *refs: gather_kernel(sizes, *refs),
        out_shape=(
            jax.ShapeDtypeStruct((down, *xt.shape), xt.dtype),
            jax.ShapeDtypeStruct((depth, across, 2, rows_a // FEW, FEW, taps * width), wa.dtype),
            jax.ShapeDtypeStruct((down, depth * across * 2 * rows_b, taps * width), wb.dtype),
        ),
        in_specs=[anywhere] * 3,
        out_specs=(in_vmem(), anywhere, anywhere),
        scratch_shapes=[
            pltpu.VMEM(wa.shape, wa.dtype),
            pltpu.VMEM(wb.shape, wb.dtype),
            pltpu.VMEM((rows_a // FEW, FEW, taps * width), wa.dtype),
            pltpu.VMEM((rows_b, taps * width), wb.dtype),
            dma((SITES,)), dma((SITES,)),
            dma((depth * across,)), dma((depth * across,)),
            dma((16,)), dma((16,)),
            dma((5,)),
        ],
        compiler_params=pltpu.CompilerParams(
            collective_id=3, has_side_effects=True, vmem_limit_bytes=16 << 20
        ),
        cost_estimate=pl.CostEstimate(flops=20_000_000_000, bytes_accessed=80_000_000, transcendentals=0),
        name="gathered_inputs",
    )(xt, wa, wb)


def gate(values):
    return 0.5 * values * (1.0 + jnp.tanh(0.7978845608 * (values + 0.044715 * values * values * values)))


PAD = 8
ROWS = 128
EDGE = 16


def conv_kernel(
    sizes, lengths_ref, xt_ref, wa_hbm, gain_hbm, keep_hbm, out_ref,
    wa_ref, gain_ref, keep_ref, n_ref, w_ref, p_ref, cols, sems,
):
    sequences, length, taps = sizes
    channels, tokens = xt_ref.shape
    chunks, few_count, _, lanes = wa_ref.shape
    chunk_rows = few_count * FEW
    loads = 4
    each = chunks // loads
    arriving = [
        pltpu.make_async_copy(wa_hbm.at[pl.ds(i * each, each)], wa_ref.at[pl.ds(i * each, each)], sems.at[i])
        for i in range(loads)
    ]
    small = [
        pltpu.make_async_copy(gain_hbm, gain_ref, sems.at[loads]),
        pltpu.make_async_copy(keep_hbm, keep_ref, sems.at[loads + 1]),
    ]
    for copy in small + arriving:
        copy.start()
    eye = lax.broadcasted_iota(jnp.int32, (BLOCK, BLOCK), 0) == lax.broadcasted_iota(
        jnp.int32, (BLOCK, BLOCK), 1
    )
    squares = jnp.zeros((1, tokens), jnp.float32)
    for i in range(channels // BLOCK):
        part = xt_ref[i * BLOCK : (i + 1) * BLOCK, :].astype(jnp.float32)
        squares = squares + jnp.sum(part * part, axis=0, keepdims=True)
    scale = lax.rsqrt(squares / channels + EPS_NORM)
    for copy in small:
        copy.wait()
    for i in range(channels // BLOCK):
        part = xt_ref[i * BLOCK : (i + 1) * BLOCK, :].astype(jnp.float32)
        gain = jnp.sum(
            jnp.where(eye, jnp.broadcast_to(gain_ref[i : i + 1, :], (BLOCK, BLOCK)), 0.0), axis=1, keepdims=True
        )
        normed = (part * scale * gain).astype(jnp.bfloat16)
        n_ref[:, i * BLOCK : (i + 1) * BLOCK] = normed.T

    token = lax.broadcasted_iota(jnp.int32, (GROUP, tokens), 1)
    position = token % length
    limit = jnp.zeros((GROUP, tokens), jnp.int32)
    for s in range(sequences):
        limit = jnp.where(token // length == s, lengths_ref[s], limit)
    view = lax.broadcasted_iota(jnp.int32, (GROUP, tokens), 0)
    keep = jnp.where(view == 0, keep_ref[0:1, :], jnp.where(view == 1, keep_ref[1:2, :], 0))
    kept = jnp.where(position < limit, keep, 0).astype(jnp.float32)
    stacked = [jnp.zeros((GROUP, tokens), jnp.float32) for _ in range(cols.shape[0])]
    per = GROUP // 2
    for k in range(taps):
        move = k - taps // 2
        rolled = kept if move == 0 else pltpu.roll(kept, (-move) % tokens, 1)
        inside = (position + move >= 0) & (position + move < length)
        rolled = jnp.where(inside, rolled, 0.0)
        down = 2 * (k % per)
        rolled = rolled if down == 0 else pltpu.roll(rolled, down, 0)
        stacked[k // per] = jnp.where(view // 2 == k % per, rolled, stacked[k // per])
    for i in range(cols.shape[0]):
        cols[i] = stacked[i].T

    group = 4

    def relay(q, _):
        pieces = [
            wa_ref[q * group + i, r].astype(jnp.float32) for i in range(group) for r in range(few_count)
        ]
        at = pl.multiple_of(q * group * chunk_rows, group * chunk_rows)
        w_ref[pl.ds(at, group * chunk_rows), :] = jnp.concatenate(pieces, axis=0).astype(jnp.bfloat16)
        return 0

    for i in range(loads):
        arriving[i].wait()
        lax.fori_loop(i * each // group, (i + 1) * each // group, relay, 0)

    width = lanes // taps
    p_ref[0:PAD, :] = jnp.zeros((PAD, lanes), jnp.float32)
    p_ref[PAD + length :, :] = jnp.zeros((PAD, lanes), jnp.float32)

    def sequence(s, _):
        start = pl.multiple_of(s * length, length)
        for r in range(length // ROWS):
            p_ref[PAD + r * ROWS : PAD + (r + 1) * ROWS, :] = jnp.dot(
                n_ref[pl.ds(start + r * ROWS, ROWS), :], w_ref[...], preferred_element_type=jnp.float32
            )
        for r in range(length // ROWS):
            hidden = []
            for v in range(2):
                acc = None
                for k in range(taps):
                    first = PAD + r * ROWS + k - taps // 2
                    piece = p_ref[first : first + ROWS, k * width : (k + 1) * width]
                    at = 2 * (k % per) + v
                    piece = piece * cols[k // per, pl.ds(start + r * ROWS, ROWS), at : at + 1]
                    acc = piece if acc is None else acc + piece
                hidden.append(gate(acc))
            out_ref[pl.ds(start + r * ROWS, ROWS), :] = jnp.concatenate(hidden, axis=1).astype(jnp.bfloat16)
        return 0

    lax.fori_loop(0, sequences, sequence, 0)


def first_conv(lengths, xt, wa, gain, keep, taps):
    channels, tokens = xt.shape
    chunks, few_count, _, lanes = wa.shape
    chunk_rows = few_count * FEW
    sequences = lengths.shape[0]
    length = tokens // sequences
    bf, f32 = jnp.bfloat16, jnp.float32
    return pl.pallas_call(
        lambda *refs: conv_kernel((sequences, length, taps), *refs),
        out_shape=jax.ShapeDtypeStruct((tokens, 2 * lanes // taps), bf),
        in_specs=[in_smem(), in_vmem()] + [pl.BlockSpec(memory_space=pl.ANY)] * 3,
        out_specs=in_vmem(),
        scratch_shapes=[
            pltpu.VMEM(wa.shape, bf),
            pltpu.VMEM(gain.shape, f32),
            pltpu.VMEM(keep.shape, keep.dtype),
            pltpu.VMEM((tokens, channels), bf),
            pltpu.VMEM((channels, lanes), bf),
            pltpu.VMEM((length + 2 * PAD, lanes), f32),
            pltpu.VMEM((-(-taps // (GROUP // 2)), tokens, GROUP), f32),
            pltpu.SemaphoreType.DMA((6,)),
        ],
        compiler_params=pltpu.CompilerParams(vmem_limit_bytes=40 << 20),
        name="first_conv",
    )(lengths, xt, wa, gain, keep)


def spread_kernel(
    sizes, h_ref, wb_in, hx_out, wb_out, ring_send, ring_recv, pair_send, pair_recv, y_send, y_recv, local
):
    here = Place(sizes)
    depth, across, down = sizes
    z, x, core, y = here.z, here.x, here.core, here.y
    here.greet()
    rows = h_ref.shape[0] // down
    window = rows + EDGE

    def source_rows(yy):
        return pl.ds(pl.multiple_of(yy * rows - EDGE * lax.rem(yy, 2), EDGE), window)

    def target_rows(yy):
        return pl.ds(pl.multiple_of(EDGE - EDGE * lax.rem(yy, 2), EDGE), window)

    ys = Sender(y_send, y_recv)
    for s in (2, 1, 3):
        other = here.y_at(s)
        ys.send(s, h_ref.at[source_rows(other), :], hx_out.at[y, target_rows(other), :], here.along_y(other))
    own = pltpu.make_async_copy(h_ref.at[source_rows(y), :], hx_out.at[y, target_rows(y), :], local.at[0])
    own.start()

    def slab(zz, xx, cc):
        return wb_out.at[:, rows_of_slab(zz, xx, cc, across), :]

    pairs = Sender(pair_send, pair_recv)

    def to_partner(s, t):
        slot = slab(here.z_at(s), here.x_at(t), core)
        pairs.send(s * across + t, slot, slot, here.partner)

    @pl.when(core == 0)
    def _():
        rings = Sender(ring_send, ring_recv)
        on_x = [
            Ring(
                rings, across, x, here.along_x,
                lambda xx, s=s: slab(here.z_at(s), xx, core),
                (2, 1) if s % 2 == 0 else (1, 2),
            )
            for s in range(depth)
        ]
        for s in range(depth):
            on_x[s].launch()
        for s in range(depth):
            to_partner(s, 0)
        for s in range(depth):
            for sign in (1, -1):
                to_partner(s, on_x[s].take(sign, 1))
        for s in range(depth):
            to_partner(s, on_x[s].take(1 if s % 2 == 0 else -1, 2))
        rings.finish()

    @pl.when(core == 1)
    def _():
        rings = Sender(ring_send, ring_recv)
        on_z = [
            Ring(
                rings, depth, z, here.along_z,
                lambda zz, t=t: slab(zz, here.x_at(t), core),
                (4, 3) if t % 2 == 0 else (3, 4),
            )
            for t in range(across)
        ]
        for t in range(across):
            on_z[t].launch()
        for t in range(across):
            to_partner(0, t)
        for h in range(1, 5):
            for t in range(across):
                for sign in (1, -1):
                    if on_z[t].has(sign, h):
                        to_partner(on_z[t].take(sign, h), t)
        rings.finish()

    for s in range(depth):
        for t in range(across):
            slot = slab(here.z_at(s), here.x_at(t), 1 - core)
            made = pairs.copy(s * across + t, slot, slot, here.partner)
            made.wait_recv()
            made.wait_send()
    for s in (2, 1, 3):
        source = here.y_at(-s)
        ys.arrived(s, hx_out.at[source, target_rows(y), :], here.along_y(source))
    ys.finish()
    own.wait()


def spread_hidden(hidden, wb, sizes):
    depth, across, down = sizes
    tokens, lanes = hidden.shape
    dma = pltpu.SemaphoreType.DMA
    anywhere = pl.BlockSpec(memory_space=pl.ANY)
    return pl.pallas_call(
        lambda *refs: spread_kernel(sizes, *refs),
        out_shape=(
            jax.ShapeDtypeStruct((down, tokens // down + 2 * EDGE, lanes), hidden.dtype),
            jax.ShapeDtypeStruct(wb.shape, wb.dtype),
        ),
        in_specs=[in_vmem(), anywhere],
        out_specs=(in_vmem(), anywhere),
        input_output_aliases={1: 1},
        scratch_shapes=[
            dma((SITES,)), dma((SITES,)),
            dma((depth * across,)), dma((depth * across,)),
            dma((4,)), dma((4,)),
            dma((1,)),
        ],
        compiler_params=pltpu.CompilerParams(
            collective_id=4, has_side_effects=True, vmem_limit_bytes=16 << 20
        ),
        cost_estimate=pl.CostEstimate(flops=10_000_000_000, bytes_accessed=40_000_000, transcendentals=0),
        name="spread_hidden",
    )(hidden, wb)


def embed_kernel(taps, length, lengths_ref, hx_ref, wb_hbm, emb_ref, out_ref, wb_ref, wide, cols, sems):
    down, rows, lanes = hx_ref.shape
    arriving = [pltpu.make_async_copy(wb_hbm.at[c], wb_ref.at[c], sems.at[c]) for c in range(down)]
    for copy in arriving:
        copy.start()
    views, tokens, width = emb_ref.shape
    odd = lax.rem(lax.axis_index(Y), 2)
    row = lax.broadcasted_iota(jnp.int32, (rows, lanes), 0)
    inside = (row >= EDGE * (1 - odd)) & (row < rows - EDGE * odd)
    per = lanes // views
    for c in range(down):
        wide[...] = jnp.where(inside, hx_ref[c].astype(jnp.float32), 0.0)
        arriving[c].wait()
        for v in range(views):
            pieces = []
            for k in range(taps):
                first = EDGE + 2 * (k - taps // 2)
                pieces.append(wide[first : first + tokens, v * per : (v + 1) * per])
            cols[...] = jnp.concatenate(pieces, axis=1).astype(jnp.bfloat16)
            part = lax.dot_general(
                cols[...], wb_ref[c], (((1,), (1,)), ((), ())), preferred_element_type=jnp.float32
            )
            if c == 0:
                emb_ref[v] = part
            else:
                emb_ref[v] += part
    moments_into(emb_ref, alive_column(lengths_ref, tokens, length), out_ref)


def embedding(lengths, hx, wb, planes, taps, length):
    down, rows, lanes = hx.shape
    width = wb.shape[1]
    tokens = rows - 2 * EDGE
    parts = share_rows(width, planes) * planes
    return pl.pallas_call(
        lambda *refs: embed_kernel(taps, length, *refs),
        out_shape=(
            jax.ShapeDtypeStruct((2, tokens, width), jnp.float32),
            jax.ShapeDtypeStruct((2, parts, BLOCK), jnp.float32),
        ),
        in_specs=[in_smem(), in_vmem(), pl.BlockSpec(memory_space=pl.ANY)],
        out_specs=(in_vmem(), in_vmem()),
        scratch_shapes=[
            pltpu.VMEM(wb.shape, wb.dtype),
            pltpu.VMEM((rows, lanes), jnp.float32),
            pltpu.VMEM((tokens, wb.shape[2]), jnp.bfloat16),
            pltpu.SemaphoreType.DMA((down,)),
        ],
        compiler_params=pltpu.CompilerParams(vmem_limit_bytes=40 << 20),
        name="embedding",
    )(lengths, hx, wb)


def shards(monomers, keep_mask, lengths, norm_gain, weight_a, weight_b):
    tokens = monomers.shape[0]
    length = tokens // lengths.shape[0]
    taps = weight_a.shape[0]
    sizes = (lax.axis_size(Z), lax.axis_size(X), lax.axis_size(Y))
    xt, wa, wb = gathered_inputs(monomers.T, weight_a, weight_b.transpose(0, 2, 1), sizes)
    hidden = first_conv(
        lengths,
        xt.reshape(-1, tokens),
        wa.reshape(-1, *wa.shape[3:]),
        norm_gain.reshape(-1, BLOCK),
        keep_mask,
        taps,
    )
    hx, wb = spread_hidden(hidden, wb, sizes)
    embedded, parts = embedding(lengths, hx, wb, sizes[1] * sizes[2], taps, length)
    total = total_moments(parts, sizes)
    inverse = inverse_factor(total, embedded.shape[2])
    other = from_partner(inverse)
    return whitened_rows(lengths, embedded, inverse, other, length)


def solution(mesh):
    torus = Mesh(
        mesh.devices.reshape(8, 4, 2, mesh.shape["chan"]), ("batch_0", "batch_1", "batch_2", "chan")
    )
    in_specs = (
        P(BATCH, "chan"),
        P(None, BATCH),
        P(BATCH),
        P(),
        P(None, BATCH, "chan"),
        P(None, "chan", BATCH),
    )
    out_specs = (P(None, BATCH_CHAN, None), P(BATCH_CHAN))
    return jax.shard_map(
        shards, mesh=torus, in_specs=in_specs, out_specs=out_specs, check_vma=False
    )
```

```python
import jax
import jax.numpy as jnp
from jax import lax
from jax.experimental import pallas as pl
from jax.experimental.pallas import tpu as pltpu
from jax.sharding import Mesh
from jax.sharding import PartitionSpec as P

BATCH = ("batch_0", "batch_1", "batch_2")
BATCH_CHAN = ("batch_0", "batch_1", "batch_2", "chan")


EPS_NORM = 1e-05
EPS_COV = 0.0001
HI = lax.Precision.HIGHEST
MESH_IDS = pl.DeviceIdType.MESH
Z, X, CORE, Y = "batch_0", "batch_1", "batch_2", "chan"
AXES = (Z, X, CORE, Y)
BLOCK = 128
GROUP = 8
LOWEST = -3.0e38
PARTS = 5


def dot_of(a, b, dims, precision=HI):
    return lax.dot_general(
        a, b, (dims, ((), ())), precision=precision, preferred_element_type=jnp.float32
    )


def in_vmem():
    return pl.BlockSpec(memory_space=pltpu.VMEM)


def block_pairs(width):
    return [(i, k) for i in range(width // BLOCK) for k in range(i + 1)]


def share_rows(width, planes):
    rows = len(block_pairs(width)) * BLOCK
    return -(-rows // (planes * GROUP)) * GROUP


def alive_column(lengths_ref, tokens, length):
    start = lax.axis_index(Y) * tokens
    limit = lengths_ref[start // length] - lax.rem(start, length)
    return jnp.where(lax.broadcasted_iota(jnp.int32, (tokens, 1), 0) < limit, 1.0, 0.0)


def in_smem():
    return pl.BlockSpec(memory_space=pltpu.SMEM)


def moments_into(emb_ref, alive, out_ref):
    views, tokens, width = emb_ref.shape
    pairs = block_pairs(width)
    at = len(pairs) * BLOCK
    half = BLOCK // 2
    for v in range(views):
        masked = emb_ref[v] * alive
        side = 2 * BLOCK
        for j in range(width // side):
            wide = (j + 1) * side
            strip = dot_of(masked[:, j * side : wide], masked[:, :wide], ((0,), (0,)))
            for i in (2 * j, 2 * j + 1):
                first = (i - 2 * j) * BLOCK
                for k in range(i + 1):
                    b = pairs.index((i, k))
                    out_ref[v, b * BLOCK : (b + 1) * BLOCK, :] = strip[
                        first : first + BLOCK, k * BLOCK : (k + 1) * BLOCK
                    ]
        if out_ref.shape[1] > at:
            out_ref[v, at:, :] = jnp.zeros((out_ref.shape[1] - at, BLOCK), jnp.float32)
        sums = jnp.sum(masked, axis=0, keepdims=True)
        spare = [sums[:, k * half : (k + 1) * half] for k in range(width // half)]
        spare.append(jnp.broadcast_to(jnp.sum(alive, axis=0, keepdims=True), (1, half)))
        out_ref[v, 0 : len(spare), half:] = jnp.concatenate(spare, axis=0)


def total_kernel(sizes, parts, part_ref, out_ref, pair_in, mine, plane_in, share, line_in, total, *sems):
    depth, across, down = sizes
    planes = across * down
    rows = share.shape[0]
    z, x = lax.axis_index(Z), lax.axis_index(X)
    core, y = lax.axis_index(CORE), lax.axis_index(Y)
    me = x * down + y
    partner = 1 - core
    pair_send, pair_recv, plane_send, plane_recv, line_send, line_recv, back_send, back_recv = sems

    def in_plane(step):
        other = lax.rem(me + step, planes)
        return other, (z, other // down, core, lax.rem(other, down))

    def in_line(step):
        other = lax.rem(z + step, depth)
        return other, (other, x, core, y)

    barrier = pltpu.get_barrier_semaphore()
    pl.semaphore_signal(barrier, inc=1, device_id=(z, x, partner, y), device_id_type=MESH_IDS)
    for step in range(1, planes):
        pl.semaphore_signal(barrier, inc=1, device_id=in_plane(step)[1], device_id_type=MESH_IDS)
    for step in range(1, depth):
        pl.semaphore_signal(barrier, inc=1, device_id=in_line(step)[1], device_id_type=MESH_IDS)
    pl.semaphore_wait(barrier, 1 + planes - 1 + depth - 1)

    def sent(src, dst, send, recv, device):
        copy = pltpu.make_async_remote_copy(
            src_ref=src, dst_ref=dst, send_sem=send, recv_sem=recv,
            device_id=device, device_id_type=MESH_IDS,
        )
        copy.start()
        return copy

    starts = [sum(parts[:i]) for i in range(len(parts))]

    def within(i):
        return pl.ds(starts[i], parts[i])

    swaps = [
        sent(
            part_ref.at[partner, :, within(i)], pair_in.at[:, within(i)],
            pair_send.at[i], pair_recv.at[i], (z, x, partner, y),
        )
        for i in range(len(parts))
    ]

    def summed(buffer, own, count, i):
        acc = None
        for source in range(count):
            piece = buffer[lax.rem(own - source + count, count), within(i)]
            acc = piece if acc is None else acc + piece
        return acc

    spread, lines, back = {}, {}, {}
    for i in range(len(parts)):
        swaps[i].wait_recv()
        mine[:, within(i)] = part_ref[core, :, within(i)] + pair_in[:, within(i)]
        for step in range(1, planes):
            other, device = in_plane(step)
            spread[i, step] = sent(
                mine.at[other, within(i)], plane_in.at[step, within(i)],
                plane_send.at[i, step], plane_recv.at[i, step], device,
            )

    def to_line(i):
        for step in range(1, planes):
            spread[i, step].wait_recv()
        plane_in[0, within(i)] = mine[me, within(i)]
        share[within(i)] = summed(plane_in, me, planes, i)
        for step in range(1, depth):
            lines[i, step] = sent(
                share.at[within(i)], line_in.at[step, within(i)],
                line_send.at[i, step], line_recv.at[i, step], in_line(step)[1],
            )

    def to_plane(i):
        for step in range(1, depth):
            lines[i, step].wait_recv()
        line_in[0, within(i)] = share[within(i)]
        total[within(i)] = summed(line_in, z, depth, i)
        for step in range(1, planes):
            back[i, step] = sent(
                total.at[within(i)], out_ref.at[me, within(i)],
                back_send.at[i, step], back_recv.at[i, step], in_plane(step)[1],
            )
        out_ref[me, within(i)] = total[within(i)]

    lag = 2
    for i in range(len(parts) + lag):
        if i < len(parts):
            to_line(i)
        if i >= lag:
            to_plane(i - lag)
    for copy in back.values():
        copy.wait_recv()
    for copy in swaps:
        copy.wait_send()
    for group in (spread, lines, back):
        for copy in group.values():
            copy.wait_send()


def total_moments(parts, mesh_sizes):
    depth, across, down = mesh_sizes
    planes = across * down
    _, all_rows, lanes = parts.shape
    rows = all_rows // planes
    tiles = rows // GROUP
    pieces = tuple(GROUP * (tiles // PARTS + (1 if i < tiles % PARTS else 0)) for i in range(PARTS))
    dma = pltpu.SemaphoreType.DMA
    vm = lambda *shape: pltpu.VMEM(shape, jnp.float32)
    return pl.pallas_call(
        lambda *refs: total_kernel(mesh_sizes, pieces, *refs),
        out_shape=jax.ShapeDtypeStruct((planes, rows, lanes), jnp.float32),
        in_specs=[in_vmem()],
        out_specs=in_vmem(),
        scratch_shapes=[
            vm(planes, rows, lanes),
            vm(planes, rows, lanes),
            vm(planes, rows, lanes),
            vm(rows, lanes),
            vm(depth, rows, lanes),
            vm(rows, lanes),
            dma((PARTS,)), dma((PARTS,)),
            dma((PARTS, planes)), dma((PARTS, planes)),
            dma((PARTS, depth)), dma((PARTS, depth)),
            dma((PARTS, planes)), dma((PARTS, planes)),
        ],
        compiler_params=pltpu.CompilerParams(
            collective_id=1, has_side_effects=True, vmem_limit_bytes=32 << 20
        ),
        name="total_moments",
    )(parts.reshape(2, planes, rows, lanes)).reshape(all_rows, lanes)


def splat_row(v, a):
    return jnp.broadcast_to(v[a : a + 1, :], (GROUP, BLOCK))


def splat_lane(v, j):
    return jnp.broadcast_to(v[:, j : j + 1], (GROUP, BLOCK))


def base_inverse(load, store):
    count = BLOCK // GROUP
    groups = [load(g) for g in range(count)]
    lane = lax.broadcasted_iota(jnp.int32, (GROUP, BLOCK), 1)
    sub = lax.broadcasted_iota(jnp.int32, (GROUP, BLOCK), 0)
    steps = range(GROUP)
    twos = range(GROUP // 2)
    for p in range(count):
        j = GROUP * p
        v = groups[p]
        cols = [jnp.maximum(splat_lane(v, j + a), LOWEST) for a in steps]
        e = [[splat_row(cols[a], b) if b >= a else None for a in steps] for b in steps]
        panel = (lane >= j) & (lane < j + GROUP)
        rows = [
            jnp.where(panel, jnp.where(lane == j + a, 1.0, 0.0), splat_row(v, a)) for a in steps
        ]
        f, inv = {}, []
        for t in twos:
            m, n = 2 * t, 2 * t + 1
            e00, e10, e11 = e[m][m], e[n][m], e[n][n]
            det = e00 * e11 - e10 * e10
            rd = 1.0 / det
            inv.append(rd)
            for b in range(n + 1, GROUP):
                f0 = (e11 * e[b][m] - e10 * e[b][n]) * rd
                f1 = (e00 * e[b][n] - e10 * e[b][m]) * rd
                f[b, t] = (f0, f1)
                for c in range(n + 1, b + 1):
                    e[b][c] = e[b][c] - (f0 * e[c][m] + f1 * e[c][n])
                rows[b] = rows[b] - (f0 * rows[m] + f1 * rows[n])
        out = None
        q = [None] * GROUP
        for t in reversed(twos):
            m, n = 2 * t, 2 * t + 1
            e00, e10, e11, rd = e[m][m], e[n][m], e[n][n], inv[t]
            q0 = (e11 * rows[m] - e10 * rows[n]) * rd
            q1 = (e00 * rows[n] - e10 * rows[m]) * rd
            for b in reversed(range(n + 1, GROUP)):
                q0 = q0 - f[b, t][0] * q[b]
                q1 = q1 - f[b, t][1] * q[b]
            q[m], q[n] = q0, q1
        for g in range(p + 1, count):
            x = groups[g]
            terms = [splat_lane(x, j + a) * q[a] for a in steps]
            pairs = [terms[2 * t] + terms[2 * t + 1] for t in twos]
            late = jnp.where(panel, 0.0, x) - ((pairs[3] + pairs[2]) + pairs[1])
            groups[g] = late - pairs[0]
        for t in twos:
            m, n = 2 * t, 2 * t + 1
            e00, e10, e11 = e[m][m], e[n][m], e[n][n]
            ratio = e10 / e00
            first = rows[m] * lax.rsqrt(e00)
            second = (rows[n] - ratio * rows[m]) * lax.rsqrt(e11 - ratio * e10)
            out = first if out is None else jnp.where(sub == m, first, out)
            out = jnp.where(sub == n, second, out)
        store(p, jnp.where(lane < j + GROUP, out, 0.0))


def factor_kernel(total_ref, out_ref, work, m_ref):
    width = work.shape[1]
    blocks = width // BLOCK
    pairs = block_pairs(width)
    half = BLOCK // 2
    spare = total_ref[0 : 2 * GROUP, half:]
    last = width // half
    count = spare[last : last + 1, 0:1]
    center = jnp.concatenate([spare[k : k + 1, :] for k in range(last)], axis=1) / count
    sub = lax.broadcasted_iota(jnp.int32, (GROUP, width), 0)
    center8 = jnp.where(sub == 0, jnp.broadcast_to(center, (GROUP, width)), 0.0)
    high = center.astype(jnp.bfloat16).astype(jnp.float32)
    middle = (center - high).astype(jnp.bfloat16).astype(jnp.float32)
    low = center - high - middle

    def stacked(parts):
        rows = jnp.zeros((GROUP, width), jnp.float32)
        for i, part in enumerate(parts):
            rows = jnp.where(sub == i, jnp.broadcast_to(part, (GROUP, width)), rows)
        return rows.astype(jnp.bfloat16)

    one_side = stacked((high, high, middle, high, low, middle, middle, low))
    other_side = stacked((high, middle, high, low, high, middle, low, middle))
    eye = lax.broadcasted_iota(jnp.int32, (BLOCK, BLOCK), 0) == lax.broadcasted_iota(
        jnp.int32, (BLOCK, BLOCK), 1
    )
    lower = lax.broadcasted_iota(jnp.int32, (BLOCK, BLOCK), 0) >= lax.broadcasted_iota(
        jnp.int32, (BLOCK, BLOCK), 1
    )
    for b, (i, k) in enumerate(pairs):
        outer = dot_of(
            one_side[:, i * BLOCK : (i + 1) * BLOCK],
            other_side[:, k * BLOCK : (k + 1) * BLOCK],
            ((0,), (0,)),
            lax.Precision.DEFAULT,
        )
        raw = total_ref[b * BLOCK : (b + 1) * BLOCK, :]
        if b == 0:
            raw = jnp.where(lower, raw, raw.T)
        block = raw / count - outer
        if i == k:
            block = block + jnp.where(eye, EPS_COV, 0.0)
        work[i * BLOCK : (i + 1) * BLOCK, k * BLOCK : (k + 1) * BLOCK] = block
        if i != k:
            work[k * BLOCK : (k + 1) * BLOCK, i * BLOCK : (i + 1) * BLOCK] = block.T
    strip_block = lax.broadcasted_iota(jnp.int32, (BLOCK, width), 1) // BLOCK
    strip_eye = jnp.where(
        lax.broadcasted_iota(jnp.int32, (BLOCK, width), 1) % BLOCK
        == lax.broadcasted_iota(jnp.int32, (BLOCK, width), 0),
        1.0,
        0.0,
    )

    def step(k, _):
        here = pl.multiple_of(k * BLOCK, BLOCK)

        def load(g):
            return work[pl.ds(pl.multiple_of(here + GROUP * g, GROUP), GROUP), pl.ds(here, BLOCK)]

        def store(g, val):
            m_ref[GROUP * g : GROUP * (g + 1), :] = val

        base_inverse(load, store)
        m = m_ref[...]
        row = jnp.where(strip_block == k, strip_eye, work[pl.ds(here, BLOCK), :])
        across = dot_of(m, row, ((1,), (0,)))
        for done in range(blocks - 1):

            @pl.when(k == done)
            def _():
                first = (done + 1) * BLOCK
                col_block = lax.broadcasted_iota(jnp.int32, (width - first, width), 1) // BLOCK
                left = dot_of(work[first:, done * BLOCK : first], m, ((1,), (1,)))
                kept = jnp.where(col_block == done, 0.0, work[first:, :])
                work[first:, :] = kept - dot_of(left, across, ((1,), (0,)))

        work[pl.ds(here, BLOCK), :] = jnp.where(strip_block <= k, across, 0.0)
        return 0

    lax.fori_loop(0, blocks, step, 0)
    out_ref[:width, :] = work[...]
    out_ref[width:, :] = center8


def inverse_factor(total, width):
    return pl.pallas_call(
        factor_kernel,
        out_shape=jax.ShapeDtypeStruct((width + GROUP, width), jnp.float32),
        in_specs=[in_vmem()],
        out_specs=in_vmem(),
        scratch_shapes=[
            pltpu.VMEM((width, width), jnp.float32),
            pltpu.VMEM((BLOCK, BLOCK), jnp.float32),
        ],
        compiler_params=pltpu.CompilerParams(vmem_limit_bytes=32 << 20),
        name="inverse_factor",
    )(total)


def swap_kernel(own_ref, out_ref, send, recv):
    z, x = lax.axis_index(Z), lax.axis_index(X)
    core, y = lax.axis_index(CORE), lax.axis_index(Y)
    other = (z, x, 1 - core, y)
    barrier = pltpu.get_barrier_semaphore()
    pl.semaphore_signal(barrier, inc=1, device_id=other, device_id_type=MESH_IDS)
    pl.semaphore_wait(barrier, 1)
    rows, width = own_ref.shape
    side = width // 2
    copies = []
    for i, (first, last, wide) in enumerate(((0, side, side), (side, rows, width))):
        part = (pl.ds(first, last - first), pl.ds(0, wide))
        copy = pltpu.make_async_remote_copy(
            src_ref=own_ref.at[part], dst_ref=out_ref.at[part], send_sem=send.at[i], recv_sem=recv.at[i],
            device_id=other, device_id_type=MESH_IDS,
        )
        copy.start()
        copies.append(copy)
    for copy in copies:
        copy.wait()


def from_partner(own):
    return pl.pallas_call(
        swap_kernel,
        out_shape=jax.ShapeDtypeStruct(own.shape, own.dtype),
        in_specs=[in_vmem()],
        out_specs=in_vmem(),
        scratch_shapes=[pltpu.SemaphoreType.DMA((2,)), pltpu.SemaphoreType.DMA((2,))],
        compiler_params=pltpu.CompilerParams(
            collective_id=2, has_side_effects=True, vmem_limit_bytes=16 << 20
        ),
        name="from_partner",
    )(own)


def whiten_kernel(length, lengths_ref, emb_ref, own_ref, other_ref, out_ref, gap_ref):
    views, tokens, width = emb_ref.shape
    core = lax.axis_index(CORE)
    alive = alive_column(lengths_ref, tokens, length)
    for ref, v in ((own_ref, core), (other_ref, 1 - core)):
        centered = (emb_ref[v] - ref[width : width + 1, :]) * alive
        part = 2 * BLOCK
        for first in range(0, width, part):
            last = first + part
            out_ref[v, :, first:last] = dot_of(centered[:, :last], ref[first:last, :last], ((1,), (1,)))
    gap = out_ref[0] - out_ref[1]
    ones = jnp.ones((GROUP, width), jnp.float32)
    sums = dot_of(ones, gap * gap, ((1,), (1,))) / width
    for k in range(tokens // BLOCK):
        gap_ref[k : k + 1, :] = sums[0:1, k * BLOCK : (k + 1) * BLOCK]


def whitened_rows(lengths, embedded, own, other, length):
    views, tokens, width = embedded.shape
    whitened, gap = pl.pallas_call(
        lambda *refs: whiten_kernel(length, *refs),
        out_shape=(
            jax.ShapeDtypeStruct(embedded.shape, jnp.float32),
            jax.ShapeDtypeStruct((tokens // BLOCK, BLOCK), jnp.float32),
        ),
        in_specs=[in_smem()] + [in_vmem()] * 3,
        out_specs=(in_vmem(), in_vmem()),
        compiler_params=pltpu.CompilerParams(vmem_limit_bytes=32 << 20),
        name="whitened_rows",
    )(lengths, embedded, own, other)
    return whitened, gap.reshape(tokens)


class Sender:
    def __init__(self, send_sems, recv_sems):
        self.send_sems, self.recv_sems = send_sems, recv_sems
        self.started, self.used = [], 0

    def site(self):
        self.used += 1
        return self.used - 1

    def copy(self, site, src, dst, device):
        return pltpu.make_async_remote_copy(
            src_ref=src, dst_ref=dst,
            send_sem=self.send_sems.at[site], recv_sem=self.recv_sems.at[site],
            device_id=device, device_id_type=MESH_IDS,
        )

    def send(self, site, src, dst, device):
        made = self.copy(site, src, dst, device)
        made.start()
        self.started.append(made)

    def arrived(self, site, dst, device):
        self.copy(site, dst, dst, device).wait_recv()

    def finish(self):
        for made in self.started:
            made.wait_send()


class Ring:
    def __init__(self, sender, size, pos, device_at, slot_at, hops, own=None):
        self.sender, self.size, self.pos = sender, size, pos
        self.device_at, self.slot_at = device_at, slot_at
        self.hops = {1: hops[0], -1: hops[1]}
        self.own = own
        self.sites = {
            (sign, h): sender.site() for sign in (1, -1) for h in range(1, self.hops[sign] + 1)
        }

    def at(self, offset):
        return lax.rem(self.pos + offset + 2 * self.size, self.size)

    def pass_on(self, sign, h):
        source = self.at(-sign * (h - 1))
        slot = self.slot_at(source)
        src = self.own if h == 1 and self.own is not None else slot
        self.sender.send(self.sites[sign, h], src, slot, self.device_at(self.at(sign)))

    def launch(self):
        for sign in (1, -1):
            self.pass_on(sign, 1)

    def has(self, sign, h):
        return h <= self.hops[sign]

    def take(self, sign, h):
        slot = self.slot_at(self.at(-sign * h))
        self.sender.arrived(self.sites[sign, h], slot, self.device_at(self.at(-sign)))
        if h < self.hops[sign]:
            self.pass_on(sign, h + 1)
        return (sign * h) % self.size


class Place:
    def __init__(self, sizes):
        self.depth, self.across, self.down = sizes
        self.z, self.x = lax.axis_index(Z), lax.axis_index(X)
        self.core, self.y = lax.axis_index(CORE), lax.axis_index(Y)
        self.partner = (self.z, self.x, 1 - self.core, self.y)

    def z_at(self, s):
        return lax.rem(self.z - s + 2 * self.depth, self.depth)

    def x_at(self, t):
        return lax.rem(self.x - t + 2 * self.across, self.across)

    def y_at(self, s):
        return lax.rem(self.y + s + 2 * self.down, self.down)

    def along_z(self, zz):
        return (zz, self.x, self.core, self.y)

    def along_x(self, xx):
        return (self.z, xx, self.core, self.y)

    def along_y(self, yy):
        return (self.z, self.x, self.core, yy)

    def greet(self):
        self.greeted(self.greeting())

    def greeting(self):
        peers = [self.along_z(self.z_at(s)) for s in (1, -1)]
        peers += [self.along_x(self.x_at(s)) for s in (1, -1)]
        peers += [self.along_y(self.y_at(s)) for s in range(1, self.down)]
        peers += [self.partner]
        barrier = pltpu.get_barrier_semaphore()
        for peer in peers:
            pl.semaphore_signal(barrier, inc=1, device_id=peer, device_id_type=MESH_IDS)
        return len(peers)

    def greeted(self, count):
        pl.semaphore_wait(pltpu.get_barrier_semaphore(), count)


SITES = 64
FEW = 4


def rows_of_slab(zz, xx, core, across):
    return pl.ds(pl.multiple_of(((zz * across + xx) * 2 + core) * GROUP, GROUP), GROUP)


def gather_kernel(
    sizes, xt_ref, hbm_a, hbm_b, xt_out, wa_out, wb_out, raw_a, raw_b, wa_ref, wb_ref,
    ring_send, ring_recv, pair_send, pair_recv, y_send, y_recv, local,
):
    here = Place(sizes)
    depth, across, down = sizes
    z, x, core, y = here.z, here.x, here.core, here.y
    greeted = here.greeting()
    load_a = pltpu.make_async_copy(hbm_a, raw_a, local.at[3])
    load_b = pltpu.make_async_copy(hbm_b, raw_b, local.at[4])
    load_a.start()
    load_b.start()
    load_a.wait()
    load_b.wait()
    rows_a = jnp.concatenate([raw_a[k] for k in range(raw_a.shape[0])], axis=1)
    for i in range(wa_ref.shape[0]):
        wa_ref[i] = rows_a[i * FEW : (i + 1) * FEW, :]
    wb_ref[...] = jnp.concatenate([raw_b[k] for k in range(raw_b.shape[0])], axis=1)
    here.greeted(greeted)
    half = xt_ref.shape[0] // 2

    def slab(zz, xx, cc):
        return wb_out.at[:, rows_of_slab(zz, xx, cc, across), :]

    def own_part(yy):
        return wb_out.at[yy, rows_of_slab(z, x, core, across), :]

    own = [
        pltpu.make_async_copy(wb_ref, own_part(y), local.at[0]),
        pltpu.make_async_copy(wa_ref, wa_out.at[z, x, core], local.at[1]),
        pltpu.make_async_copy(xt_ref, xt_out.at[y], local.at[2]),
    ]
    for copy in own:
        copy.start()

    ys = Sender(y_send, y_recv)
    wb_sites = {s: ys.site() for s in range(1, down)}
    for s in range(1, down):
        ys.send(wb_sites[s], wb_ref, own_part(y), here.along_y(here.y_at(s)))

    def piece(yy, p):
        return xt_out.at[yy, p * half : (p + 1) * half, :]

    xt_sites = {(sign, p, h): ys.site() for sign in (1, -1) for p in (0, 1) for h in (1, 2)}
    for first in (0, 1):
        for sign in (1, -1):
            p = first if sign == 1 else 1 - first
            ys.send(
                xt_sites[sign, p, 1], xt_ref.at[p * half : (p + 1) * half, :], piece(y, p),
                here.along_y(here.y_at(sign)),
            )

    def first_pieces():
        for sign, p in ((1, 0), (-1, 1)):
            source = here.y_at(-sign)
            ys.arrived(xt_sites[sign, p, 1], piece(source, p), here.along_y(source))
            ys.send(xt_sites[sign, p, 2], piece(source, p), piece(source, p), here.along_y(here.y_at(sign)))

    def last_pieces():
        for sign, p in ((1, 1), (-1, 0)):
            source = here.y_at(-sign)
            ys.arrived(xt_sites[sign, p, 1], piece(source, p), here.along_y(source))
        for sign, p in ((1, 0), (-1, 1)):
            ys.arrived(xt_sites[sign, p, 2], piece(here.y_at(2), p), here.along_y(here.y_at(-sign)))

    def slabs_ready():
        for s in range(1, down):
            source = here.y_at(-s)
            ys.arrived(wb_sites[s], own_part(source), here.along_y(source))
        own[0].wait()

    pairs = Sender(pair_send, pair_recv)

    def to_partner(s, t):
        slot = wa_out.at[here.z_at(s), here.x_at(t), core]
        src = wa_ref if s == 0 and t == 0 else slot
        pairs.send(s * across + t, src, slot, here.partner)

    @pl.when(core == 0)
    def _():
        rings = Sender(ring_send, ring_recv)
        down_z = Ring(rings, depth, z, here.along_z, lambda zz: wa_out.at[zz, x, core], (4, 3), wa_ref)
        slabs_z = Ring(rings, depth, z, here.along_z, lambda zz: slab(zz, x, core), (3, 4))
        on_x = [
            Ring(
                rings, across, x, here.along_x,
                lambda xx, s=s: wa_out.at[here.z_at(s), xx, core],
                (2, 1) if s % 2 == 0 else (1, 2),
                wa_ref if s == 0 else None,
            )
            for s in range(depth)
        ]
        down_z.launch()
        on_x[0].launch()
        to_partner(0, 0)
        slabs_ready()
        slabs_z.launch()
        waiting = [0]
        for h in range(1, 5):
            arrived = []
            for sign in (1, -1):
                if down_z.has(sign, h):
                    s = down_z.take(sign, h)
                    on_x[s].launch()
                    to_partner(s, 0)
                    arrived.append(s)
            for sign in (1, -1):
                if slabs_z.has(sign, h):
                    slabs_z.take(sign, h)
            for s in waiting:
                for sign in (1, -1):
                    to_partner(s, on_x[s].take(sign, 1))
            waiting = arrived
            if h == 3:
                first_pieces()
        for s in waiting:
            for sign in (1, -1):
                to_partner(s, on_x[s].take(sign, 1))
        for s in [0, 1, 7, 2, 6, 3, 5, 4]:
            to_partner(s, on_x[s].take(1 if s % 2 == 0 else -1, 2))
        rings.finish()

    @pl.when(core == 1)
    def _():
        rings = Sender(ring_send, ring_recv)
        own_x = Ring(rings, across, x, here.along_x, lambda xx: wa_out.at[z, xx, core], (2, 1), wa_ref)
        slabs_x = Ring(rings, across, x, here.along_x, lambda xx: slab(z, xx, core), (1, 2))
        on_z = [
            Ring(
                rings, depth, z, here.along_z,
                lambda zz, t=t: wa_out.at[zz, here.x_at(t), core],
                (4, 3) if t % 2 == 0 else (3, 4),
                wa_ref if t == 0 else None,
            )
            for t in range(across)
        ]
        own_x.launch()
        on_z[0].launch()
        to_partner(0, 0)
        slabs_ready()
        slabs_x.launch()
        for sign, h in ((1, 1), (-1, 1), (1, 2)):
            t = own_x.take(sign, h)
            on_z[t].launch()
            to_partner(0, t)
        for sign, h in ((1, 1), (-1, 1), (-1, 2)):
            slabs_x.take(sign, h)
        for h in range(1, 5):
            for t in (0, 1, 3, 2):
                for sign in (1, -1):
                    if on_z[t].has(sign, h):
                        to_partner(on_z[t].take(sign, h), t)
            if h == 1:
                first_pieces()
        rings.finish()

    last_pieces()
    for s in range(depth):
        for t in range(across):
            slot = wa_out.at[here.z_at(s), here.x_at(t), 1 - core]
            made = pairs.copy(s * across + t, slot, slot, here.partner)
            made.wait_recv()
            made.wait_send()
    ys_wait = ys.started
    for made in ys_wait[: down - 1 + 4]:
        made.wait_send()
    for sign, p in ((1, 0), (-1, 1)):
        ys.copy(
            xt_sites[sign, p, 2], piece(here.y_at(-sign), p), piece(here.y_at(-sign), p),
            here.along_y(here.y_at(sign)),
        ).wait_send()
    own[1].wait()
    own[2].wait()


def gathered_inputs(xt, wa, wb, sizes):
    depth, across, down = sizes
    dma = pltpu.SemaphoreType.DMA
    anywhere = pl.BlockSpec(memory_space=pl.ANY)
    taps, rows_a, width = wa.shape
    rows_b = wb.shape[1]
    return pl.pallas_call(
        lambda *refs: gather_kernel(sizes, *refs),
        out_shape=(
            jax.ShapeDtypeStruct((down, *xt.shape), xt.dtype),
            jax.ShapeDtypeStruct((depth, across, 2, rows_a // FEW, FEW, taps * width), wa.dtype),
            jax.ShapeDtypeStruct((down, depth * across * 2 * rows_b, taps * width), wb.dtype),
        ),
        in_specs=[anywhere] * 3,
        out_specs=(in_vmem(), anywhere, anywhere),
        scratch_shapes=[
            pltpu.VMEM(wa.shape, wa.dtype),
            pltpu.VMEM(wb.shape, wb.dtype),
            pltpu.VMEM((rows_a // FEW, FEW, taps * width), wa.dtype),
            pltpu.VMEM((rows_b, taps * width), wb.dtype),
            dma((SITES,)), dma((SITES,)),
            dma((depth * across,)), dma((depth * across,)),
            dma((16,)), dma((16,)),
            dma((5,)),
        ],
        compiler_params=pltpu.CompilerParams(
            collective_id=3, has_side_effects=True, vmem_limit_bytes=16 << 20
        ),
        cost_estimate=pl.CostEstimate(flops=20_000_000_000, bytes_accessed=80_000_000, transcendentals=0),
        name="gathered_inputs",
    )(xt, wa, wb)


def gate(values):
    return 0.5 * values * (1.0 + jnp.tanh(0.7978845608 * (values + 0.044715 * values * values * values)))


PAD = 8
ROWS = 128
EDGE = 16


def conv_kernel(
    sizes, lengths_ref, xt_ref, wa_hbm, gain_hbm, keep_hbm, out_ref,
    wa_ref, gain_ref, keep_ref, n_ref, w_ref, p_ref, cols, sems,
):
    sequences, length, taps = sizes
    channels, tokens = xt_ref.shape
    chunks, few_count, _, lanes = wa_ref.shape
    chunk_rows = few_count * FEW
    loads = 4
    each = chunks // loads
    arriving = [
        pltpu.make_async_copy(wa_hbm.at[pl.ds(i * each, each)], wa_ref.at[pl.ds(i * each, each)], sems.at[i])
        for i in range(loads)
    ]
    small = [
        pltpu.make_async_copy(gain_hbm, gain_ref, sems.at[loads]),
        pltpu.make_async_copy(keep_hbm, keep_ref, sems.at[loads + 1]),
    ]
    for copy in small + arriving:
        copy.start()
    eye = lax.broadcasted_iota(jnp.int32, (BLOCK, BLOCK), 0) == lax.broadcasted_iota(
        jnp.int32, (BLOCK, BLOCK), 1
    )
    squares = jnp.zeros((1, tokens), jnp.float32)
    for i in range(channels // BLOCK):
        part = xt_ref[i * BLOCK : (i + 1) * BLOCK, :].astype(jnp.float32)
        squares = squares + jnp.sum(part * part, axis=0, keepdims=True)
    scale = lax.rsqrt(squares / channels + EPS_NORM)
    for copy in small:
        copy.wait()
    for i in range(channels // BLOCK):
        part = xt_ref[i * BLOCK : (i + 1) * BLOCK, :].astype(jnp.float32)
        gain = jnp.sum(
            jnp.where(eye, jnp.broadcast_to(gain_ref[i : i + 1, :], (BLOCK, BLOCK)), 0.0), axis=1, keepdims=True
        )
        normed = (part * scale * gain).astype(jnp.bfloat16)
        n_ref[:, i * BLOCK : (i + 1) * BLOCK] = normed.T

    token = lax.broadcasted_iota(jnp.int32, (GROUP, tokens), 1)
    position = token % length
    limit = jnp.zeros((GROUP, tokens), jnp.int32)
    for s in range(sequences):
        limit = jnp.where(token // length == s, lengths_ref[s], limit)
    view = lax.broadcasted_iota(jnp.int32, (GROUP, tokens), 0)
    keep = jnp.where(view == 0, keep_ref[0:1, :], jnp.where(view == 1, keep_ref[1:2, :], 0))
    kept = jnp.where(position < limit, keep, 0).astype(jnp.float32)
    stacked = [jnp.zeros((GROUP, tokens), jnp.float32) for _ in range(cols.shape[0])]
    per = GROUP // 2
    for k in range(taps):
        move = k - taps // 2
        rolled = kept if move == 0 else pltpu.roll(kept, (-move) % tokens, 1)
        inside = (position + move >= 0) & (position + move < length)
        rolled = jnp.where(inside, rolled, 0.0)
        down = 2 * (k % per)
        rolled = rolled if down == 0 else pltpu.roll(rolled, down, 0)
        stacked[k // per] = jnp.where(view // 2 == k % per, rolled, stacked[k // per])
    for i in range(cols.shape[0]):
        cols[i] = stacked[i].T

    group = 4

    def relay(q, _):
        pieces = [
            wa_ref[q * group + i, r].astype(jnp.float32) for i in range(group) for r in range(few_count)
        ]
        at = pl.multiple_of(q * group * chunk_rows, group * chunk_rows)
        w_ref[pl.ds(at, group * chunk_rows), :] = jnp.concatenate(pieces, axis=0).astype(jnp.bfloat16)
        return 0

    for i in range(loads):
        arriving[i].wait()
        lax.fori_loop(i * each // group, (i + 1) * each // group, relay, 0)

    width = lanes // taps
    p_ref[0:PAD, :] = jnp.zeros((PAD, lanes), jnp.float32)
    p_ref[PAD + length :, :] = jnp.zeros((PAD, lanes), jnp.float32)

    def sequence(s, _):
        start = pl.multiple_of(s * length, length)
        for r in range(length // ROWS):
            p_ref[PAD + r * ROWS : PAD + (r + 1) * ROWS, :] = jnp.dot(
                n_ref[pl.ds(start + r * ROWS, ROWS), :], w_ref[...], preferred_element_type=jnp.float32
            )
        for r in range(length // ROWS):
            hidden = []
            for v in range(2):
                acc = None
                for k in range(taps):
                    first = PAD + r * ROWS + k - taps // 2
                    piece = p_ref[first : first + ROWS, k * width : (k + 1) * width]
                    at = 2 * (k % per) + v
                    piece = piece * cols[k // per, pl.ds(start + r * ROWS, ROWS), at : at + 1]
                    acc = piece if acc is None else acc + piece
                hidden.append(gate(acc))
            out_ref[pl.ds(start + r * ROWS, ROWS), :] = jnp.concatenate(hidden, axis=1).astype(jnp.bfloat16)
        return 0

    lax.fori_loop(0, sequences, sequence, 0)


def first_conv(lengths, xt, wa, gain, keep, taps):
    channels, tokens = xt.shape
    chunks, few_count, _, lanes = wa.shape
    chunk_rows = few_count * FEW
    sequences = lengths.shape[0]
    length = tokens // sequences
    bf, f32 = jnp.bfloat16, jnp.float32
    return pl.pallas_call(
        lambda *refs: conv_kernel((sequences, length, taps), *refs),
        out_shape=jax.ShapeDtypeStruct((tokens, 2 * lanes // taps), bf),
        in_specs=[in_smem(), in_vmem()] + [pl.BlockSpec(memory_space=pl.ANY)] * 3,
        out_specs=in_vmem(),
        scratch_shapes=[
            pltpu.VMEM(wa.shape, bf),
            pltpu.VMEM(gain.shape, f32),
            pltpu.VMEM(keep.shape, keep.dtype),
            pltpu.VMEM((tokens, channels), bf),
            pltpu.VMEM((channels, lanes), bf),
            pltpu.VMEM((length + 2 * PAD, lanes), f32),
            pltpu.VMEM((-(-taps // (GROUP // 2)), tokens, GROUP), f32),
            pltpu.SemaphoreType.DMA((6,)),
        ],
        compiler_params=pltpu.CompilerParams(vmem_limit_bytes=40 << 20),
        name="first_conv",
    )(lengths, xt, wa, gain, keep)


def spread_kernel(
    sizes, h_ref, wb_in, hx_out, wb_out, ring_send, ring_recv, pair_send, pair_recv, y_send, y_recv, local
):
    here = Place(sizes)
    depth, across, down = sizes
    z, x, core, y = here.z, here.x, here.core, here.y
    here.greet()
    rows = h_ref.shape[0] // down
    window = rows + EDGE

    def source_rows(yy):
        return pl.ds(pl.multiple_of(yy * rows - EDGE * lax.rem(yy, 2), EDGE), window)

    def target_rows(yy):
        return pl.ds(pl.multiple_of(EDGE - EDGE * lax.rem(yy, 2), EDGE), window)

    ys = Sender(y_send, y_recv)
    for s in (2, 1, 3):
        other = here.y_at(s)
        ys.send(s, h_ref.at[source_rows(other), :], hx_out.at[y, target_rows(other), :], here.along_y(other))
    own = pltpu.make_async_copy(h_ref.at[source_rows(y), :], hx_out.at[y, target_rows(y), :], local.at[0])
    own.start()

    def slab(zz, xx, cc):
        return wb_out.at[:, rows_of_slab(zz, xx, cc, across), :]

    pairs = Sender(pair_send, pair_recv)

    def to_partner(s, t):
        slot = slab(here.z_at(s), here.x_at(t), core)
        pairs.send(s * across + t, slot, slot, here.partner)

    @pl.when(core == 0)
    def _():
        rings = Sender(ring_send, ring_recv)
        on_x = [
            Ring(
                rings, across, x, here.along_x,
                lambda xx, s=s: slab(here.z_at(s), xx, core),
                (2, 1) if s % 2 == 0 else (1, 2),
            )
            for s in range(depth)
        ]
        for s in range(depth):
            on_x[s].launch()
        for s in range(depth):
            to_partner(s, 0)
        for s in range(depth):
            for sign in (1, -1):
                to_partner(s, on_x[s].take(sign, 1))
        for s in range(depth):
            to_partner(s, on_x[s].take(1 if s % 2 == 0 else -1, 2))
        rings.finish()

    @pl.when(core == 1)
    def _():
        rings = Sender(ring_send, ring_recv)
        on_z = [
            Ring(
                rings, depth, z, here.along_z,
                lambda zz, t=t: slab(zz, here.x_at(t), core),
                (4, 3) if t % 2 == 0 else (3, 4),
            )
            for t in range(across)
        ]
        for t in range(across):
            on_z[t].launch()
        for t in range(across):
            to_partner(0, t)
        for h in range(1, 5):
            for t in range(across):
                for sign in (1, -1):
                    if on_z[t].has(sign, h):
                        to_partner(on_z[t].take(sign, h), t)
        rings.finish()

    for s in range(depth):
        for t in range(across):
            slot = slab(here.z_at(s), here.x_at(t), 1 - core)
            made = pairs.copy(s * across + t, slot, slot, here.partner)
            made.wait_recv()
            made.wait_send()
    for s in (2, 1, 3):
        source = here.y_at(-s)
        ys.arrived(s, hx_out.at[source, target_rows(y), :], here.along_y(source))
    ys.finish()
    own.wait()


def spread_hidden(hidden, wb, sizes):
    depth, across, down = sizes
    tokens, lanes = hidden.shape
    dma = pltpu.SemaphoreType.DMA
    anywhere = pl.BlockSpec(memory_space=pl.ANY)
    return pl.pallas_call(
        lambda *refs: spread_kernel(sizes, *refs),
        out_shape=(
            jax.ShapeDtypeStruct((down, tokens // down + 2 * EDGE, lanes), hidden.dtype),
            jax.ShapeDtypeStruct(wb.shape, wb.dtype),
        ),
        in_specs=[in_vmem(), anywhere],
        out_specs=(in_vmem(), anywhere),
        input_output_aliases={1: 1},
        scratch_shapes=[
            dma((SITES,)), dma((SITES,)),
            dma((depth * across,)), dma((depth * across,)),
            dma((4,)), dma((4,)),
            dma((1,)),
        ],
        compiler_params=pltpu.CompilerParams(
            collective_id=4, has_side_effects=True, vmem_limit_bytes=16 << 20
        ),
        cost_estimate=pl.CostEstimate(flops=10_000_000_000, bytes_accessed=40_000_000, transcendentals=0),
        name="spread_hidden",
    )(hidden, wb)


def embed_kernel(taps, length, lengths_ref, hx_ref, wb_hbm, emb_ref, out_ref, wb_ref, wide, cols, sems):
    down, rows, lanes = hx_ref.shape
    arriving = [pltpu.make_async_copy(wb_hbm.at[c], wb_ref.at[c], sems.at[c]) for c in range(down)]
    for copy in arriving:
        copy.start()
    views, tokens, width = emb_ref.shape
    odd = lax.rem(lax.axis_index(Y), 2)
    row = lax.broadcasted_iota(jnp.int32, (rows, lanes), 0)
    inside = (row >= EDGE * (1 - odd)) & (row < rows - EDGE * odd)
    per = lanes // views
    for c in range(down):
        wide[...] = jnp.where(inside, hx_ref[c].astype(jnp.float32), 0.0)
        arriving[c].wait()
        for v in range(views):
            pieces = []
            for k in range(taps):
                first = EDGE + 2 * (k - taps // 2)
                pieces.append(wide[first : first + tokens, v * per : (v + 1) * per])
            cols[...] = jnp.concatenate(pieces, axis=1).astype(jnp.bfloat16)
            part = lax.dot_general(
                cols[...], wb_ref[c], (((1,), (1,)), ((), ())), preferred_element_type=jnp.float32
            )
            if c == 0:
                emb_ref[v] = part
            else:
                emb_ref[v] += part
    moments_into(emb_ref, alive_column(lengths_ref, tokens, length), out_ref)


def embedding(lengths, hx, wb, planes, taps, length):
    down, rows, lanes = hx.shape
    width = wb.shape[1]
    tokens = rows - 2 * EDGE
    parts = share_rows(width, planes) * planes
    return pl.pallas_call(
        lambda *refs: embed_kernel(taps, length, *refs),
        out_shape=(
            jax.ShapeDtypeStruct((2, tokens, width), jnp.float32),
            jax.ShapeDtypeStruct((2, parts, BLOCK), jnp.float32),
        ),
        in_specs=[in_smem(), in_vmem(), pl.BlockSpec(memory_space=pl.ANY)],
        out_specs=(in_vmem(), in_vmem()),
        scratch_shapes=[
            pltpu.VMEM(wb.shape, wb.dtype),
            pltpu.VMEM((rows, lanes), jnp.float32),
            pltpu.VMEM((tokens, wb.shape[2]), jnp.bfloat16),
            pltpu.SemaphoreType.DMA((down,)),
        ],
        compiler_params=pltpu.CompilerParams(vmem_limit_bytes=40 << 20),
        name="embedding",
    )(lengths, hx, wb)


def shards(monomers, keep_mask, lengths, norm_gain, weight_a, weight_b):
    tokens = monomers.shape[0]
    length = tokens // lengths.shape[0]
    taps = weight_a.shape[0]
    sizes = (lax.axis_size(Z), lax.axis_size(X), lax.axis_size(Y))
    xt, wa, wb = gathered_inputs(monomers.T, weight_a, weight_b.transpose(0, 2, 1), sizes)
    hidden = first_conv(
        lengths,
        xt.reshape(-1, tokens),
        wa.reshape(-1, *wa.shape[3:]),
        norm_gain.reshape(-1, BLOCK),
        keep_mask,
        taps,
    )
    hx, wb = spread_hidden(hidden, wb, sizes)
    embedded, parts = embedding(lengths, hx, wb, sizes[1] * sizes[2], taps, length)
    total = total_moments(parts, sizes)
    inverse = inverse_factor(total, embedded.shape[2])
    other = from_partner(inverse)
    return whitened_rows(lengths, embedded, inverse, other, length)


def solution(mesh):
    torus = Mesh(
        mesh.devices.reshape(8, 4, 2, mesh.shape["chan"]), ("batch_0", "batch_1", "batch_2", "chan")
    )
    in_specs = (
        P(BATCH, "chan"),
        P(None, BATCH),
        P(BATCH),
        P(),
        P(None, BATCH, "chan"),
        P(None, "chan", BATCH),
    )
    out_specs = (P(None, BATCH_CHAN, None), P(BATCH_CHAN))
    return jax.shard_map(
        shards, mesh=torus, in_specs=in_specs, out_specs=out_specs, check_vma=False
    )
```
